32 devices in a mesh: dp: 8 (over z, x), seq: 4 (over y, core).
Axes of the slice: x: 2, y: 2, z: 4, core: 2. Of those that a mesh axis runs over, the one named last changes fastest.
Arguments:
- tokens: bfloat16 [8, 1024, 768], P('dp', 'seq'), may hold values from -6 to 6
- segment_ids: int32 [8, 1024], P('dp'), may hold values from 0 to 5, never falling along the last dimension, each value on 1 to 512 neighbouring positions
- pad_lengths: int32 [8], P('dp'), may hold values from 0 to 511
- threshold: float32 [1], replicated, may hold values from 0.05 to 2
- gains: float32 [2, 768], replicated, may hold values from 0.5 to 1.5
- gain_first: float32 [2, 768], replicated, may hold values from -256 to 256
- gain_second: float32 [2, 768], replicated, may hold values from 2048 to 8192
- slot_tiles: int32 [448], replicated, may hold values from 0 to 447, as said below
- weight_slots: float32 [448, 128, 128], P(('dp', 'seq')), may hold values from -2 to 2
- first_moment: float32 [448, 128, 128], P(('dp', 'seq')), may hold values from -160 to 160
- second_moment: float32 [448, 128, 128], P(('dp', 'seq')), may hold values from 819.2 to 3276.8
- basis_left: float32 [448, 128, 128], P(('dp', 'seq')), may hold values from -1 to 1, as said below
- basis_right: float32 [448, 128, 128], P(('dp', 'seq')), may hold values from -1 to 1, as said below
- out_grad: bfloat16 [8, 1024, 768], P('dp', 'seq'), may hold values from -6 to 6
Outputs:
- output: bfloat16 [8, 1024, 768], P('dp', 'seq')
- input_grad: float32 [8, 1024, 768], P('dp', 'seq')
- fraction: float32 [8], P('dp')
- moment_first: float32 [448, 128, 128], P(('dp', 'seq'))
- moment_second: float32 [448, 128, 128], P(('dp', 'seq'))
- new_weights: float32 [448, 128, 128], P(('dp', 'seq'))
- gain_update: float32 [2, 768], replicated
- gain_moment: float32 [2, 768], replicated
- gain_square: float32 [2, 768], replicated
The draws below stay inside these ranges and needn't reach their ends.
Inputs may be any that keep to these rules, and one draw needn't show every extreme that they name: `segment_ids`: segment numbers never fall along a row; each segment has 1 to 512 positions, one exactly that many. `slot_tiles`: a permutation of the slot numbers; a slot whose entry is 432 or more holds no tile. `basis_left`: each slot's matrix is orthogonal. `basis_right`: each slot's matrix is orthogonal.
All inputs are finite; a program needn't handle non-finite values.
Results may differ from the reference program's by a relative error of at most 0.011.
Values may be sent and summed in bfloat16 or wider, within the bound.
No kernel may reach another device: no remote copies, remote signals or barrier semaphores. Data moves between devices by JAX's collectives and lax.ppermute only.
A program may use at most 192 MiB of HBM per device.

```python
import math
import jax
import jax.numpy as jnp
import numpy as np
from jax import lax

D = 768
H = 12
HD = 64
FF = 3072
LEN = 1024
B = 128
STEP = 3
ROWS = 8
TILES = 432
SLOTS = 448


def slot_order(key):
    return jax.random.permutation(jax.random.fold_in(key, 17), SLOTS).astype(jnp.int32)


def draw_slot_tiles(key, part):
    return slot_order(key)


def draw_weight_slots(key, part):
    tile_ids = slot_order(key)
    area = B * B
    first_end = 3 * D * D // area
    second_end = first_end + D * D // area
    third_end = second_end + D * FF // area
    fourth_end = third_end + FF * D // area
    scale = jnp.where(tile_ids < first_end, D ** (-0.5), jnp.where(tile_ids < second_end, (D // 16) ** (-0.5), jnp.where(tile_ids < third_end, D ** (-0.5), jnp.where(tile_ids < fourth_end, FF ** (-0.5), D ** (-0.5)))))
    head_factor = min(1.0, 48.0 / LEN)
    across_tiles = 3 * D // B
    lead_column = (tile_ids < first_end) & (tile_ids % across_tiles == 0)
    scale = scale * jnp.where(lead_column, head_factor, 1.0)
    noise = jax.random.normal(jax.random.fold_in(key, 23), (SLOTS, B, B), jnp.float32)
    return jnp.clip(noise, -6.0, 6.0) * scale.astype(jnp.float32)[:, None, None]


def orthogonal_tiles(key):
    subkeys = jax.random.split(key, 3)
    counter = jnp.arange(B, dtype=jnp.float32)
    table = jnp.cos(math.pi * (2.0 * counter[None, :] + 1.0) * counter[:, None] / (2.0 * B)) * (2.0 / B) ** 0.5
    table = table * jnp.where(counter == 0.0, 0.5 ** 0.5, 1.0)[:, None]
    orders = jax.vmap(lambda subkey: jax.random.permutation(subkey, B))(jax.random.split(subkeys[0], SLOTS))
    left_signs = jnp.where(jax.random.bernoulli(subkeys[1], 0.5, (SLOTS, B)), 1.0, -1.0)
    right_signs = jnp.where(jax.random.bernoulli(subkeys[2], 0.5, (SLOTS, B)), 1.0, -1.0)
    return (left_signs[:, :, None] * table[orders] * right_signs[:, None, :]).astype(jnp.float32)


def draw_basis_left(key, part):
    return orthogonal_tiles(jax.random.fold_in(key, 31))


def draw_basis_right(key, part):
    return orthogonal_tiles(jax.random.fold_in(key, 37))


def place_ends(array, key, low, largest):
    index_at = [jax.random.randint(jax.random.fold_in(key, axis), (), 0, length) for axis, length in enumerate(array.shape)]
    widest = array.shape.index(max(array.shape))
    beside = index_at[:widest] + [(index_at[widest] + 1) % array.shape[widest]] + index_at[widest + 1:]
    return array.at[tuple(index_at)].set(low).at[tuple(beside)].set(largest)


def steps_of(rng, extent, shards, low, high):
    level = 1.0
    for axis_at, shards_of in shards:
        draws = jax.random.uniform(jax.random.fold_in(jax.random.fold_in(rng, 6), axis_at), (shards_of,), jnp.float32, low / len(shards), high / len(shards))
        level = level * jnp.repeat(jnp.exp(draws), extent[axis_at] // shards_of).reshape((-1,) + (1,) * (len(extent) - 1 - axis_at))
    return level


def profile(count, total, most, slope):
    weights = [(1 << 20) // math.isqrt(grade ** slope) + 1 for grade in range(2, count + 1)]
    spare, counts = total - most - (count - 1), [1] * (count - 1)
    while spare > 0:
        candidates = [i for i in range(count - 1) if counts[i] < most]
        mass, left = sum([weights[i] for i in candidates]), spare
        for i in candidates:
            addition = min(most - counts[i], max(1, left * weights[i] // mass), spare)
            counts[i] = counts[i] + addition
            spare = spare - addition
    return np.array([most] + counts)


def ragged_sizes(key, amount, total, bound, skew):
    if amount == 2:
        one = jax.random.randint(key, (), max(1, total - bound), min(bound, total - 1) + 1)
        return jnp.stack([one, total - one])
    sizes = jnp.asarray(profile(amount, total, bound, skew), jnp.int32)
    couples = (amount - 1) // 2
    giver, taker = sizes[1:1 + 2 * couples:2], sizes[2:2 + 2 * couples:2]
    room = jnp.minimum(giver - 1, bound - taker)
    moved = jax.random.randint(jax.random.fold_in(key, 1), (couples,), 0, 1 << 20) % (room + 1)
    sizes = sizes.at[1:1 + 2 * couples:2].set(giver - moved).at[2:2 + 2 * couples:2].set(taker + moved)
    return sizes[jax.random.permutation(jax.random.fold_in(key, 2), amount)]


def bell_draw(key, dims, scale, reach, cuts=(), kind=jnp.bfloat16):
    factor_of = steps_of(key, dims, cuts, -0.22, 0.18) if cuts else 1.0
    drawn = jax.random.normal(key, dims, jnp.float32) * scale * factor_of
    return jnp.minimum(jnp.maximum(drawn, -reach), reach).astype(kind)


def setup_inputs(seed: int = 0) -> dict:
    seeds = jax.random.split(jax.random.key(seed), 15)
    return {
        "tokens": bell_draw(seeds[0], (ROWS, LEN, D), 1.0, 6.0, ((0, 8), (1, 4))),
        "segment_ids": jax.vmap(lambda own: jnp.searchsorted(jnp.cumsum(ragged_sizes(own, 6, LEN, LEN // 2, 0)), jnp.arange(LEN), side="right"))(jax.random.split(seeds[1], ROWS)).reshape((ROWS, LEN)).astype(jnp.int32),
        "pad_lengths": place_ends(jax.random.randint(seeds[2], (ROWS,), 0, LEN // 2), jax.random.fold_in(seeds[2], 1), 0, (LEN // 2) - 1).astype(jnp.int32),
        "threshold": jnp.clip(jnp.exp(jax.random.uniform(seeds[3], (1,), jnp.float32, math.log(0.05), math.log(2.0))), 0.05, 2.0),
        "gains": jnp.clip(1.0 + 0.1 * jax.random.normal(seeds[4], (2, D), jnp.float32), 0.5, 1.5),
        "gain_first": bell_draw(seeds[5], (2, D), (0.5 * (ROWS * LEN) ** 0.5), 256.0, (), jnp.float32),
        "gain_second": jnp.clip(jnp.exp(jax.random.uniform(seeds[6], (2, D), jnp.float32, math.log(2048.0), math.log(8192.0))), 2048.0, 8192.0),
        "slot_tiles": draw_slot_tiles(jax.random.fold_in(seeds[14], 71), 0),
        "weight_slots": draw_weight_slots(jax.random.fold_in(seeds[14], 71), 0),
        "first_moment": bell_draw(seeds[9], (SLOTS, B, B), (0.3 * (ROWS * LEN) ** 0.5), 160.0, ((0, 32),), jnp.float32),
        "second_moment": jnp.clip(jnp.exp(math.log(3276.8) - 1.3862944 * jax.random.uniform(seeds[10], (SLOTS, B, B), jnp.float32) ** steps_of(seeds[10], (SLOTS, B, B), ((0, 32),), -0.2, 0.2)), 819.2, 3276.8),
        "basis_left": draw_basis_left(jax.random.fold_in(seeds[14], 71), 0),
        "basis_right": draw_basis_right(jax.random.fold_in(seeds[14], 71), 0),
        "out_grad": bell_draw(seeds[13], (ROWS, LEN, D), 1.0, 6.0, ((0, 8), (1, 4))),
    }


select_scale = 0.2
fraction_slope = 2.0
first_decay = 0.5
second_decay = 0.5
adam_epsilon = 1e-08
weight_rate = 0.05
gain_rate = 0.2
decay_rate = 0.1
norm_epsilon = 1e-05
precise = lax.Precision.HIGHEST

@jax.custom_vjp
def low(v):
    return lax.optimization_barrier(v.astype(jnp.bfloat16)).astype(jnp.float32)

@jax.custom_vjp
def low_back(v):
    return v

def low_keep(v):
    return (low(v), None)

def low_pass(kept, grad):
    return (grad,)

def back_keep(v):
    return (v, None)

def back_low(kept, grad):
    return (low(grad),)
low.defvjp(low_keep, low_pass)
low_back.defvjp(back_keep, back_low)

def layer_norm(values, gain):
    centred = values - lax.optimization_barrier(jnp.mean(values, axis=-1, keepdims=True))
    spread = lax.optimization_barrier(jnp.mean(centred * centred, axis=-1, keepdims=True))
    return centred * lax.rsqrt(spread + norm_epsilon) * gain

def tiles_of(matrix, tile_side):
    height, across = matrix.shape
    shaped = matrix.reshape(height // tile_side, tile_side, across // tile_side, tile_side)
    return shaped.transpose(0, 2, 1, 3).reshape(-1, tile_side, tile_side)

def matrix_of(tile_stack, height, across):
    tile_side = tile_stack.shape[-1]
    shaped = tile_stack.reshape(height // tile_side, across // tile_side, tile_side, tile_side)
    return shaped.transpose(0, 2, 1, 3).reshape(height, across)

def split_tiles(tile_stack, width, hidden_width):
    tile_side = tile_stack.shape[-1]
    shapes = [(width, 3 * width), (width, width), (width, hidden_width), (hidden_width, width)]
    result = []
    offset = 0
    for height, across in shapes:
        count_here = height * across // (tile_side * tile_side)
        result.append(matrix_of(tile_stack[offset:offset + count_here], height, across))
        offset = offset + count_here
    return result

def row_forward(row_input, w_qkv, w_out, w_up, w_down, gains, seg_row, valid_row):
    length, width = row_input.shape
    normed_pre = low(layer_norm(row_input, gains[0]))
    projected = jnp.dot(normed_pre, low(w_qkv), precision=precise)
    query_rows = low(low_back(projected[:, :width])).reshape(length, H, HD)
    key_heads = low(low_back(projected[:, width:2 * width])).reshape(length, H, HD)
    value_heads = low(low_back(projected[:, 2 * width:])).reshape(length, H, HD)
    scores = low_back(jnp.einsum('qhd,khd->hqk', query_rows, key_heads, precision=precise) * 0.125)
    places = jnp.arange(length, dtype=jnp.int32)
    allowed = (seg_row[:, None] == seg_row[None, :]) & (places[None, :] <= places[:, None])
    allowed = allowed & (valid_row[None, :] | (places[None, :] == places[:, None]))
    strict = allowed & (places[None, :] < places[:, None])
    select = select_scale * jax.nn.relu(scores[0]) * strict.astype(jnp.float32)
    shadow = jnp.cumsum(select, axis=0) - select
    logits = jnp.where(allowed[None], scores - shadow[None], -jnp.inf)
    probs = jax.nn.softmax(logits, axis=-1)
    mixed_out = jnp.einsum('hqk,khd->qhd', probs, value_heads, precision=precise).reshape(length, width)
    mixed_out = low(low_back(mixed_out))
    branch = low_back(jnp.dot(mixed_out, low(w_out), precision=precise))
    hidden_one = row_input + branch
    normed_mid = low(layer_norm(hidden_one, gains[1]))
    upper = low_back(jnp.dot(normed_mid, low(w_up), precision=precise))
    active = low(jax.nn.gelu(upper, approximate=True))
    result = hidden_one + jnp.dot(active, low(w_down), precision=precise)
    return (result, lax.optimization_barrier(jnp.sum(select, axis=0)))

def rotated_adam(grad_slots, first, second, left, right, weight, correction):
    turned = jnp.einsum('sji,sjk->sik', left, grad_slots, precision=precise)
    turned = jnp.einsum('sik,skl->sil', turned, right, precision=precise)
    first_new = first_decay * first + (1.0 - first_decay) * turned
    second_new = second_decay * second + (1.0 - second_decay) * turned * turned
    norm_step = first_new / correction / (jnp.sqrt(second_new / correction) + adam_epsilon)
    back = jnp.einsum('sik,skl->sil', left, norm_step, precision=precise)
    back = jnp.einsum('sil,sjl->sij', back, right, precision=precise)
    return (first_new, second_new, weight - weight_rate * back - weight_rate * decay_rate * weight)

def reference(tokens, segment_ids, pad_lengths, threshold, gains, gain_first, gain_second, slot_tiles, weight_slots, first_moment, second_moment, basis_left, basis_right, out_grad):
    tile_ids = jnp.arange(TILES, dtype=jnp.int32)
    slot_ids = jnp.arange(SLOTS, dtype=jnp.int32)
    position = lax.optimization_barrier(jnp.sum(jnp.where(slot_tiles[None, :] == tile_ids[:, None], slot_ids[None, :], 0), axis=1)).astype(jnp.int32)
    w_qkv, w_out, w_up, w_down = split_tiles(weight_slots[position], D, FF)
    length = LEN

    def per_row(sums, row_data):
        row_input, seg_row, pad_row, row_grad = row_data
        valid_row = jnp.arange(length, dtype=jnp.int32) < length - pad_row

        def forward(values, first_w, second_w, third_w, fourth_w, gain_pair):
            return row_forward(values, first_w, second_w, third_w, fourth_w, gain_pair, seg_row, valid_row)
        result, pullback, selected = jax.vjp(forward, row_input.astype(jnp.float32), w_qkv, w_out, w_up, w_down, gains, has_aux=True)
        grads = pullback(row_grad.astype(jnp.float32))
        counted = jnp.sum(valid_row.astype(jnp.float32) * jax.nn.sigmoid((selected - threshold[0]) * fraction_slope))
        fraction_row = counted / (length - pad_row).astype(jnp.float32)
        new_sums = tuple((total + grad for total, grad in zip(sums, grads[1:])))
        return (new_sums, (result.astype(jnp.bfloat16), grads[0], fraction_row))
    start_sums = (jnp.zeros_like(w_qkv), jnp.zeros_like(w_out), jnp.zeros_like(w_up), jnp.zeros_like(w_down), jnp.zeros_like(gains))
    sums, (output, input_grad, fraction) = lax.scan(per_row, start_sums, (tokens, segment_ids, pad_lengths, out_grad))
    grad_tiles = jnp.concatenate([tiles_of(total, B) for total in sums[:4]] + [jnp.zeros((1, B, B), jnp.float32)], axis=0)
    grad_slots = grad_tiles[jnp.minimum(slot_tiles, TILES)]
    correction = 1.0 - first_decay ** STEP
    moment_first, moment_second, new_weights = rotated_adam(grad_slots, first_moment, second_moment, basis_left, basis_right, weight_slots, correction)
    gain_grad = sums[4]
    gain_moment = first_decay * gain_first + (1.0 - first_decay) * gain_grad
    gain_square = second_decay * gain_second + (1.0 - second_decay) * gain_grad * gain_grad
    gain_update = gains - gain_rate * (gain_moment / correction) / (jnp.sqrt(gain_square / correction) + adam_epsilon)
    return (output, input_grad, fraction, moment_first, moment_second, new_weights, gain_update, gain_moment, gain_square)
```

```python
import functools

import jax
import jax.numpy as jnp
from jax import lax
from jax.experimental import pallas as pl
from jax.experimental.pallas import tpu as pltpu
from jax.sharding import PartitionSpec as P

H = 12
HD = 64
FF = 3072
STEP = 3
SPAN = 512
CHUNK = 256

select_scale = 0.2
fraction_slope = 2.0
first_decay = 0.5
second_decay = 0.5
adam_epsilon = 1e-08
weight_rate = 0.05
gain_rate = 0.2
decay_rate = 0.1
norm_epsilon = 1e-05
precise = lax.Precision.HIGHEST

BF = jnp.bfloat16
F32 = jnp.float32
VMEM = pltpu.VMEM
SMEM = pltpu.SMEM


def mm(a, b):
    return lax.dot_general(a, b, (((1,), (0,)), ((), ())), preferred_element_type=F32)


def mm_nt(a, b):
    return lax.dot_general(a, b, (((1,), (1,)), ((), ())), preferred_element_type=F32)


def split(x):
    high = x.astype(BF)
    return high, (x - high.astype(F32)).astype(BF)


def mm_split(x, exact):
    high, rest = split(x)
    return mm(high, exact) + mm(rest, exact)


def lane_half(shape, second):
    lane = lax.broadcasted_iota(jnp.int32, shape, 1)
    return (lane >= HD) if second else (lane < HD)


def keep_half(x, second):
    return jnp.where(lane_half(x.shape, second), x, jnp.zeros_like(x))


def norm_parts(x):
    centred = x - jnp.mean(x, axis=-1, keepdims=True)
    rate = lax.rsqrt(jnp.mean(centred * centred, axis=-1, keepdims=True) + norm_epsilon)
    return centred * rate, rate


def send_tile(tile_ref, dst, keep, send, sem):
    half = keep.shape[0]

    @pl.when(dst < half)
    def _():
        pltpu.make_async_copy(tile_ref, keep.at[dst], sem).start()

    @pl.when(dst >= half)
    def _():
        pltpu.make_async_copy(tile_ref, send.at[dst - half], sem).start()


def layer_kernel(
    tiles,
    src,
    dst,
    scal,
    thr,
    tok,
    gains,
    dy,
    segc,
    segr,
    w_hbm,
    out,
    ghid,
    gq,
    gk,
    gv,
    nrm_t,
    wqkv,
    q0,
    k0t,
    part0,
    mask0,
    colsum,
    small,
    keep,
    send,
    wall,
    nrm,
    q_s,
    q_e,
    k_s,
    v_s,
    kt_s,
    vt_s,
    bias,
    gsh,
    probs,
    mixt,
    mixb,
    mixbt,
    wout,
    hid,
    xhat,
    nm,
    nmt,
    acc,
    gmid,
    g_s,
    gt_s,
    wu,
    wd,
    stage,
    zero,
    wsem,
    gsem,
    zsem,
):
    n_qkv, n_out, n_up, n_down = tiles
    width = tok.shape[1]
    own = dy.shape[0]
    window = tok.shape[0]
    back = window - own
    side = wall.shape[-1]
    dt = width // side
    pairs = width // side
    total_slots = 2 * keep.shape[0]
    load = pltpu.make_async_copy(w_hbm, wall, wsem)
    load.start()
    zero[...] = jnp.zeros_like(zero)
    tile_count = n_qkv + n_out + n_up + n_down
    empty = total_slots - tile_count

    @pl.loop(0, empty)
    def _(e):
        send_tile(zero, dst[tile_count + e], keep, send, zsem)

    gain_pre = gains[0:1, :]
    gain_mid = gains[1:2, :]

    @pl.loop(0, window // own)
    def _(b):
        rows = pl.ds(pl.multiple_of(b * own, own), own)
        hat, _ = norm_parts(tok[rows, :].astype(F32))
        value = (hat * gain_pre).astype(BF)
        nrm[rows, :] = value
        nrm_t[:, rows] = value.T

    load.wait()
    per_row = 3 * dt

    @pl.loop(0, 3 * dt // 2)
    def _(j):
        for i in range(dt):
            for jj in range(2):
                wqkv[i * side : (i + 1) * side, pl.ds(pl.multiple_of((2 * j + jj) * side, side), side)] = wall[
                    src[i * per_row + 2 * j + jj]
                ]

    for i in range(dt):
        for j in range(dt):
            wout[i * side : (i + 1) * side, j * side : (j + 1) * side] = wall[src[n_qkv + i * dt + j]]

    @pl.loop(0, dt // 2)
    def _(j):
        cols = pl.ds(pl.multiple_of(2 * j * side, 2 * side), 2 * side)
        got = (mm(nrm[back:, :], wqkv[:, cols]) * 0.125).astype(BF)
        q_s[2 * j] = got[:, :side]
        q_s[2 * j + 1] = got[:, side:]

    q_e[...] = (mm(nrm[:back, :], wqkv[:, 0:side]) * 0.125).astype(BF)

    @pl.loop(0, dt // 2)
    def _(j):
        cols = pl.ds(pl.multiple_of(width + 2 * j * side, 2 * side), 2 * side)
        got = mm(nrm[...], wqkv[:, cols]).astype(BF)
        got_t = got.T
        k_s[2 * j] = got[:, :side]
        k_s[2 * j + 1] = got[:, side:]
        kt_s[2 * j] = got_t[:side, :]
        kt_s[2 * j + 1] = got_t[side:, :]

    @pl.loop(0, dt // 2)
    def _(j):
        cols = pl.ds(pl.multiple_of(2 * width + 2 * j * side, 2 * side), 2 * side)
        got = mm(nrm[...], wqkv[:, cols]).astype(BF)
        got_t = got.T
        v_s[2 * j] = got[:, :side]
        v_s[2 * j + 1] = got[:, side:]
        vt_s[2 * j] = got_t[:side, :]
        vt_s[2 * j + 1] = got_t[side:, :]

    q0[...] = q_s[0]
    k0t[...] = kt_s[0]

    valid_len = scal[0]
    start = scal[1]
    is_last = scal[2]
    key_at = lax.broadcasted_iota(jnp.int32, (window, own), 0)
    query_at = lax.broadcasted_iota(jnp.int32, (window, own), 1)
    key_valid = (key_at + (start - back)) < valid_len
    key_seg = segc[...]
    k_first = k_s[0]

    def selected(q_rows, first):
        s = mm_nt(k_first, keep_half(q_rows, False))
        same = key_seg == segr[:, first : first + own]
        strict = same & key_valid & (key_at < query_at + first)
        return s, same, jnp.where(strict, select_scale * jnp.maximum(s, 0.0), 0.0), strict

    prefix = jnp.zeros((window, 1), F32)
    for b in range(back // own):
        _, _, chosen, _ = selected(q_e[b * own : (b + 1) * own, :], b * own)
        prefix = prefix + jnp.sum(chosen, axis=1, keepdims=True)
    s_own, same, chosen, strict = selected(q_s[0], back)
    tri_row = lax.broadcasted_iota(jnp.int32, (own, own), 0)
    tri_col = lax.broadcasted_iota(jnp.int32, (own, own), 1)
    earlier = jnp.where(tri_row < tri_col, 1.0, 0.0).astype(BF)
    shadow = prefix + mm_split(chosen, earlier)
    allowed = strict | (same & (key_at == query_at + back))
    bias[...] = jnp.where(allowed, -shadow, -1e30)
    mask0[...] = jnp.where(strict & (s_own > 0.0), 1.0, 0.0).astype(BF)
    column_total = prefix + jnp.sum(chosen, axis=1, keepdims=True)
    key_col = lax.broadcasted_iota(jnp.int32, (window, 1), 0)
    key_pos = key_col + (start - back)
    counts = (key_pos >= 0) & (key_pos < valid_len) & ((key_col < own) | (is_last > 0))
    soft = 1.0 / (1.0 + jnp.exp(-fraction_slope * (column_total - thr[0])))
    counted = jnp.sum(jnp.where(counts, soft, 0.0), axis=0, keepdims=True)
    small[...] = jnp.zeros_like(small)
    small[1:2, :] = jnp.broadcast_to(counted / valid_len.astype(F32), (1, width))

    @pl.loop(0, pairs)
    def _(p):
        q2 = q_s[p]
        k2 = k_s[p]
        for hh in range(2):
            s = mm_nt(k2, keep_half(q2, hh == 1)) + bias[...]
            e = jnp.exp(s - jnp.max(s, axis=0, keepdims=True))
            pr = (e * (1.0 / jnp.sum(e, axis=0, keepdims=True))).astype(BF)
            probs[2 * p + hh] = pr
            vt = vt_s[p, hh * HD : (hh + 1) * HD, :]
            mixt[pl.ds(pl.multiple_of(p * side + hh * HD, HD), HD), :] = mm(vt, pr)

    mixbt[...] = mixt[...].astype(BF)
    mixb[...] = mixbt[...].T
    hid[...] = tok[back:, :].astype(F32) + mm(mixb[...], wout[...])
    hat, rate = norm_parts(hid[...])
    xhat[...] = hat
    nm[...] = (hat * gain_mid).astype(BF)
    nmt[...] = nm[...].T

    acc[...] = jnp.zeros_like(acc)
    gmid[...] = jnp.zeros_like(gmid)
    cw = CHUNK // side
    f_tiles = FF // side
    per_chunk = 2 * cw * dt
    chunks = FF // CHUNK

    @pl.loop(0, chunks)
    def _(c):
        slot = lax.rem(c, 2)
        for i in range(dt):
            for jj in range(cw):
                wu[i * side : (i + 1) * side, jj * side : (jj + 1) * side] = wall[
                    src[n_qkv + n_out + i * f_tiles + cw * c + jj]
                ]
        for ii in range(cw):
            for j in range(dt):
                wd[ii * side : (ii + 1) * side, j * side : (j + 1) * side] = wall[
                    src[n_qkv + n_out + n_up + (cw * c + ii) * dt + j]
                ]
        up = mm(nm[...], wu[...])
        cube = 0.7978845608028654 * (up + 0.044715 * up * up * up)
        th = jnp.tanh(cube)
        active = (0.5 * up * (1.0 + th)).astype(BF)
        slope = 0.5 * (1.0 + th) + 0.5 * up * (1.0 - th * th) * (
            0.7978845608028654 * (1.0 + 3.0 * 0.044715 * up * up)
        )
        acc[...] += mm(active, wd[...])
        gu = (mm_nt(dy[...], wd[...]) * slope).astype(BF)
        gmid[...] += mm_nt(gu, wu[...])

        @pl.when(c >= 2)
        def _():
            pltpu.make_async_copy(stage.at[slot], keep.at[pl.ds(0, per_chunk)], gsem.at[slot]).wait()

        g_down = mm(active.T, dy[...]).astype(BF)
        for ii in range(cw):
            for j in range(dt):
                at = ii * dt + j
                stage[slot, at] = g_down[ii * side : (ii + 1) * side, j * side : (j + 1) * side]
        g_up = mm(nmt[...], gu).astype(BF)
        for i in range(dt):
            for jj in range(cw):
                at = cw * dt + i * cw + jj
                stage[slot, at] = g_up[i * side : (i + 1) * side, jj * side : (jj + 1) * side]
        for ii in range(cw):
            for j in range(dt):
                at = ii * dt + j
                t = n_qkv + n_out + n_up + (cw * c + ii) * dt + j
                send_tile(stage.at[slot, at], dst[t], keep, send, gsem.at[slot])
        for i in range(dt):
            for jj in range(cw):
                at = cw * dt + i * cw + jj
                t = n_qkv + n_out + i * f_tiles + cw * c + jj
                send_tile(stage.at[slot, at], dst[t], keep, send, gsem.at[slot])

    out[...] = (hid[...] + acc[...]).astype(BF)
    hat = xhat[...]
    gm = gmid[...]
    small[0:1, :] = jnp.sum(gm * hat, axis=0, keepdims=True)
    scaled = gm * gain_mid
    gh = dy[...].astype(F32) + rate * (
        scaled
        - jnp.mean(scaled, axis=-1, keepdims=True)
        - hat * jnp.mean(scaled * hat, axis=-1, keepdims=True)
    )
    ghid[...] = gh
    gb = gh.astype(BF)
    gmix = mm_nt(gb, wout[...]).astype(BF)
    for p in range(pairs):
        g_s[p] = gmix[:, p * side : (p + 1) * side]
    gt_s[...] = gmix.T

    for slot in range(2):
        pltpu.make_async_copy(stage.at[slot], keep.at[pl.ds(0, per_chunk)], gsem.at[slot]).wait()
    half_out = dt // 2
    for part in range(2):
        g_out = mm(mixbt[part * half_out * side : (part + 1) * half_out * side, :], gb).astype(BF)
        for i in range(half_out):
            for j in range(dt):
                stage[part, i * dt + j] = g_out[i * side : (i + 1) * side, j * side : (j + 1) * side]
        for i in range(half_out):
            for j in range(dt):
                t = n_qkv + (part * half_out + i) * dt + j
                send_tile(stage.at[part, i * dt + j], dst[t], keep, send, gsem.at[part])

    gsh[...] = jnp.zeros_like(gsh)

    @pl.loop(0, pairs)
    def _(p):
        g2 = g_s[p]
        q2 = q_s[p]
        v2 = v_s[p]
        later = jnp.where(p > 0, 1.0, 0.0)
        dk = jnp.zeros((window, side), F32)
        dv = jnp.zeros((window, side), F32)
        dqs = []
        for hh in range(2):
            rows = pl.ds(pl.multiple_of(p * side + hh * HD, HD), HD)
            delta = jnp.sum(gt_s[rows, :].astype(F32) * mixt[rows, :], axis=0, keepdims=True)
            gm2 = keep_half(g2, hh == 1)
            pr = probs[2 * p + hh]
            dl = pr.astype(F32) * (mm_nt(v2, gm2) - delta)
            gsh[...] += dl
            dv = dv + mm(pr, gm2)
            gs = dl.astype(BF)
            dq = mm(kt_s[p, hh * HD : (hh + 1) * HD, :], gs)
            dk_h = mm(gs, keep_half(q2, hh == 1))
            if hh == 0:
                dq = dq * later
                dk_h = dk_h * later

                @pl.when(p == 0)
                def _():
                    part0[...] = dl

            dqs.append(dq)
            dk = dk + dk_h
        cols = pl.ds(pl.multiple_of(p * side, side), side)
        gq[:, cols] = (jnp.concatenate(dqs, axis=0) * 0.125).T.astype(BF)
        gk[:, cols] = dk.astype(BF)
        gv[:, cols] = dv.astype(BF)

    ones = jnp.ones((8, own), BF)
    high, rest = split(-gsh[...])
    colsum[...] = mm_nt(ones, high) + mm_nt(ones, rest)
    after = jnp.where(tri_row > tri_col, 1.0, 0.0).astype(BF)
    part0[...] += select_scale * mask0[...].astype(F32) * (mm(high, after) + mm(rest, after))

    for part in range(2):
        pltpu.make_async_copy(
            stage.at[part, pl.ds(0, half_out * dt)], keep.at[pl.ds(0, half_out * dt)], gsem.at[part]
        ).wait()
    pltpu.make_async_copy(keep.at[pl.ds(0, empty)], keep.at[pl.ds(0, empty)], zsem).wait()


def qkv_kernel(
    dst, part0, mask0, suffix, q0, k0t, gq, gk, gv, nrm_t, keep_in, send_in, gq_out, gk_out, keep, send, stage, gsem
):
    own, width = gq.shape
    window = gk.shape[0]
    side = stage.shape[-1]
    dt = width // side
    back = window - own
    column = jnp.broadcast_to(suffix[0:1, :], (side, window)).T
    column = jnp.concatenate([column] * (own // side), axis=1)
    gs = (part0[...] + select_scale * mask0[...].astype(F32) * column).astype(BF)
    dq = (mm(k0t[0:HD, :], gs) * 0.125).T
    dk = mm(gs, keep_half(q0[...], False)).astype(BF)
    gq_out[...] = gq[...]
    gk_out[...] = gk[...]
    gq_out[:, 0:side] = gq[:, 0:side] + jnp.concatenate([dq, jnp.zeros_like(dq)], axis=1).astype(BF)
    gk_out[:, 0:side] = gk[:, 0:side] + dk

    for which in range(3):
        for jc in range(dt // 2):
            cols = slice(2 * jc * side, 2 * (jc + 1) * side)
            if which == 0:
                g = mm(nrm_t[:, back:], gq_out[:, cols])
            elif which == 1:
                g = mm(nrm_t[...], gk_out[:, cols])
            else:
                g = mm(nrm_t[...], gv[:, cols])
            g = g.astype(BF)
            for i in range(dt):
                for jj in range(2):
                    j = which * dt + 2 * jc + jj
                    t = i * 3 * dt + j
                    stage[t] = g[i * side : (i + 1) * side, jj * side : (jj + 1) * side]
                    send_tile(stage.at[t], dst[t], keep, send, gsem)
    count = 3 * dt * dt
    pltpu.make_async_copy(stage, keep.at[pl.ds(0, count)], gsem).wait()


def pre_kernel(tok, gq, gk, gv, wqkv, far, near, mine, small):
    own, width = gq.shape
    window = gk.shape[0]
    back = window - own
    total = jnp.zeros((1, width), F32)
    for b in range(window // own):
        rows = slice(b * own, (b + 1) * own)
        g = mm_nt(gk[rows, :], wqkv[:, width : 2 * width]) + mm_nt(gv[rows, :], wqkv[:, 2 * width :])
        if b == window // own - 1:
            g = g + mm_nt(gq[...], wqkv[:, :width])
            mine[...] = g
        elif b == 0:
            far[...] = g.astype(far.dtype)
        else:
            near[...] = g.astype(near.dtype)
        hat, _ = norm_parts(tok[rows, :].astype(F32))
        total = total + jnp.sum(g * hat, axis=0, keepdims=True)
    small[...] = jnp.broadcast_to(total, small.shape)


def input_kernel(tok, gains, ghid, mine, near, far, out):
    hat, rate = norm_parts(tok[...].astype(F32))
    g = mine[...] + near[...].astype(F32) + far[...].astype(F32)
    scaled = g * gains[0:1, :]
    out[...] = ghid[...] + rate * (
        scaled
        - jnp.mean(scaled, axis=-1, keepdims=True)
        - hat * jnp.mean(scaled * hat, axis=-1, keepdims=True)
    )


def rotated_adam(grad_slots, first, second, left, right, weight, correction):
    turned = jnp.einsum("sji,sjk->sik", left, grad_slots, precision=precise)
    turned = jnp.einsum("sik,skl->sil", turned, right, precision=precise)
    first_new = first_decay * first + (1.0 - first_decay) * turned
    second_new = second_decay * second + (1.0 - second_decay) * turned * turned
    norm_step = first_new / correction / (jnp.sqrt(second_new / correction) + adam_epsilon)
    back = jnp.einsum("sik,skl->sil", left, norm_step, precision=precise)
    back = jnp.einsum("sil,sjl->sij", back, right, precision=precise)
    return (first_new, second_new, weight - weight_rate * back - weight_rate * decay_rate * weight)


def bit_plan(devices, per_device):
    bits = [1 << b for b in range(devices.bit_length() - 1)]
    first, rest = bits[0], bits[1:]
    if devices == 32:
        orders = [(2, 4, 8, 16), (4, 8, 2, 16), (8, 16, 2, 4)]
    else:
        orders = [tuple(rest[i:] + rest[:i]) for i in range(3)]
    third = per_device * 3 // 7
    sizes = [third, per_device - third] if per_device < 4 else [third, per_device * 5 // 14, 0]
    if len(sizes) == 3:
        sizes[2] = per_device - sizes[0] - sizes[1]
    plan = []
    at = 0
    for size, order in zip(sizes, orders):
        if size:
            plan.append((at, size, order))
            at += size
    return first, plan


def local(
    tokens,
    segment_ids,
    pad_lengths,
    threshold,
    gains,
    gain_first,
    gain_second,
    slot_tiles,
    weight_slots,
    first_moment,
    second_moment,
    basis_left,
    basis_right,
    out_grad,
):
    axes = ("dp", "seq")
    n_dp, n_seq = lax.axis_size("dp"), lax.axis_size("seq")
    devices = n_dp * n_seq
    me = lax.axis_index(axes)
    seq_at = lax.axis_index("seq")
    _, own, width = tokens.shape
    length = segment_ids.shape[1]
    side = weight_slots.shape[-1]
    per_device = weight_slots.shape[0]
    slot_total = slot_tiles.shape[0]
    dt = width // side
    tiles = (3 * dt * dt, dt * dt, dt * (FF // side), dt * (FF // side))
    tile_count = sum(tiles)
    back = SPAN
    window = back + own

    shared = lax.all_gather(weight_slots.astype(BF), axes, axis=0, tiled=True)

    slot_ids = jnp.arange(slot_total, dtype=jnp.int32)
    position = jnp.sum(
        jnp.where(slot_tiles[None, :] == slot_ids[:, None], slot_ids[None, :], 0), axis=1
    )
    owner = position // per_device
    inner = position % per_device
    apart = owner ^ me
    first_bit, plan = bit_plan(devices, per_device)
    half = slot_total // 2
    spread = devices // 2
    place = jnp.zeros_like(position)
    for at, size, order in plan:
        index = jnp.zeros_like(position)
        for bit in order:
            index = index * 2 + ((apart & bit) != 0).astype(jnp.int32)
        here = at * spread + index * size + (inner - at)
        place = jnp.where((inner >= at) & (inner < at + size), here, place)
    dst = place + jnp.where((apart & first_bit) != 0, half, 0)
    src = position

    mine_tok = tokens[0]
    pieces = []
    for step in range(back // own, 0, -1):
        pieces.append(lax.ppermute(mine_tok, "seq", [(i, i + step) for i in range(n_seq - step)]))
    tok = jnp.concatenate(pieces + [mine_tok], axis=0)
    start = seq_at * own
    seg_window = lax.dynamic_slice_in_dim(
        jnp.concatenate([jnp.full((back,), -1, jnp.int32), segment_ids[0]]), start, window
    )
    valid_len = length - pad_lengths[0]
    scal = jnp.stack([valid_len, start, (seq_at == n_seq - 1).astype(jnp.int32)])

    hbm = pl.BlockSpec(memory_space=pl.ANY)
    vm = pl.BlockSpec(memory_space=VMEM)
    sm = pl.BlockSpec(memory_space=SMEM)
    shp = jax.ShapeDtypeStruct
    tile_buffer = shp((half, side, side), BF)


    per_chunk = 2 * (CHUNK // side) * dt
    outs = pl.pallas_call(
        functools.partial(layer_kernel, tiles),
        out_shape=(
            shp((own, width), BF),
            shp((own, width), F32),
            shp((own, width), BF),
            shp((window, width), BF),
            shp((window, width), BF),
            shp((width, window), BF),
            shp((width, 3 * width), BF),
            shp((own, side), BF),
            shp((side, window), BF),
            shp((window, own), F32),
            shp((window, own), BF),
            shp((8, window), F32),
            shp((8, width), F32),
            tile_buffer,
            tile_buffer,
        ),
        in_specs=[sm] * 4 + [vm] * 5 + [hbm],
        out_specs=tuple([vm] * 13 + [hbm] * 2),
        scratch_shapes=[
            VMEM((slot_total, side, side), BF),
            VMEM((window, width), BF),
            VMEM((dt, own, side), BF),
            VMEM((back, side), BF),
            VMEM((dt, window, side), BF),
            VMEM((dt, window, side), BF),
            VMEM((dt, side, window), BF),
            VMEM((dt, side, window), BF),
            VMEM((window, own), F32),
            VMEM((window, own), F32),
            VMEM((H, window, own), BF),
            VMEM((width, own), F32),
            VMEM((own, width), BF),
            VMEM((width, own), BF),
            VMEM((width, width), BF),
            VMEM((own, width), F32),
            VMEM((own, width), F32),
            VMEM((own, width), BF),
            VMEM((width, own), BF),
            VMEM((own, width), F32),
            VMEM((own, width), F32),
            VMEM((dt, own, side), BF),
            VMEM((width, own), BF),
            VMEM((width, CHUNK), BF),
            VMEM((CHUNK, width), BF),
            VMEM((2, per_chunk, side, side), BF),
            VMEM((side, side), BF),
            pltpu.SemaphoreType.DMA,
            pltpu.SemaphoreType.DMA((2,)),
            pltpu.SemaphoreType.DMA,
        ],
        compiler_params=pltpu.CompilerParams(vmem_limit_bytes=60 << 20),
        name="layer",
    )(
        src,
        dst,
        scal,
        threshold,
        tok,
        gains,
        out_grad[0],
        seg_window[:, None],
        seg_window[None, :],
        shared,
    )
    (output, ghid, gq, gk, gv, nrm_t, wqkv, q0, k0t, part0, mask0, colsum, small, keep, send) = outs

    sums = colsum[0]
    suffix = jnp.zeros((window,), F32)
    for step in range(1, back // own + 1):
        reach = window - step * own
        got = lax.ppermute(sums[:reach], "seq", [(i, i - step) for i in range(step, n_seq)])
        suffix = suffix + jnp.concatenate([jnp.zeros((step * own,), F32), got])
    suffix = jnp.broadcast_to(suffix[None, :], (8, window))

    gq, gk, keep, send = pl.pallas_call(
        qkv_kernel,
        out_shape=(shp((own, width), BF), shp((window, width), BF), tile_buffer, tile_buffer),
        in_specs=[sm] + [vm] * 9 + [hbm] * 2,
        out_specs=(vm, vm, hbm, hbm),
        scratch_shapes=[VMEM((tiles[0], side, side), BF), pltpu.SemaphoreType.DMA],
        input_output_aliases={10: 2, 11: 3},
        compiler_params=pltpu.CompilerParams(vmem_limit_bytes=40 << 20),
        name="qkv_grad",
    )(dst, part0, mask0, suffix, q0, k0t, gq, gk, gv, nrm_t, keep, send)

    def swap(x, bit):
        return lax.ppermute(x, axes, [(i, i ^ bit) for i in range(devices)])

    def plus(a, b):
        return (a.astype(F32) + b.astype(F32)).astype(BF)

    parts = []
    for at, size, order in plan:
        rows = slice(at * spread, (at + size) * spread)
        parts.append(plus(keep[rows], swap(send[rows], first_bit)))
    for step in range(len(plan[0][2])):
        for which, (_, _, order) in enumerate(plan):
            middle = parts[which].shape[0] // 2
            parts[which] = plus(parts[which][:middle], swap(parts[which][middle:], order[step]))
    owned_grad = jnp.concatenate(parts, axis=0).astype(F32)

    far, near, mine, small_pre = pl.pallas_call(
        pre_kernel,
        out_shape=(
            shp((own, width), BF),
            shp((own, width), BF),
            shp((own, width), F32),
            shp((8, width), F32),
        ),
        in_specs=[vm] * 5,
        out_specs=tuple([vm] * 4),
        compiler_params=pltpu.CompilerParams(vmem_limit_bytes=40 << 20),
        name="pre_grad",
    )(tok, gq, gk, gv, wqkv)
    far = lax.ppermute(far, "seq", [(i, i - 2) for i in range(2, n_seq)])
    near = lax.ppermute(near, "seq", [(i, i - 1) for i in range(1, n_seq)])
    input_grad = pl.pallas_call(
        input_kernel,
        out_shape=shp((own, width), F32),
        in_specs=[vm] * 6,
        out_specs=vm,
        compiler_params=pltpu.CompilerParams(vmem_limit_bytes=20 << 20),
        name="input_grad",
    )(mine_tok, gains, ghid, mine, near, far)

    row_at = lax.axis_index("dp")
    spots = jnp.arange(width, dtype=jnp.int32)
    totals = jnp.stack([small_pre[0], small[0], jnp.where(spots == row_at, small[1], 0.0)])
    bit = 1
    while bit < devices:
        totals = totals + swap(totals, bit)
        bit *= 2
    gain_total = totals[:2]
    fraction = lax.dynamic_slice_in_dim(totals[2], row_at, 1)

    correction = 1.0 - first_decay**STEP
    moment_first, moment_second, new_weights = rotated_adam(
        owned_grad, first_moment, second_moment, basis_left, basis_right, weight_slots, correction
    )
    gain_moment = first_decay * gain_first + (1.0 - first_decay) * gain_total
    gain_square = second_decay * gain_second + (1.0 - second_decay) * gain_total * gain_total
    gain_update = gains - gain_rate * (gain_moment / correction) / (
        jnp.sqrt(gain_square / correction) + adam_epsilon
    )
    return (
        output[None],
        input_grad[None],
        fraction,
        moment_first,
        moment_second,
        new_weights,
        gain_update,
        gain_moment,
        gain_square,
    )


def solution(mesh):
    in_specs = (
        P("dp", "seq", None),
        P("dp", None),
        P("dp"),
        P(),
        P(),
        P(),
        P(),
        P(),
        P(("dp", "seq"), None, None),
        P(("dp", "seq"), None, None),
        P(("dp", "seq"), None, None),
        P(("dp", "seq"), None, None),
        P(("dp", "seq"), None, None),
        P("dp", "seq", None),
    )
    out_specs = (
        P("dp", "seq", None),
        P("dp", "seq", None),
        P("dp"),
        P(("dp", "seq"), None, None),
        P(("dp", "seq"), None, None),
        P(("dp", "seq"), None, None),
        P(),
        P(),
        P(),
    )
    return jax.shard_map(local, mesh=mesh, in_specs=in_specs, out_specs=out_specs, check_vma=False)
```

```python
import functools

import jax
import jax.numpy as jnp
from jax import lax
from jax.experimental import pallas as pl
from jax.experimental.pallas import tpu as pltpu
from jax.sharding import PartitionSpec as P

H = 12
HD = 64
FF = 3072
STEP = 3
SPAN = 512
CHUNK = 768
ADAM_GROUP = 7

select_scale = 0.2
fraction_slope = 2.0
first_decay = 0.5
second_decay = 0.5
adam_epsilon = 1e-08
weight_rate = 0.05
gain_rate = 0.2
decay_rate = 0.1
norm_epsilon = 1e-05

BF = jnp.bfloat16
F32 = jnp.float32
VMEM = pltpu.VMEM
SMEM = pltpu.SMEM


def mm(a, b):
    return lax.dot_general(a, b, (((1,), (0,)), ((), ())), preferred_element_type=F32)


def mm_nt(a, b):
    return lax.dot_general(a, b, (((1,), (1,)), ((), ())), preferred_element_type=F32)


def split(x):
    high = x.astype(BF)
    return high, (x - high.astype(F32)).astype(BF)


def mm_split(x, exact):
    high, rest = split(x)
    return mm(high, exact) + mm(rest, exact)


def lane_half(shape, second):
    lane = lax.broadcasted_iota(jnp.int32, shape, 1)
    return (lane >= HD) if second else (lane < HD)


def keep_half(x, second):
    return jnp.where(lane_half(x.shape, second), x, jnp.zeros_like(x))


def norm_parts(x):
    centred = x - jnp.mean(x, axis=-1, keepdims=True)
    rate = lax.rsqrt(jnp.mean(centred * centred, axis=-1, keepdims=True) + norm_epsilon)
    return centred * rate, rate


def send_tile(tile_ref, dst, sums, sem):
    stay, away = sums
    half = stay.shape[0]

    @pl.when(dst < half)
    def _():
        pltpu.make_async_copy(tile_ref, stay.at[dst], sem).start()

    @pl.when(dst >= half)
    def _():
        pltpu.make_async_copy(tile_ref, away.at[dst - half], sem).start()


def wait_tiles(stage_ref, sums, sem):
    pltpu.make_async_copy(stage_ref, sums[0].at[pl.ds(0, stage_ref.shape[0])], sem).wait()


def mm3(a, b):
    (ah, al), (bh, bl) = a, b
    return mm(jnp.concatenate([ah, ah, al], axis=1), jnp.concatenate([bh, bl, bh], axis=0))


def mm3_nt(a, b):
    (ah, al), (bh, bl) = a, b
    return mm_nt(jnp.concatenate([ah, ah, al], axis=1), jnp.concatenate([bh, bl, bh], axis=1))


def lane_half(shape, second):
    lane = lax.broadcasted_iota(jnp.int32, shape, 1)
    return (lane >= HD) if second else (lane < HD)


def keep_half(x, second):
    return jnp.where(lane_half(x.shape, second), x, jnp.zeros_like(x))


def norm_parts(x):
    centred = x - jnp.mean(x, axis=-1, keepdims=True)
    rate = lax.rsqrt(jnp.mean(centred * centred, axis=-1, keepdims=True) + norm_epsilon)
    return centred * rate, rate


def send_tile(tile_ref, dst, sums, sem):
    stay, away = sums
    half = stay.shape[0]

    @pl.when(dst < half)
    def _():
        pltpu.make_async_copy(tile_ref, stay.at[dst], sem).start()

    @pl.when(dst >= half)
    def _():
        pltpu.make_async_copy(tile_ref, away.at[dst - half], sem).start()


def wait_tiles(stage_ref, sums, sem):
    pltpu.make_async_copy(stage_ref, sums[0].at[pl.ds(0, stage_ref.shape[0])], sem).wait()


def mm3(a, b):
    (ah, al), (bh, bl) = a, b
    return mm(ah, bh) + (mm(ah, bl) + mm(al, bh))


def mm3_nt(a, b):
    (ah, al), (bh, bl) = a, b
    return mm_nt(ah, bh) + (mm_nt(ah, bl) + mm_nt(al, bh))


def layer_kernel(tiles, sizes, *refs):
    (src, dst, scal, thr, tok, gains, dy, segc, segr), refs = refs[:9], refs[9:]
    w_parts, refs = refs[: len(sizes)], refs[len(sizes) :]
    (out_h, ghid_h, gq_h, gk_h, gv_h, nrm_t_h, wqkv_h, q0_h, k0t_h, part0_h, mask0_h, colsum, small, *sums), refs = (
        refs[:15],
        refs[15:],
    )
    (out, ghid, gq, gk, gv, nrm_t, wqkv, part0, mask0), refs = refs[:9], refs[9:]
    (wall, nrm, q_s, q_e, k_s, v_s, kt_s, vt_s, bias, gsh, probs, mixt, mixb, mixbt, wout, hid, xhat), refs = (
        refs[:17],
        refs[17:],
    )
    nm, nmt, acc, gmid, g_s, gt_s, wu, wd, stage, zero, wsem, gsem, zsem, osem = refs

    writes = []

    def write(ref, target):
        copy = pltpu.make_async_copy(ref, target, osem.at[len(writes)])
        copy.start()
        writes.append(copy)

    n_qkv, n_out, n_up, n_down = tiles
    width = tok.shape[1]
    own = dy.shape[0]
    window = tok.shape[0]
    back = window - own
    side = wall.shape[-1]
    dt = width // side
    pairs = width // side
    total_slots = 2 * sums[0].shape[0]
    loads = []
    at = 0
    for index, (part, size) in enumerate(zip(w_parts, sizes)):
        loads.append(pltpu.make_async_copy(part, wall.at[pl.ds(at, size)], wsem.at[index]))
        loads[-1].start()
        at += size
    zero[...] = jnp.zeros_like(zero)
    tile_count = n_qkv + n_out + n_up + n_down
    empty = total_slots - tile_count

    @pl.loop(0, empty)
    def _(e):
        send_tile(zero, dst[tile_count + e], sums, zsem)

    gain_pre = gains[0:1, :]
    gain_mid = gains[1:2, :]

    @pl.loop(0, window // own)
    def _(b):
        rows = pl.ds(pl.multiple_of(b * own, own), own)
        hat, _ = norm_parts(tok[rows, :].astype(F32))
        value = (hat * gain_pre).astype(BF)
        nrm[rows, :] = value
        nrm_t[:, rows] = value.T

    write(nrm_t, nrm_t_h)
    for load in loads:
        load.wait()
    per_row = 3 * dt

    @pl.loop(0, 3 * dt // 2)
    def _(j):
        for i in range(dt):
            for jj in range(2):
                wqkv[i * side : (i + 1) * side, pl.ds(pl.multiple_of((2 * j + jj) * side, side), side)] = wall[
                    src[i * per_row + 2 * j + jj]
                ]

    write(wqkv, wqkv_h)
    for i in range(dt):
        for j in range(dt):
            wout[i * side : (i + 1) * side, j * side : (j + 1) * side] = wall[src[n_qkv + i * dt + j]]

    @pl.loop(0, dt // 2)
    def _(j):
        cols = pl.ds(pl.multiple_of(2 * j * side, 2 * side), 2 * side)
        got = (mm(nrm[back:, :], wqkv[:, cols]) * 0.125).astype(BF)
        q_s[2 * j] = got[:, :side]
        q_s[2 * j + 1] = got[:, side:]

    q_e[...] = (mm(nrm[:back, :], wqkv[:, 0:side]) * 0.125).astype(BF)

    @pl.loop(0, dt // 2)
    def _(j):
        cols = pl.ds(pl.multiple_of(width + 2 * j * side, 2 * side), 2 * side)
        got = mm(nrm[...], wqkv[:, cols]).astype(BF)
        got_t = got.T
        k_s[2 * j] = got[:, :side]
        k_s[2 * j + 1] = got[:, side:]
        kt_s[2 * j] = got_t[:side, :]
        kt_s[2 * j + 1] = got_t[side:, :]

    @pl.loop(0, dt // 2)
    def _(j):
        cols = pl.ds(pl.multiple_of(2 * width + 2 * j * side, 2 * side), 2 * side)
        got = mm(nrm[...], wqkv[:, cols]).astype(BF)
        got_t = got.T
        v_s[2 * j] = got[:, :side]
        v_s[2 * j + 1] = got[:, side:]
        vt_s[2 * j] = got_t[:side, :]
        vt_s[2 * j + 1] = got_t[side:, :]

    write(q_s.at[0], q0_h)
    write(kt_s.at[0], k0t_h)

    valid_len = scal[0]
    start = scal[1]
    is_last = scal[2]
    key_at = lax.broadcasted_iota(jnp.int32, (window, own), 0)
    query_at = lax.broadcasted_iota(jnp.int32, (window, own), 1)
    key_valid = (key_at + (start - back)) < valid_len
    key_seg = segc[...]
    k_first = k_s[0]

    def selected(q_rows, first):
        s = mm_nt(k_first, keep_half(q_rows, False))
        same = key_seg == segr[:, first : first + own]
        strict = same & key_valid & (key_at < query_at + first)
        return s, same, jnp.where(strict, select_scale * jnp.maximum(s, 0.0), 0.0), strict

    prefix = jnp.zeros((window, 1), F32)
    for b in range(back // own):
        _, _, chosen, _ = selected(q_e[b * own : (b + 1) * own, :], b * own)
        prefix = prefix + jnp.sum(chosen, axis=1, keepdims=True)
    s_own, same, chosen, strict = selected(q_s[0], back)
    tri_row = lax.broadcasted_iota(jnp.int32, (own, own), 0)
    tri_col = lax.broadcasted_iota(jnp.int32, (own, own), 1)
    earlier = jnp.where(tri_row < tri_col, 1.0, 0.0).astype(BF)
    shadow = prefix + mm_split(chosen, earlier)
    allowed = strict | (same & (key_at == query_at + back))
    bias[...] = jnp.where(allowed, -shadow, -1e30)
    mask0[...] = jnp.where(strict & (s_own > 0.0), 1.0, 0.0).astype(BF)
    write(mask0, mask0_h)
    column_total = prefix + jnp.sum(chosen, axis=1, keepdims=True)
    key_col = lax.broadcasted_iota(jnp.int32, (window, 1), 0)
    key_pos = key_col + (start - back)
    counts = (key_pos >= 0) & (key_pos < valid_len) & ((key_col < own) | (is_last > 0))
    soft = 1.0 / (1.0 + jnp.exp(-fraction_slope * (column_total - thr[0])))
    counted = jnp.sum(jnp.where(counts, soft, 0.0), axis=0, keepdims=True)
    small[...] = jnp.zeros_like(small)
    small[1:2, :] = jnp.broadcast_to(counted / valid_len.astype(F32), (1, width))

    @pl.loop(0, pairs)
    def _(p):
        q2 = q_s[p]
        k2 = k_s[p]
        both = [mm_nt(k2, keep_half(q2, hh == 1)) for hh in range(2)]
        prs = []
        for hh in range(2):
            s = both[hh] + bias[...]
            e = jnp.exp(s - jnp.max(s, axis=0, keepdims=True))
            prs.append((e * (1.0 / jnp.sum(e, axis=0, keepdims=True))).astype(BF))
        for hh in range(2):
            probs[2 * p + hh] = prs[hh]
        mixed = [mm(vt_s[p, hh * HD : (hh + 1) * HD, :], prs[hh]) for hh in range(2)]
        mixt[pl.ds(pl.multiple_of(p * side, side), side), :] = jnp.concatenate(mixed, axis=0)

    mixbt[...] = mixt[...].astype(BF)
    mixb[...] = mixbt[...].T
    hid[...] = tok[back:, :].astype(F32) + mm(mixb[...], wout[...])
    hat, rate = norm_parts(hid[...])
    xhat[...] = hat
    nm[...] = (hat * gain_mid).astype(BF)
    nmt[...] = nm[...].T

    acc[...] = jnp.zeros_like(acc)
    gmid[...] = jnp.zeros_like(gmid)
    cw = CHUNK // side
    f_tiles = FF // side
    per_chunk = 2 * cw * dt
    chunks = FF // CHUNK

    @pl.loop(0, chunks)
    def _(c):
        slot = lax.rem(c, 2)
        for i in range(dt):
            for jj in range(cw):
                wu[i * side : (i + 1) * side, jj * side : (jj + 1) * side] = wall[
                    src[n_qkv + n_out + i * f_tiles + cw * c + jj]
                ]
        for ii in range(cw):
            for j in range(dt):
                wd[ii * side : (ii + 1) * side, j * side : (j + 1) * side] = wall[
                    src[n_qkv + n_out + n_up + (cw * c + ii) * dt + j]
                ]
        up = mm(nm[...], wu[...])
        cube = 0.7978845608028654 * (up + 0.044715 * up * up * up)
        th = jnp.tanh(cube)
        active = (0.5 * up * (1.0 + th)).astype(BF)
        slope = 0.5 * (1.0 + th) + 0.5 * up * (1.0 - th * th) * (
            0.7978845608028654 * (1.0 + 3.0 * 0.044715 * up * up)
        )
        acc[...] += mm(active, wd[...])
        gu = (mm_nt(dy[...], wd[...]) * slope).astype(BF)
        gmid[...] += mm_nt(gu, wu[...])

        @pl.when(c >= 2)
        def _():
            wait_tiles(stage.at[slot], sums, gsem.at[slot])

        g_down = mm(active.T, dy[...]).astype(BF)
        for ii in range(cw):
            for j in range(dt):
                at = ii * dt + j
                stage[slot, at] = g_down[ii * side : (ii + 1) * side, j * side : (j + 1) * side]
        g_up = mm(nmt[...], gu).astype(BF)
        for i in range(dt):
            for jj in range(cw):
                at = cw * dt + i * cw + jj
                stage[slot, at] = g_up[i * side : (i + 1) * side, jj * side : (jj + 1) * side]
        for ii in range(cw):
            for j in range(dt):
                at = ii * dt + j
                t = n_qkv + n_out + n_up + (cw * c + ii) * dt + j
                send_tile(stage.at[slot, at], dst[t], sums, gsem.at[slot])
        for i in range(dt):
            for jj in range(cw):
                at = cw * dt + i * cw + jj
                t = n_qkv + n_out + i * f_tiles + cw * c + jj
                send_tile(stage.at[slot, at], dst[t], sums, gsem.at[slot])

    out[...] = (hid[...] + acc[...]).astype(BF)
    write(out, out_h)
    hat = xhat[...]
    gm = gmid[...]
    small[0:1, :] = jnp.sum(gm * hat, axis=0, keepdims=True)
    scaled = gm * gain_mid
    gh = dy[...].astype(F32) + rate * (
        scaled
        - jnp.mean(scaled, axis=-1, keepdims=True)
        - hat * jnp.mean(scaled * hat, axis=-1, keepdims=True)
    )
    ghid[...] = gh
    write(ghid, ghid_h)
    gb = gh.astype(BF)
    gmix = mm_nt(gb, wout[...]).astype(BF)
    for p in range(pairs):
        g_s[p] = gmix[:, p * side : (p + 1) * side]
    gt_s[...] = gmix.T

    for slot in range(2):
        wait_tiles(stage.at[slot], sums, gsem.at[slot])
    half_out = dt // 2
    for part in range(2):
        g_out = mm(mixbt[part * half_out * side : (part + 1) * half_out * side, :], gb).astype(BF)
        for i in range(half_out):
            for j in range(dt):
                stage[part, i * dt + j] = g_out[i * side : (i + 1) * side, j * side : (j + 1) * side]
        for i in range(half_out):
            for j in range(dt):
                t = n_qkv + (part * half_out + i) * dt + j
                send_tile(stage.at[part, i * dt + j], dst[t], sums, gsem.at[part])

    gsh[...] = jnp.zeros_like(gsh)

    @pl.loop(0, pairs)
    def _(p):
        g2 = g_s[p]
        q2 = q_s[p]
        v2 = v_s[p]
        later = jnp.where(p > 0, 1.0, 0.0)
        halves = [keep_half(g2, hh == 1) for hh in range(2)]
        dps = [mm_nt(v2, halves[hh]) for hh in range(2)]
        prs = [probs[2 * p + hh] for hh in range(2)]
        rows = pl.ds(pl.multiple_of(p * side, side), side)
        product = gt_s[rows, :].astype(F32) * mixt[rows, :]
        dls = []
        for hh in range(2):
            delta = jnp.sum(product[hh * HD : (hh + 1) * HD, :], axis=0, keepdims=True)
            dls.append(prs[hh].astype(F32) * (dps[hh] - delta))
        gsh[...] += dls[0] + dls[1]

        @pl.when(p == 0)
        def _():
            part0[...] = dls[0]

        gs = [(dls[0] * later).astype(BF), dls[1].astype(BF)]
        dv = mm(prs[0], halves[0]) + mm(prs[1], halves[1])
        dk = mm(gs[0], keep_half(q2, False)) + mm(gs[1], keep_half(q2, True))
        dqs = [mm(kt_s[p, hh * HD : (hh + 1) * HD, :], gs[hh]) for hh in range(2)]
        cols = pl.ds(pl.multiple_of(p * side, side), side)
        gq[:, cols] = (jnp.concatenate(dqs, axis=0) * 0.125).T.astype(BF)
        gk[:, cols] = dk.astype(BF)
        gv[:, cols] = dv.astype(BF)

    write(gq, gq_h)
    write(gk, gk_h)
    write(gv, gv_h)
    ones = jnp.ones((8, own), BF)
    high, rest = split(-gsh[...])
    colsum[...] = mm_nt(ones, high) + mm_nt(ones, rest)
    after = jnp.where(tri_row > tri_col, 1.0, 0.0).astype(BF)
    part0[...] += select_scale * mask0[...].astype(F32) * (mm(high, after) + mm(rest, after))
    write(part0, part0_h)

    for part in range(2):
        wait_tiles(stage.at[part, pl.ds(0, half_out * dt)], sums, gsem.at[part])
    pltpu.make_async_copy(sums[0].at[pl.ds(0, empty)], sums[0].at[pl.ds(0, empty)], zsem).wait()
    for copy in writes:
        copy.wait()


def load_all(pairs, sem):
    copies = [pltpu.make_async_copy(a, b, sem.at[i]) for i, (a, b) in enumerate(pairs)]
    for copy in copies:
        copy.start()
    return copies


def qkv_kernel(dst, gq_h, gk_h, gv_h, nrm_h, stay_in, away_in, stay, away, gq, gk, gv, nrm_t, stage, lsem, gsem):
    own, width = gq.shape
    side = stage.shape[-1]
    dt = width // side
    back = gk.shape[0] - own
    sums = (stay, away)
    copies = load_all([(nrm_h, nrm_t), (gv_h, gv), (gk_h, gk), (gq_h, gq)], lsem)
    copies[0].wait()
    count = 0
    for which, copy in ((2, copies[1]), (1, copies[2]), (0, copies[3])):
        copy.wait()
        bounds = [(c, c + 2) for c in range(0, dt, 2)] if which == 2 else [(1, 2)] + [(c, c + 2) for c in range(2, dt, 2)]
        for lo, hi in bounds:
            cols = slice(lo * side, hi * side)
            if which == 0:
                g = mm(nrm_t[:, back:], gq[:, cols])
            else:
                g = mm(nrm_t[...], (gk if which == 1 else gv)[:, cols])
            g = g.astype(BF)
            for i in range(dt):
                for j in range(lo, hi):
                    stage[count] = g[i * side : (i + 1) * side, (j - lo) * side : (j - lo + 1) * side]
                    send_tile(stage.at[count], dst[i * 3 * dt + which * dt + j], sums, gsem)
                    count += 1
    wait_tiles(stage, sums, gsem)


def head_kernel(
    dst, suffix, part0_h, mask0_h, q0_h, k0t_h, gq_h, gk_h, nrm_h, stay_in, away_in, gq_out, gk_out, stay, away,
    part0, mask0, q0, k0t, gq, gk, nrm_t, stage, lsem, gsem,
):
    own, side = gq.shape
    window = gk.shape[0]
    back = window - own
    dt = nrm_t.shape[0] // side
    sums = (stay, away)
    head = pl.ds(0, side)
    copies = load_all(
        [
            (part0_h, part0),
            (mask0_h, mask0),
            (k0t_h, k0t),
            (q0_h, q0),
            (gq_h.at[:, head], gq),
            (gk_h.at[:, head], gk),
            (nrm_h, nrm_t),
        ],
        lsem,
    )
    column = jnp.broadcast_to(suffix[0:1, :], (side, window)).T
    column = jnp.concatenate([column] * (own // side), axis=1)
    for copy in copies[:-1]:
        copy.wait()
    gs = (part0[...] + select_scale * mask0[...].astype(F32) * column).astype(BF)
    dq = (mm(k0t[0:HD, :], gs) * 0.125).T
    dk = mm(gs, keep_half(q0[...], False)).astype(BF)
    gq_new = gq[...] + jnp.concatenate([dq, jnp.zeros_like(dq)], axis=1).astype(BF)
    gk_new = gk[...] + dk
    gq_out[...] = gq_new
    gk_out[...] = gk_new
    copies[-1].wait()
    g_q = mm(nrm_t[:, back:], gq_new).astype(BF)
    g_k = mm(nrm_t[...], gk_new).astype(BF)
    for which, g in ((0, g_q), (1, g_k)):
        for i in range(dt):
            stage[which * dt + i] = g[i * side : (i + 1) * side, :]
            send_tile(stage.at[which * dt + i], dst[i * 3 * dt + which * dt], sums, gsem)
    wait_tiles(stage, sums, gsem)


def pre_kernel(tok, gq_head, gk_head, gq_h, gk_h, gv_h, wqkv_h, far, near, mine, small, gq, gk, gv, wqkv, lsem):
    own, width = gq.shape
    window = gk.shape[0]
    side = gq_head.shape[1]
    rest = pl.ds(side, width - side)
    copies = load_all(
        [(wqkv_h, wqkv), (gk_h.at[:, rest], gk.at[:, rest]), (gv_h, gv), (gq_h.at[:, rest], gq.at[:, rest])], lsem
    )
    gq[:, 0:side] = gq_head[...]
    gk[:, 0:side] = gk_head[...]
    for copy in copies:
        copy.wait()
    total = jnp.zeros((1, width), F32)
    for b in range(window // own):
        rows = slice(b * own, (b + 1) * own)
        g = mm_nt(gk[rows, :], wqkv[:, width : 2 * width]) + mm_nt(gv[rows, :], wqkv[:, 2 * width :])
        if b == window // own - 1:
            g = g + mm_nt(gq[...], wqkv[:, :width])
            mine[...] = g
        elif b == 0:
            far[...] = g.astype(far.dtype)
        else:
            near[...] = g.astype(near.dtype)
        hat, _ = norm_parts(tok[rows, :].astype(F32))
        total = total + jnp.sum(g * hat, axis=0, keepdims=True)
    small[...] = jnp.broadcast_to(total, small.shape)


def input_kernel(tok, gains, ghid, mine, near, far, out):
    hat, rate = norm_parts(tok[...].astype(F32))
    g = mine[...] + near[...].astype(F32) + far[...].astype(F32)
    scaled = g * gains[0:1, :]
    out[...] = ghid[...] + rate * (
        scaled
        - jnp.mean(scaled, axis=-1, keepdims=True)
        - hat * jnp.mean(scaled * hat, axis=-1, keepdims=True)
    )


def adam_kernel(correction, parts, *refs):
    grads, refs = refs[: 2 * len(parts)], refs[2 * len(parts) :]
    holds, first, second, left, right, weight, first_out, second_out, weight_out = refs
    slots = []
    for index, (at, size, _) in enumerate(parts):
        slots += [(at + k, grads[2 * index], grads[2 * index + 1], k) for k in range(size)]
    for low in range(0, len(slots), ADAM_GROUP):
        group = slots[low : low + ADAM_GROUP]
        rights, turned, steps, undone = {}, {}, {}, {}
        for slot, mine, other, k in group:
            grad = mine[k].astype(F32) + other[k].astype(F32)
            grad = jnp.where(holds[slot] > 0, grad, 0.0)
            rights[slot] = split(right[slot])
            turned[slot] = mm3(split(grad), rights[slot])
        for slot, *_ in group:
            turned[slot] = mm3(split(left[slot].T), split(turned[slot]))
        for slot, *_ in group:
            t = turned[slot]
            first_new = first_decay * first[slot] + (1.0 - first_decay) * t
            second_new = second_decay * second[slot] + (1.0 - second_decay) * t * t
            first_out[slot] = first_new
            second_out[slot] = second_new
            steps[slot] = first_new / correction / (jnp.sqrt(second_new / correction) + adam_epsilon)
        for slot, *_ in group:
            undone[slot] = mm3_nt(split(steps[slot]), rights[slot])
        for slot, *_ in group:
            back = mm3(split(left[slot]), split(undone[slot]))
            w = weight[slot]
            weight_out[slot] = w - weight_rate * back - weight_rate * decay_rate * w


def bit_plan(devices, per_device):
    bits = [1 << b for b in range(devices.bit_length() - 1)]
    first, rest = bits[0], bits[1:]
    if devices == 32:
        orders = [(2, 4, 8, 16), (4, 8, 2, 16), (8, 16, 2, 4)]
    else:
        orders = [tuple(rest[i:] + rest[:i]) for i in range(3)]
    third = per_device * 3 // 7
    sizes = [third, per_device - third] if per_device < 4 else [third, per_device * 5 // 14, 0]
    if len(sizes) == 3:
        sizes[2] = per_device - sizes[0] - sizes[1]
    plan = []
    at = 0
    for size, order in zip(sizes, orders):
        if size:
            plan.append((at, size, order))
            at += size
    return first, plan


def gather_parts(devices, per_device):
    if devices != 32 or per_device < 8:
        return per_device, []
    size = per_device * 2 // 7
    first = per_device - 2 * size
    return first, [(first, size, (16, 8, 4, 2, 1)), (first + size, size, (16, 8, 2, 4, 1))]


def local(
    tokens,
    segment_ids,
    pad_lengths,
    threshold,
    gains,
    gain_first,
    gain_second,
    slot_tiles,
    weight_slots,
    first_moment,
    second_moment,
    basis_left,
    basis_right,
    out_grad,
):
    axes = ("dp", "seq")
    n_dp, n_seq = lax.axis_size("dp"), lax.axis_size("seq")
    devices = n_dp * n_seq
    me = lax.axis_index(axes)
    seq_at = lax.axis_index("seq")
    _, own, width = tokens.shape
    length = segment_ids.shape[1]
    side = weight_slots.shape[-1]
    per_device = weight_slots.shape[0]
    slot_total = slot_tiles.shape[0]
    dt = width // side
    tiles = (3 * dt * dt, dt * dt, dt * (FF // side), dt * (FF // side))
    tile_count = sum(tiles)
    back = SPAN
    window = back + own

    def swap(x, bit):
        return lax.ppermute(x, axes, [(i, i ^ bit) for i in range(devices)])

    slot_ids = jnp.arange(slot_total, dtype=jnp.int32)
    position = jnp.sum(
        jnp.where(slot_tiles[None, :] == slot_ids[:, None], slot_ids[None, :], 0), axis=1
    )
    owner = position // per_device
    inner = position % per_device
    apart = owner ^ me
    first_bit, plan = bit_plan(devices, per_device)
    half = slot_total // 2
    spread = devices // 2
    place = jnp.zeros_like(position)
    for at, size, order in plan:
        index = jnp.zeros_like(position)
        for bit in order:
            index = index * 2 + ((apart & bit) != 0).astype(jnp.int32)
        here = at * spread + index * size + (inner - at)
        place = jnp.where((inner >= at) & (inner < at + size), here, place)
    dst = place + jnp.where((apart & first_bit) != 0, half, 0)
    by_gather, gather_plan = gather_parts(devices, per_device)
    src = owner * by_gather + inner
    base = devices * by_gather
    for at, size, order in gather_plan:
        index = jnp.zeros_like(position)
        for bit in reversed(order):
            index = index * 2 + ((apart & bit) != 0).astype(jnp.int32)
        here = base + index * size + (inner - at)
        src = jnp.where((inner >= at) & (inner < at + size), here, src)
        base += devices * size

    mine_tok = tokens[0]
    seen = []
    for step in range(back // own, 0, -1):
        seen.append(lax.ppermute(mine_tok, "seq", [(i, i + step) for i in range(n_seq - step)]))
    tok = jnp.concatenate(seen + [mine_tok], axis=0)
    start = seq_at * own
    seg_window = lax.dynamic_slice_in_dim(
        jnp.concatenate([jnp.full((back,), -1, jnp.int32), segment_ids[0]]), start, window
    )
    valid_len = length - pad_lengths[0]
    scal = jnp.stack([valid_len, start, (seq_at == n_seq - 1).astype(jnp.int32)])

    segc, segr = seg_window[:, None], seg_window[None, :]

    rounded = weight_slots.astype(BF)
    pieces = [lax.all_gather(rounded[:by_gather], axes, axis=0, tiled=True)]
    held = [rounded[at : at + size] for at, size, _ in gather_plan]
    for step in range(len(gather_plan[0][2]) - 2 if gather_plan else 0):
        held = [jnp.concatenate([h, swap(h, o[2][step])], axis=0) for h, o in zip(held, gather_plan)]
        if step == 1:
            held, tok, src, dst, scal, segc, segr = lax.optimization_barrier((held, tok, src, dst, scal, segc, segr))
    for h, (_, _, order) in zip(held, gather_plan):
        two = [h, swap(h, order[-2])]
        pieces += two + [swap(x, order[-1]) for x in two]
    sizes = [p.shape[0] for p in pieces]

    hbm = pl.BlockSpec(memory_space=pltpu.HBM)
    vm = pl.BlockSpec(memory_space=VMEM)
    sm = pl.BlockSpec(memory_space=SMEM)
    shp = jax.ShapeDtypeStruct
    sums_shape = shp((half, side, side), BF)
    per_chunk = 2 * (CHUNK // side) * dt
    outs = pl.pallas_call(
        functools.partial(layer_kernel, tiles, sizes),
        out_shape=(
            shp((own, width), BF),
            shp((own, width), F32),
            shp((own, width), BF),
            shp((window, width), BF),
            shp((window, width), BF),
            shp((width, window), BF),
            shp((width, 3 * width), BF),
            shp((own, side), BF),
            shp((side, window), BF),
            shp((window, own), F32),
            shp((window, own), BF),
            shp((8, window), F32),
            shp((8, width), F32),
            sums_shape,
            sums_shape,
        ),
        in_specs=[sm] * 4 + [vm] * 5 + [hbm] * len(sizes),
        out_specs=tuple([hbm] * 11 + [vm] * 2 + [hbm] * 2),
        scratch_shapes=[
            VMEM((own, width), BF),
            VMEM((own, width), F32),
            VMEM((own, width), BF),
            VMEM((window, width), BF),
            VMEM((window, width), BF),
            VMEM((width, window), BF),
            VMEM((width, 3 * width), BF),
            VMEM((window, own), F32),
            VMEM((window, own), BF),
            VMEM((slot_total, side, side), BF),
            VMEM((window, width), BF),
            VMEM((dt, own, side), BF),
            VMEM((back, side), BF),
            VMEM((dt, window, side), BF),
            VMEM((dt, window, side), BF),
            VMEM((dt, side, window), BF),
            VMEM((dt, side, window), BF),
            VMEM((window, own), F32),
            VMEM((window, own), F32),
            VMEM((H, window, own), BF),
            VMEM((width, own), F32),
            VMEM((own, width), BF),
            VMEM((width, own), BF),
            VMEM((width, width), BF),
            VMEM((own, width), F32),
            VMEM((own, width), F32),
            VMEM((own, width), BF),
            VMEM((width, own), BF),
            VMEM((own, width), F32),
            VMEM((own, width), F32),
            VMEM((dt, own, side), BF),
            VMEM((width, own), BF),
            VMEM((width, CHUNK), BF),
            VMEM((CHUNK, width), BF),
            VMEM((2, per_chunk, side, side), BF),
            VMEM((side, side), BF),
            pltpu.SemaphoreType.DMA((len(sizes),)),
            pltpu.SemaphoreType.DMA((2,)),
            pltpu.SemaphoreType.DMA,
            pltpu.SemaphoreType.DMA((11,)),
        ],
        compiler_params=pltpu.CompilerParams(vmem_limit_bytes=60 << 20),
        name="layer",
    )(
        src,
        dst,
        scal,
        threshold,
        tok,
        gains,
        out_grad[0],
        segc,
        segr,
        *pieces,
    )
    (output, ghid, gq, gk, gv, nrm_t, wqkv, q0, k0t, part0, mask0, colsum, small, stay, away) = outs

    columns = colsum[0]
    suffix = jnp.zeros((window,), F32)
    for step in range(1, back // own + 1):
        reach = window - step * own
        got = lax.ppermute(columns[:reach], "seq", [(i, i - step) for i in range(step, n_seq)])
        suffix = suffix + jnp.concatenate([jnp.zeros((step * own,), F32), got])
    suffix = jnp.broadcast_to(suffix[None, :], (8, window))

    main_tiles = tiles[0] - 2 * dt
    stay, away = pl.pallas_call(
        qkv_kernel,
        out_shape=(sums_shape, sums_shape),
        in_specs=[sm] + [hbm] * 6,
        out_specs=(hbm, hbm),
        scratch_shapes=[
            VMEM((own, width), BF),
            VMEM((window, width), BF),
            VMEM((window, width), BF),
            VMEM((width, window), BF),
            VMEM((main_tiles, side, side), BF),
            pltpu.SemaphoreType.DMA((4,)),
            pltpu.SemaphoreType.DMA,
        ],
        input_output_aliases={5: 0, 6: 1},
        compiler_params=pltpu.CompilerParams(vmem_limit_bytes=60 << 20),
        cost_estimate=pl.CostEstimate(
            flops=2 * (2 * window + own) * width * width, bytes_accessed=8 << 20, transcendentals=0
        ),
        name="qkv_grad",
    )(dst, gq, gk, gv, nrm_t, stay, away)
    gq_head, gk_head, stay, away = pl.pallas_call(
        head_kernel,
        out_shape=(shp((own, side), BF), shp((window, side), BF), sums_shape, sums_shape),
        in_specs=[sm, vm] + [hbm] * 9,
        out_specs=(vm, vm, hbm, hbm),
        scratch_shapes=[
            VMEM((window, own), F32),
            VMEM((window, own), BF),
            VMEM((own, side), BF),
            VMEM((side, window), BF),
            VMEM((own, side), BF),
            VMEM((window, side), BF),
            VMEM((width, window), BF),
            VMEM((2 * dt, side, side), BF),
            pltpu.SemaphoreType.DMA((7,)),
            pltpu.SemaphoreType.DMA,
        ],
        input_output_aliases={9: 2, 10: 3},
        compiler_params=pltpu.CompilerParams(vmem_limit_bytes=60 << 20),
        cost_estimate=pl.CostEstimate(flops=1 << 30, bytes_accessed=4 << 20, transcendentals=0),
        name="head_grad",
    )(dst, suffix, part0, mask0, q0, k0t, gq, gk, nrm_t, stay, away)

    def plus(a, b):
        return (a.astype(F32) + b.astype(F32)).astype(BF)

    got = swap(away, first_bit)

    far, near, mine, small_pre = pl.pallas_call(
        pre_kernel,
        out_shape=(
            shp((own, width), BF),
            shp((own, width), BF),
            shp((own, width), F32),
            shp((8, width), F32),
        ),
        in_specs=[vm] * 3 + [hbm] * 4,
        out_specs=tuple([vm] * 4),
        scratch_shapes=[
            VMEM((own, width), BF),
            VMEM((window, width), BF),
            VMEM((window, width), BF),
            VMEM((width, 3 * width), BF),
            pltpu.SemaphoreType.DMA((4,)),
        ],
        compiler_params=pltpu.CompilerParams(vmem_limit_bytes=30 << 20),
        cost_estimate=pl.CostEstimate(
            flops=2 * (2 * window + own) * width * width, bytes_accessed=10 << 20, transcendentals=0
        ),
        name="pre_grad",
    )(tok, gq_head, gk_head, gq, gk, gv, wqkv)
    row_at = lax.axis_index("dp")
    spots = jnp.arange(width, dtype=jnp.int32)
    totals = jnp.stack([small_pre[0], small[0], jnp.where(spots == row_at, small[1], 0.0)])
    totals = jnp.pad(totals.reshape(3 * dt, side), ((0, side // 2 - 3 * dt), (0, 0)))
    got, totals = lax.optimization_barrier((got, totals))
    gathered = lax.all_gather(totals, axes)
    steps = len(plan[0][2])
    sent = []
    for at, size, _ in plan:
        rows = slice(at * spread + size * spread // 2, (at + size) * spread)
        got, piece = lax.optimization_barrier((got, plus(stay[rows], got[rows])))
        sent.append(piece)
    came = [swap(piece, order[0]) for piece, (_, _, order) in zip(sent, plan)]
    left = []
    for at, size, _ in plan:
        rows = slice(at * spread, at * spread + size * spread // 2)
        left.append(plus(stay[rows], got[rows]))
    for step in range(1, steps):
        for which, (_, _, order) in enumerate(plan):
            middle = left[which].shape[0] // 2
            piece = plus(left[which][middle:], came[which][middle:])
            if which == 0 and step == 1:
                piece, far, near = lax.optimization_barrier((piece, far, near))
                far = lax.ppermute(far, "seq", [(i, i - 2) for i in range(2, n_seq)])
                near = lax.ppermute(near, "seq", [(i, i - 1) for i in range(1, n_seq)])
                first_piece = piece
            if which == 2 and step == 2:
                piece, first_piece = lax.optimization_barrier((piece, first_piece))
            if which == 0 and step == steps - 1:
                piece, far, near, mine, gathered = lax.optimization_barrier((piece, far, near, mine, gathered))
            rest = plus(left[which][:middle], came[which][:middle])
            came[which] = swap(piece, order[step])
            left[which] = rest
    pairs = list(zip(left, came))
    totals = jnp.sum(gathered[:, : 3 * dt], axis=0).reshape(3, width)
    correction = 1.0 - first_decay**STEP
    holds = lax.dynamic_slice_in_dim((slot_tiles < tile_count).astype(jnp.int32), me * per_device, per_device)
    moment_first, moment_second, new_weights = pl.pallas_call(
        functools.partial(adam_kernel, correction, plan),
        out_shape=tuple([shp(weight_slots.shape, F32)] * 3),
        in_specs=[vm] * (2 * len(plan)) + [sm] + [vm] * 5,
        out_specs=tuple([vm] * 3),
        compiler_params=pltpu.CompilerParams(vmem_limit_bytes=30 << 20),
        name="adam",
    )(*[x for pair in pairs for x in pair], holds, first_moment, second_moment, basis_left, basis_right, weight_slots)
    input_grad = pl.pallas_call(
        input_kernel,
        out_shape=shp((own, width), F32),
        in_specs=[vm] * 6,
        out_specs=vm,
        compiler_params=pltpu.CompilerParams(vmem_limit_bytes=20 << 20),
        name="input_grad",
    )(mine_tok, gains, ghid, mine, near, far)

    gain_total = totals[:2]
    fraction = lax.dynamic_slice_in_dim(totals[2], row_at, 1)

    gain_moment = first_decay * gain_first + (1.0 - first_decay) * gain_total
    gain_square = second_decay * gain_second + (1.0 - second_decay) * gain_total * gain_total
    gain_update = gains - gain_rate * (gain_moment / correction) / (
        jnp.sqrt(gain_square / correction) + adam_epsilon
    )
    return (
        output[None],
        input_grad[None],
        fraction,
        moment_first,
        moment_second,
        new_weights,
        gain_update,
        gain_moment,
        gain_square,
    )


def solution(mesh):
    in_specs = (
        P("dp", "seq", None),
        P("dp", None),
        P("dp"),
        P(),
        P(),
        P(),
        P(),
        P(),
        P(("dp", "seq"), None, None),
        P(("dp", "seq"), None, None),
        P(("dp", "seq"), None, None),
        P(("dp", "seq"), None, None),
        P(("dp", "seq"), None, None),
        P("dp", "seq", None),
    )
    out_specs = (
        P("dp", "seq", None),
        P("dp", "seq", None),
        P("dp"),
        P(("dp", "seq"), None, None),
        P(("dp", "seq"), None, None),
        P(("dp", "seq"), None, None),
        P(),
        P(),
        P(),
    )
    return jax.shard_map(local, mesh=mesh, in_specs=in_specs, out_specs=out_specs, check_vma=False)
```

```python
import functools

import jax
import jax.numpy as jnp
from jax import lax
from jax.experimental import pallas as pl
from jax.experimental.pallas import tpu as pltpu
from jax.sharding import PartitionSpec as P

H = 12
HD = 64
FF = 3072
STEP = 3
SPAN = 512
CHUNK = 768
ADAM_GROUP = 7

select_scale = 0.2
fraction_slope = 2.0
first_decay = 0.5
second_decay = 0.5
adam_epsilon = 1e-08
weight_rate = 0.05
gain_rate = 0.2
decay_rate = 0.1
norm_epsilon = 1e-05

BF = jnp.bfloat16
F32 = jnp.float32
VMEM = pltpu.VMEM
SMEM = pltpu.SMEM


def mm(a, b):
    return lax.dot_general(a, b, (((1,), (0,)), ((), ())), preferred_element_type=F32)


def mm_nt(a, b):
    return lax.dot_general(a, b, (((1,), (1,)), ((), ())), preferred_element_type=F32)


def split(x):
    high = x.astype(BF)
    return high, (x - high.astype(F32)).astype(BF)


def mm_split(x, exact):
    high, rest = split(x)
    return mm(high, exact) + mm(rest, exact)


def lane_half(shape, second):
    lane = lax.broadcasted_iota(jnp.int32, shape, 1)
    return (lane >= HD) if second else (lane < HD)


def keep_half(x, second):
    return jnp.where(lane_half(x.shape, second), x, jnp.zeros_like(x))


def norm_parts(x):
    centred = x - jnp.mean(x, axis=-1, keepdims=True)
    rate = lax.rsqrt(jnp.mean(centred * centred, axis=-1, keepdims=True) + norm_epsilon)
    return centred * rate, rate


def send_tile(tile_ref, dst, sums, sem):
    low = 0
    for buffer in sums:
        high = low + buffer.shape[0]

        @pl.when((dst >= low) & (dst < high))
        def _(buffer=buffer, low=low):
            pltpu.make_async_copy(tile_ref, buffer.at[dst - low], sem).start()

        low = high


def wait_tiles(stage_ref, sums, sem):
    pltpu.make_async_copy(stage_ref, sums[0].at[pl.ds(0, stage_ref.shape[0])], sem).wait()


def mm3(a, b):
    (ah, al), (bh, bl) = a, b
    return mm(jnp.concatenate([ah, ah, al], axis=1), jnp.concatenate([bh, bl, bh], axis=0))


def mm3_nt(a, b):
    (ah, al), (bh, bl) = a, b
    return mm_nt(jnp.concatenate([ah, ah, al], axis=1), jnp.concatenate([bh, bl, bh], axis=1))


def layer_kernel(tiles, sizes, *refs):
    (src, dst, scal, thr, tok, gains, dy, segc, segr), refs = refs[:9], refs[9:]
    w_parts, refs = refs[: len(sizes)], refs[len(sizes) :]
    (out_h, ghid_h, gq_h, gk_h, gv_h, nrm_t_h, wqkv_h, q0_h, k0t_h, part0_h, mask0_h, colsum, small, *sums), refs = (
        refs[:16],
        refs[16:],
    )
    (out, ghid, gq, gk, gv, nrm_t, wqkv, part0, mask0), refs = refs[:9], refs[9:]
    (wall, nrm, q_s, q_e, k_s, v_s, kt_s, vt_s, bias, gsh, probs, mixt, mixb, mixbt, wout, hid, xhat), refs = (
        refs[:17],
        refs[17:],
    )
    nm, nmt, acc, gmid, g_s, gt_s, wu, wd, stage, zero, wsem, gsem, zsem, osem = refs

    writes = []

    def write(ref, target):
        copy = pltpu.make_async_copy(ref, target, osem.at[len(writes)])
        copy.start()
        writes.append(copy)

    n_qkv, n_out, n_up, n_down = tiles
    width = tok.shape[1]
    own = dy.shape[0]
    window = tok.shape[0]
    back = window - own
    side = wall.shape[-1]
    dt = width // side
    pairs = width // side
    total_slots = 2 * sums[0].shape[0]
    loads = []
    at = 0
    for index, (part, size) in enumerate(zip(w_parts, sizes)):
        loads.append(pltpu.make_async_copy(part, wall.at[pl.ds(at, size)], wsem.at[index]))
        loads[-1].start()
        at += size
    zero[...] = jnp.zeros_like(zero)
    tile_count = n_qkv + n_out + n_up + n_down
    empty = total_slots - tile_count

    @pl.loop(0, empty)
    def _(e):
        send_tile(zero, dst[tile_count + e], sums, zsem)

    gain_pre = gains[0:1, :]
    gain_mid = gains[1:2, :]

    @pl.loop(0, window // own)
    def _(b):
        rows = pl.ds(pl.multiple_of(b * own, own), own)
        hat, _ = norm_parts(tok[rows, :].astype(F32))
        value = (hat * gain_pre).astype(BF)
        nrm[rows, :] = value
        nrm_t[:, rows] = value.T

    write(nrm_t, nrm_t_h)
    for load in loads:
        load.wait()
    per_row = 3 * dt

    @pl.loop(0, 3 * dt // 2)
    def _(j):
        for i in range(dt):
            for jj in range(2):
                wqkv[i * side : (i + 1) * side, pl.ds(pl.multiple_of((2 * j + jj) * side, side), side)] = wall[
                    src[i * per_row + 2 * j + jj]
                ]

    write(wqkv, wqkv_h)
    for i in range(dt):
        for j in range(dt):
            wout[i * side : (i + 1) * side, j * side : (j + 1) * side] = wall[src[n_qkv + i * dt + j]]

    @pl.loop(0, dt // 2, unroll=True)
    def _(j):
        cols = pl.ds(pl.multiple_of(2 * j * side, 2 * side), 2 * side)
        got = (mm(nrm[back:, :], wqkv[:, cols]) * 0.125).astype(BF)
        q_s[2 * j] = got[:, :side]
        q_s[2 * j + 1] = got[:, side:]

    q_e[...] = (mm(nrm[:back, :], wqkv[:, 0:side]) * 0.125).astype(BF)

    @pl.loop(0, dt // 2, unroll=True)
    def _(j):
        cols = pl.ds(pl.multiple_of(width + 2 * j * side, 2 * side), 2 * side)
        got = mm(nrm[...], wqkv[:, cols]).astype(BF)
        got_t = got.T
        k_s[2 * j] = got[:, :side]
        k_s[2 * j + 1] = got[:, side:]
        kt_s[2 * j] = got_t[:side, :]
        kt_s[2 * j + 1] = got_t[side:, :]

    @pl.loop(0, dt // 2, unroll=True)
    def _(j):
        cols = pl.ds(pl.multiple_of(2 * width + 2 * j * side, 2 * side), 2 * side)
        got = mm(nrm[...], wqkv[:, cols]).astype(BF)
        got_t = got.T
        v_s[2 * j] = got[:, :side]
        v_s[2 * j + 1] = got[:, side:]
        vt_s[2 * j] = got_t[:side, :]
        vt_s[2 * j + 1] = got_t[side:, :]

    write(q_s.at[0], q0_h)
    write(kt_s.at[0], k0t_h)

    valid_len = scal[0]
    start = scal[1]
    is_last = scal[2]
    key_at = lax.broadcasted_iota(jnp.int32, (window, own), 0)
    query_at = lax.broadcasted_iota(jnp.int32, (window, own), 1)
    key_valid = (key_at + (start - back)) < valid_len
    key_seg = segc[...]
    k_first = k_s[0]

    def selected(q_rows, first):
        s = mm_nt(k_first, keep_half(q_rows, False))
        same = key_seg == segr[:, first : first + own]
        strict = same & key_valid & (key_at < query_at + first)
        return s, same, jnp.where(strict, select_scale * jnp.maximum(s, 0.0), 0.0), strict

    prefix = jnp.zeros((window, 1), F32)
    for b in range(back // own):
        _, _, chosen, _ = selected(q_e[b * own : (b + 1) * own, :], b * own)
        prefix = prefix + jnp.sum(chosen, axis=1, keepdims=True)
    s_own, same, chosen, strict = selected(q_s[0], back)
    tri_row = lax.broadcasted_iota(jnp.int32, (own, own), 0)
    tri_col = lax.broadcasted_iota(jnp.int32, (own, own), 1)
    earlier = jnp.where(tri_row < tri_col, 1.0, 0.0).astype(BF)
    shadow = prefix + mm_split(chosen, earlier)
    allowed = strict | (same & (key_at == query_at + back))
    bias[...] = jnp.where(allowed, -shadow, -1e30)
    mask0[...] = jnp.where(strict & (s_own > 0.0), 1.0, 0.0).astype(BF)
    write(mask0, mask0_h)
    column_total = prefix + jnp.sum(chosen, axis=1, keepdims=True)
    key_col = lax.broadcasted_iota(jnp.int32, (window, 1), 0)
    key_pos = key_col + (start - back)
    counts = (key_pos >= 0) & (key_pos < valid_len) & ((key_col < own) | (is_last > 0))
    soft = 1.0 / (1.0 + jnp.exp(-fraction_slope * (column_total - thr[0])))
    counted = jnp.sum(jnp.where(counts, soft, 0.0), axis=0, keepdims=True)
    small[...] = jnp.zeros_like(small)
    small[1:2, :] = jnp.broadcast_to(counted / valid_len.astype(F32), (1, width))

    @pl.loop(0, pairs, unroll=2)
    def _(p):
        q2 = q_s[p]
        k2 = k_s[p]
        both = [mm_nt(k2, keep_half(q2, hh == 1)) for hh in range(2)]
        prs = []
        for hh in range(2):
            s = both[hh] + bias[...]
            e = jnp.exp(s - jnp.max(s, axis=0, keepdims=True))
            prs.append((e * (1.0 / jnp.sum(e, axis=0, keepdims=True))).astype(BF))
        for hh in range(2):
            probs[2 * p + hh] = prs[hh]
        mixed = [mm(vt_s[p, hh * HD : (hh + 1) * HD, :], prs[hh]) for hh in range(2)]
        mixt[pl.ds(pl.multiple_of(p * side, side), side), :] = jnp.concatenate(mixed, axis=0)

    mixbt[...] = mixt[...].astype(BF)
    mixb[...] = mixbt[...].T
    hid[...] = tok[back:, :].astype(F32) + mm(mixb[...], wout[...])
    hat, rate = norm_parts(hid[...])
    xhat[...] = hat
    nm[...] = (hat * gain_mid).astype(BF)
    nmt[...] = nm[...].T

    acc[...] = jnp.zeros_like(acc)
    gmid[...] = jnp.zeros_like(gmid)
    cw = CHUNK // side
    f_tiles = FF // side
    per_chunk = 2 * cw * dt
    chunks = FF // CHUNK

    @pl.loop(0, chunks)
    def _(c):
        slot = lax.rem(c, 2)
        for i in range(dt):
            for jj in range(cw):
                wu[i * side : (i + 1) * side, jj * side : (jj + 1) * side] = wall[
                    src[n_qkv + n_out + i * f_tiles + cw * c + jj]
                ]
        for ii in range(cw):
            for j in range(dt):
                wd[ii * side : (ii + 1) * side, j * side : (j + 1) * side] = wall[
                    src[n_qkv + n_out + n_up + (cw * c + ii) * dt + j]
                ]
        up = mm(nm[...], wu[...])
        cube = 0.7978845608028654 * (up + 0.044715 * up * up * up)
        th = jnp.tanh(cube)
        active = (0.5 * up * (1.0 + th)).astype(BF)
        slope = 0.5 * (1.0 + th) + 0.5 * up * (1.0 - th * th) * (
            0.7978845608028654 * (1.0 + 3.0 * 0.044715 * up * up)
        )
        acc[...] += mm(active, wd[...])
        gu = (mm_nt(dy[...], wd[...]) * slope).astype(BF)
        gmid[...] += mm_nt(gu, wu[...])

        @pl.when(c >= 2)
        def _():
            wait_tiles(stage.at[slot], sums, gsem.at[slot])

        g_down = mm(active.T, dy[...]).astype(BF)
        for ii in range(cw):
            for j in range(dt):
                at = ii * dt + j
                stage[slot, at] = g_down[ii * side : (ii + 1) * side, j * side : (j + 1) * side]
        g_up = mm(nmt[...], gu).astype(BF)
        for i in range(dt):
            for jj in range(cw):
                at = cw * dt + i * cw + jj
                stage[slot, at] = g_up[i * side : (i + 1) * side, jj * side : (jj + 1) * side]
        for ii in range(cw):
            for j in range(dt):
                at = ii * dt + j
                t = n_qkv + n_out + n_up + (cw * c + ii) * dt + j
                send_tile(stage.at[slot, at], dst[t], sums, gsem.at[slot])
        for i in range(dt):
            for jj in range(cw):
                at = cw * dt + i * cw + jj
                t = n_qkv + n_out + i * f_tiles + cw * c + jj
                send_tile(stage.at[slot, at], dst[t], sums, gsem.at[slot])

    out[...] = (hid[...] + acc[...]).astype(BF)
    write(out, out_h)
    hat = xhat[...]
    gm = gmid[...]
    small[0:1, :] = jnp.sum(gm * hat, axis=0, keepdims=True)
    scaled = gm * gain_mid
    gh = dy[...].astype(F32) + rate * (
        scaled
        - jnp.mean(scaled, axis=-1, keepdims=True)
        - hat * jnp.mean(scaled * hat, axis=-1, keepdims=True)
    )
    ghid[...] = gh
    write(ghid, ghid_h)
    gb = gh.astype(BF)
    gmix = mm_nt(gb, wout[...]).astype(BF)
    for p in range(pairs):
        g_s[p] = gmix[:, p * side : (p + 1) * side]
    gt_s[...] = gmix.T

    for slot in range(2):
        wait_tiles(stage.at[slot], sums, gsem.at[slot])
    half_out = dt // 2
    for part in range(2):
        g_out = mm(mixbt[part * half_out * side : (part + 1) * half_out * side, :], gb).astype(BF)
        for i in range(half_out):
            for j in range(dt):
                stage[part, i * dt + j] = g_out[i * side : (i + 1) * side, j * side : (j + 1) * side]
        for i in range(half_out):
            for j in range(dt):
                t = n_qkv + (part * half_out + i) * dt + j
                send_tile(stage.at[part, i * dt + j], dst[t], sums, gsem.at[part])

    gsh[...] = jnp.zeros_like(gsh)

    @pl.loop(0, pairs)
    def _(p):
        g2 = g_s[p]
        q2 = q_s[p]
        v2 = v_s[p]
        later = jnp.where(p > 0, 1.0, 0.0)
        halves = [keep_half(g2, hh == 1) for hh in range(2)]
        dps = [mm_nt(v2, halves[hh]) for hh in range(2)]
        prs = [probs[2 * p + hh] for hh in range(2)]
        rows = pl.ds(pl.multiple_of(p * side, side), side)
        product = gt_s[rows, :].astype(F32) * mixt[rows, :]
        dls = []
        for hh in range(2):
            delta = jnp.sum(product[hh * HD : (hh + 1) * HD, :], axis=0, keepdims=True)
            dls.append(prs[hh].astype(F32) * (dps[hh] - delta))
        gsh[...] += dls[0] + dls[1]

        @pl.when(p == 0)
        def _():
            part0[...] = dls[0]

        gs = [(dls[0] * later).astype(BF), dls[1].astype(BF)]
        dv = mm(prs[0], halves[0]) + mm(prs[1], halves[1])
        dk = mm(gs[0], keep_half(q2, False)) + mm(gs[1], keep_half(q2, True))
        dqs = [mm(kt_s[p, hh * HD : (hh + 1) * HD, :], gs[hh]) for hh in range(2)]
        cols = pl.ds(pl.multiple_of(p * side, side), side)
        gq[:, cols] = (jnp.concatenate(dqs, axis=0) * 0.125).T.astype(BF)
        gk[:, cols] = dk.astype(BF)
        gv[:, cols] = dv.astype(BF)

    write(gq, gq_h)
    write(gk, gk_h)
    write(gv, gv_h)
    ones = jnp.ones((8, own), BF)
    high, rest = split(-gsh[...])
    colsum[...] = mm_nt(ones, high) + mm_nt(ones, rest)
    after = jnp.where(tri_row > tri_col, 1.0, 0.0).astype(BF)
    part0[...] += select_scale * mask0[...].astype(F32) * (mm(high, after) + mm(rest, after))
    write(part0, part0_h)

    for part in range(2):
        wait_tiles(stage.at[part, pl.ds(0, half_out * dt)], sums, gsem.at[part])
    pltpu.make_async_copy(sums[0].at[pl.ds(0, empty)], sums[0].at[pl.ds(0, empty)], zsem).wait()
    for copy in writes:
        copy.wait()


def load_all(pairs, sem):
    copies = [pltpu.make_async_copy(a, b, sem.at[i]) for i, (a, b) in enumerate(pairs)]
    for copy in copies:
        copy.start()
    return copies


def qkv_kernel(dst, gq_h, gk_h, gv_h, nrm_h, *refs):
    sums = refs[3:6]
    gq, gk, gv, nrm_t, stage, lsem, gsem = refs[6:]
    own, width = gq.shape
    side = stage.shape[-1]
    dt = width // side
    back = gk.shape[0] - own
    copies = load_all([(nrm_h, nrm_t), (gv_h, gv), (gk_h, gk), (gq_h, gq)], lsem)
    copies[0].wait()
    count = 0
    for which, copy in ((2, copies[1]), (1, copies[2]), (0, copies[3])):
        copy.wait()
        bounds = [(c, c + 2) for c in range(0, dt, 2)] if which == 2 else [(1, 2)] + [(c, c + 2) for c in range(2, dt, 2)]
        for lo, hi in bounds:
            cols = slice(lo * side, hi * side)
            if which == 0:
                g = mm(nrm_t[:, back:], gq[:, cols])
            else:
                g = mm(nrm_t[...], (gk if which == 1 else gv)[:, cols])
            g = g.astype(BF)
            for i in range(dt):
                for j in range(lo, hi):
                    stage[count] = g[i * side : (i + 1) * side, (j - lo) * side : (j - lo + 1) * side]
                    send_tile(stage.at[count], dst[i * 3 * dt + which * dt + j], sums, gsem)
                    count += 1
    wait_tiles(stage, sums, gsem)


def head_kernel(dst, near_sums, far_sums, part0_h, mask0_h, q0_h, k0t_h, gq_h, gk_h, nrm_h, *refs):
    gq_out, gk_out = refs[3:5]
    sums = refs[5:8]
    part0, mask0, q0, k0t, gq, gk, nrm_t, stage, lsem, gsem = refs[8:]
    own, side = gq.shape
    window = gk.shape[0]
    back = window - own
    dt = nrm_t.shape[0] // side
    head = pl.ds(0, side)
    copies = load_all(
        [
            (part0_h, part0),
            (mask0_h, mask0),
            (k0t_h, k0t),
            (q0_h, q0),
            (gq_h.at[:, head], gq),
            (gk_h.at[:, head], gk),
            (nrm_h, nrm_t),
        ],
        lsem,
    )
    none = jnp.zeros((1, own), F32)
    suffix = jnp.concatenate([none, near_sums[0:1, : window - own]], axis=1)
    suffix = suffix + jnp.concatenate([none, none, far_sums[0:1, : window - 2 * own]], axis=1)
    column = jnp.broadcast_to(suffix, (side, window)).T
    column = jnp.concatenate([column] * (own // side), axis=1)
    for copy in copies[:-1]:
        copy.wait()
    gs = (part0[...] + select_scale * mask0[...].astype(F32) * column).astype(BF)
    dq = (mm(k0t[0:HD, :], gs) * 0.125).T
    dk = mm(gs, keep_half(q0[...], False)).astype(BF)
    gq_new = gq[...] + jnp.concatenate([dq, jnp.zeros_like(dq)], axis=1).astype(BF)
    gk_new = gk[...] + dk
    gq_out[...] = gq_new
    gk_out[...] = gk_new
    copies[-1].wait()
    g_q = mm(nrm_t[:, back:], gq_new).astype(BF)
    g_k = mm(nrm_t[...], gk_new).astype(BF)
    for which, g in ((0, g_q), (1, g_k)):
        for i in range(dt):
            stage[which * dt + i] = g[i * side : (i + 1) * side, :]
            send_tile(stage.at[which * dt + i], dst[i * 3 * dt + which * dt], sums, gsem)
    wait_tiles(stage, sums, gsem)


def pre_kernel(tok, gq_head, gk_head, gq_h, gk_h, gv_h, wqkv_h, far, near, mine, small, gq, gk, gv, wqkv, lsem):
    own, width = gq.shape
    window = gk.shape[0]
    side = gq_head.shape[1]
    rest = pl.ds(side, width - side)
    copies = load_all(
        [(wqkv_h, wqkv), (gk_h.at[:, rest], gk.at[:, rest]), (gv_h, gv), (gq_h.at[:, rest], gq.at[:, rest])], lsem
    )
    gq[:, 0:side] = gq_head[...]
    gk[:, 0:side] = gk_head[...]
    for copy in copies:
        copy.wait()
    total = jnp.zeros((1, width), F32)
    for b in range(window // own):
        rows = slice(b * own, (b + 1) * own)
        g = mm_nt(gk[rows, :], wqkv[:, width : 2 * width]) + mm_nt(gv[rows, :], wqkv[:, 2 * width :])
        if b == window // own - 1:
            g = g + mm_nt(gq[...], wqkv[:, :width])
            mine[...] = g
        elif b == 0:
            far[...] = g.astype(far.dtype)
        else:
            near[...] = g.astype(near.dtype)
        hat, _ = norm_parts(tok[rows, :].astype(F32))
        total = total + jnp.sum(g * hat, axis=0, keepdims=True)
    small[...] = jnp.broadcast_to(total, small.shape)


def input_kernel(tok, gains, ghid, mine, near, far, out):
    hat, rate = norm_parts(tok[...].astype(F32))
    g = mine[...] + near[...].astype(F32) + far[...].astype(F32)
    scaled = g * gains[0:1, :]
    out[...] = ghid[...] + rate * (
        scaled
        - jnp.mean(scaled, axis=-1, keepdims=True)
        - hat * jnp.mean(scaled * hat, axis=-1, keepdims=True)
    )


def adam_kernel(correction, parts, *refs):
    grads, refs = refs[: 2 * len(parts)], refs[2 * len(parts) :]
    holds, first, second, left, right, weight, first_out, second_out, weight_out = refs
    slots = []
    for index, (at, size, _) in enumerate(parts):
        slots += [(at + k, grads[2 * index], grads[2 * index + 1], k) for k in range(size)]
    for low in range(0, len(slots), ADAM_GROUP):
        group = slots[low : low + ADAM_GROUP]
        rights, turned, steps, undone = {}, {}, {}, {}
        for slot, mine, other, k in group:
            grad = mine[k].astype(F32) + other[k].astype(F32)
            grad = jnp.where(holds[slot] > 0, grad, 0.0)
            rights[slot] = split(right[slot])
            turned[slot] = mm3(split(grad), rights[slot])
        for slot, *_ in group:
            turned[slot] = mm3(split(left[slot].T), split(turned[slot]))
        for slot, *_ in group:
            t = turned[slot]
            first_new = first_decay * first[slot] + (1.0 - first_decay) * t
            second_new = second_decay * second[slot] + (1.0 - second_decay) * t * t
            first_out[slot] = first_new
            second_out[slot] = second_new
            steps[slot] = first_new / correction / (jnp.sqrt(second_new / correction) + adam_epsilon)
        for slot, *_ in group:
            undone[slot] = mm3_nt(split(steps[slot]), rights[slot])
        for slot, *_ in group:
            back = mm3(split(left[slot]), split(undone[slot]))
            w = weight[slot]
            weight_out[slot] = w - weight_rate * back - weight_rate * decay_rate * w


def after(x, earlier):
    return lax.optimization_barrier((x, earlier))[0]


def bit_plan(devices, per_device):
    bits = [1 << b for b in range(devices.bit_length() - 1)]
    first, rest = bits[0], bits[1:]
    if devices == 32:
        orders = [(2, 4, 8, 16), (4, 8, 2, 16), (8, 16, 2, 4)]
    else:
        orders = [tuple(rest[i:] + rest[:i]) for i in range(3)]
    if per_device < 4:
        sizes = [1] * per_device
    else:
        sizes = [per_device * 3 // 7, per_device * 5 // 14]
        sizes.append(per_device - sum(sizes))
    plan = []
    at = 0
    for size, order in zip(sizes, orders):
        if size:
            plan.append((at, size, order))
            at += size
    return first, plan


def gather_parts(devices, per_device):
    if devices != 32 or per_device < 8:
        return per_device, []
    size = per_device * 2 // 7
    first = per_device * 3 // 14
    return first, [
        (first, size, (16, 8, 4, 2, 1)),
        (first + size, size, (16, 8, 2, 4, 1)),
        (first + 2 * size, per_device - first - 2 * size, (4, 2, 16, 8, 1)),
    ]


def local(
    tokens,
    segment_ids,
    pad_lengths,
    threshold,
    gains,
    gain_first,
    gain_second,
    slot_tiles,
    weight_slots,
    first_moment,
    second_moment,
    basis_left,
    basis_right,
    out_grad,
):
    axes = ("dp", "seq")
    n_dp, n_seq = lax.axis_size("dp"), lax.axis_size("seq")
    devices = n_dp * n_seq
    me = lax.axis_index(axes)
    seq_at = lax.axis_index("seq")
    _, own, width = tokens.shape
    length = segment_ids.shape[1]
    side = weight_slots.shape[-1]
    per_device = weight_slots.shape[0]
    slot_total = slot_tiles.shape[0]
    dt = width // side
    tiles = (3 * dt * dt, dt * dt, dt * (FF // side), dt * (FF // side))
    tile_count = sum(tiles)
    back = SPAN
    window = back + own

    def swap(x, bit):
        return lax.ppermute(x, axes, [(i, i ^ bit) for i in range(devices)])

    slot_ids = jnp.arange(slot_total, dtype=jnp.int32)
    position = jnp.sum(
        jnp.where(slot_tiles[None, :] == slot_ids[:, None], slot_ids[None, :], 0), axis=1
    )
    owner = position // per_device
    inner = position % per_device
    apart = owner ^ me
    first_bit, plan = bit_plan(devices, per_device)
    half = slot_total // 2
    spread = devices // 2
    place = jnp.zeros_like(position)
    for at, size, order in plan:
        index = jnp.zeros_like(position)
        for bit in order:
            index = index * 2 + ((apart & bit) != 0).astype(jnp.int32)
        here = at * spread + index * size + (inner - at)
        place = jnp.where((inner >= at) & (inner < at + size), here, place)
    dst = place + jnp.where((apart & first_bit) != 0, half, 0)
    by_gather, gather_plan = gather_parts(devices, per_device)
    src = owner * by_gather + inner
    base = devices * by_gather
    for at, size, order in gather_plan:
        index = jnp.zeros_like(position)
        for bit in reversed(order):
            index = index * 2 + ((apart & bit) != 0).astype(jnp.int32)
        here = base + index * size + (inner - at)
        src = jnp.where((inner >= at) & (inner < at + size), here, src)
        base += devices * size

    mine_tok = tokens[0]
    seen = []
    for step in range(back // own, 0, -1):
        seen.append(lax.ppermute(mine_tok, "seq", [(i, i + step) for i in range(n_seq - step)]))
    tok = jnp.concatenate(seen + [mine_tok], axis=0)
    start = seq_at * own
    seg_window = lax.dynamic_slice_in_dim(
        jnp.concatenate([jnp.full((back,), -1, jnp.int32), segment_ids[0]]), start, window
    )
    valid_len = length - pad_lengths[0]
    scal = jnp.stack([valid_len, start, (seq_at == n_seq - 1).astype(jnp.int32)])

    segc, segr = seg_window[:, None], seg_window[None, :]

    rounded = weight_slots.astype(BF)
    pieces = [lax.all_gather(rounded[:by_gather], axes, axis=0, tiled=True)]
    held = [rounded[at : at + size] for at, size, _ in gather_plan]
    for step in range(len(gather_plan[0][2]) - 2 if gather_plan else 0):
        held = [jnp.concatenate([h, swap(h, o[2][step])], axis=0) for h, o in zip(held, gather_plan)]
        if step == 1:
            held[0], tok, src, dst, scal, segc, segr = lax.optimization_barrier(
                (held[0], tok, src, dst, scal, segc, segr)
            )
    for h, (_, _, order) in zip(held, gather_plan):
        two = [h, swap(h, order[-2])]
        pieces += two + [swap(x, order[-1]) for x in two]
    sizes = [p.shape[0] for p in pieces]

    hbm = pl.BlockSpec(memory_space=pltpu.HBM)
    vm = pl.BlockSpec(memory_space=VMEM)
    sm = pl.BlockSpec(memory_space=SMEM)
    shp = jax.ShapeDtypeStruct
    first_rows = plan[0][1] * spread
    sums_shapes = [shp((n, side, side), BF) for n in (half, first_rows, half - first_rows)]
    per_chunk = 2 * (CHUNK // side) * dt
    outs = pl.pallas_call(
        functools.partial(layer_kernel, tiles, sizes),
        out_shape=(
            shp((own, width), BF),
            shp((own, width), F32),
            shp((own, width), BF),
            shp((window, width), BF),
            shp((window, width), BF),
            shp((width, window), BF),
            shp((width, 3 * width), BF),
            shp((own, side), BF),
            shp((side, window), BF),
            shp((window, own), F32),
            shp((window, own), BF),
            shp((8, window), F32),
            shp((8, width), F32),
            *sums_shapes,
        ),
        in_specs=[sm] * 4 + [vm] * 5 + [hbm] * len(sizes),
        out_specs=tuple([hbm] * 11 + [vm] * 2 + [hbm] * 3),
        scratch_shapes=[
            VMEM((own, width), BF),
            VMEM((own, width), F32),
            VMEM((own, width), BF),
            VMEM((window, width), BF),
            VMEM((window, width), BF),
            VMEM((width, window), BF),
            VMEM((width, 3 * width), BF),
            VMEM((window, own), F32),
            VMEM((window, own), BF),
            VMEM((slot_total, side, side), BF),
            VMEM((window, width), BF),
            VMEM((dt, own, side), BF),
            VMEM((back, side), BF),
            VMEM((dt, window, side), BF),
            VMEM((dt, window, side), BF),
            VMEM((dt, side, window), BF),
            VMEM((dt, side, window), BF),
            VMEM((window, own), F32),
            VMEM((window, own), F32),
            VMEM((H, window, own), BF),
            VMEM((width, own), F32),
            VMEM((own, width), BF),
            VMEM((width, own), BF),
            VMEM((width, width), BF),
            VMEM((own, width), F32),
            VMEM((own, width), F32),
            VMEM((own, width), BF),
            VMEM((width, own), BF),
            VMEM((own, width), F32),
            VMEM((own, width), F32),
            VMEM((dt, own, side), BF),
            VMEM((width, own), BF),
            VMEM((width, CHUNK), BF),
            VMEM((CHUNK, width), BF),
            VMEM((2, per_chunk, side, side), BF),
            VMEM((side, side), BF),
            pltpu.SemaphoreType.DMA((len(sizes),)),
            pltpu.SemaphoreType.DMA((2,)),
            pltpu.SemaphoreType.DMA,
            pltpu.SemaphoreType.DMA((11,)),
        ],
        compiler_params=pltpu.CompilerParams(vmem_limit_bytes=60 << 20),
        name="layer",
    )(
        src,
        dst,
        scal,
        threshold,
        tok,
        gains,
        out_grad[0],
        segc,
        segr,
        *pieces,
    )
    (output, ghid, gq, gk, gv, nrm_t, wqkv, q0, k0t, part0, mask0, colsum, small, *sums) = outs

    near_sums, far_sums = [
        lax.ppermute(colsum, "seq", [(i, i - step) for i in range(step, n_seq)]) for step in (1, 2)
    ]
    main_tiles = tiles[0] - 2 * dt
    sums = pl.pallas_call(
        qkv_kernel,
        out_shape=sums_shapes,
        in_specs=[sm] + [hbm] * 7,
        out_specs=[hbm] * 3,
        scratch_shapes=[
            VMEM((own, width), BF),
            VMEM((window, width), BF),
            VMEM((window, width), BF),
            VMEM((width, window), BF),
            VMEM((main_tiles, side, side), BF),
            pltpu.SemaphoreType.DMA((4,)),
            pltpu.SemaphoreType.DMA,
        ],
        input_output_aliases={5: 0, 6: 1, 7: 2},
        compiler_params=pltpu.CompilerParams(vmem_limit_bytes=60 << 20),
        cost_estimate=pl.CostEstimate(
            flops=2 * (2 * window + own) * width * width, bytes_accessed=8 << 20, transcendentals=0
        ),
        name="qkv_grad",
    )(dst, gq, gk, gv, nrm_t, *sums)
    gq_head, gk_head, stay, *aways = pl.pallas_call(
        head_kernel,
        out_shape=(shp((own, side), BF), shp((window, side), BF), *sums_shapes),
        in_specs=[sm, vm, vm] + [hbm] * 10,
        out_specs=(vm, vm, hbm, hbm, hbm),
        scratch_shapes=[
            VMEM((window, own), F32),
            VMEM((window, own), BF),
            VMEM((own, side), BF),
            VMEM((side, window), BF),
            VMEM((own, side), BF),
            VMEM((window, side), BF),
            VMEM((width, window), BF),
            VMEM((2 * dt, side, side), BF),
            pltpu.SemaphoreType.DMA((7,)),
            pltpu.SemaphoreType.DMA,
        ],
        input_output_aliases={10: 2, 11: 3, 12: 4},
        compiler_params=pltpu.CompilerParams(vmem_limit_bytes=60 << 20),
        cost_estimate=pl.CostEstimate(flops=1 << 30, bytes_accessed=4 << 20, transcendentals=0),
        name="head_grad",
    )(dst, near_sums, far_sums, part0, mask0, q0, k0t, gq, gk, nrm_t, *sums)

    def plus(a, b):
        return (a.astype(F32) + b.astype(F32)).astype(BF)

    got = [swap(aways[0], first_bit)]
    aways[1] = after(aways[1], got[0])
    got.append(swap(aways[1], first_bit))
    steps = len(plan[0][2])

    def from_got(which, low, high):
        at, size, _ = plan[which]
        start = at * spread
        source, base = (got[0], 0) if which == 0 else (got[1], first_rows)
        rows = slice(start + low * size * spread // 2, start + high * size * spread // 2)
        return plus(stay[rows], source[rows.start - base : rows.stop - base])

    sent = [from_got(0, 1, 2)]
    for which in range(1, len(plan)):
        got[1] = after(got[1], sent[-1])
        sent.append(from_got(which, 1, 2))
    gq_head = after(gq_head, sent[-1])
    came = [swap(piece, order[0]) for piece, (_, _, order) in zip(sent, plan)]
    left = [from_got(which, 0, 1) for which in range(len(plan))]
    far, near, mine, small_pre = pl.pallas_call(
        pre_kernel,
        out_shape=(
            shp((own, width), BF),
            shp((own, width), BF),
            shp((own, width), F32),
            shp((8, width), F32),
        ),
        in_specs=[vm] * 3 + [hbm] * 4,
        out_specs=tuple([vm] * 4),
        scratch_shapes=[
            VMEM((own, width), BF),
            VMEM((window, width), BF),
            VMEM((window, width), BF),
            VMEM((width, 3 * width), BF),
            pltpu.SemaphoreType.DMA((4,)),
        ],
        compiler_params=pltpu.CompilerParams(vmem_limit_bytes=30 << 20),
        cost_estimate=pl.CostEstimate(
            flops=2 * (2 * window + own) * width * width, bytes_accessed=10 << 20, transcendentals=0
        ),
        name="pre_grad",
    )(tok, gq_head, gk_head, gq, gk, gv, wqkv)
    row_at = lax.axis_index("dp")
    spots = jnp.arange(width, dtype=jnp.int32)
    totals = jnp.stack([small_pre[0], small[0], jnp.where(spots == row_at, small[1], 0.0)])
    totals = jnp.pad(totals.reshape(3 * dt, side), ((0, side // 2 - 3 * dt), (0, 0)))
    gathered = lax.all_gather(totals, axes)
    last = (sent[-1], totals)
    for step in range(1, steps):
        for which in reversed(range(len(plan))):
            order = plan[which][2]
            came[which] = after(came[which], last)
            middle = left[which].shape[0] // 2
            piece = plus(left[which][middle:], came[which][middle:])
            rest = plus(left[which][:middle], came[which][:middle])
            if which == 0 and step == 1:
                far, near = after(far, piece), after(near, piece)
                far = lax.ppermute(far, "seq", [(i, i - 2) for i in range(2, n_seq)])
                near = lax.ppermute(near, "seq", [(i, i - 1) for i in range(1, n_seq)])
            if which == 0 and step == steps - 1:
                far, near, mine = after(far, piece), after(near, piece), after(mine, piece)
                rest, gathered = lax.optimization_barrier((rest, gathered))
            came[which] = swap(piece, order[step])
            left[which] = rest
            last = piece
    pairs = list(zip(left, came))
    totals = jnp.sum(gathered[:, : 3 * dt], axis=0).reshape(3, width)
    correction = 1.0 - first_decay**STEP
    holds = lax.dynamic_slice_in_dim((slot_tiles < tile_count).astype(jnp.int32), me * per_device, per_device)
    moment_first, moment_second, new_weights = pl.pallas_call(
        functools.partial(adam_kernel, correction, plan),
        out_shape=tuple([shp(weight_slots.shape, F32)] * 3),
        in_specs=[vm] * (2 * len(plan)) + [sm] + [vm] * 5,
        out_specs=tuple([vm] * 3),
        compiler_params=pltpu.CompilerParams(vmem_limit_bytes=30 << 20),
        name="adam",
    )(*[x for pair in pairs for x in pair], holds, first_moment, second_moment, basis_left, basis_right, weight_slots)
    input_grad = pl.pallas_call(
        input_kernel,
        out_shape=shp((own, width), F32),
        in_specs=[vm] * 6,
        out_specs=vm,
        compiler_params=pltpu.CompilerParams(vmem_limit_bytes=20 << 20),
        name="input_grad",
    )(mine_tok, gains, ghid, mine, near, far)

    gain_total = totals[:2]
    fraction = lax.dynamic_slice_in_dim(totals[2], row_at, 1)

    gain_moment = first_decay * gain_first + (1.0 - first_decay) * gain_total
    gain_square = second_decay * gain_second + (1.0 - second_decay) * gain_total * gain_total
    gain_update = gains - gain_rate * (gain_moment / correction) / (
        jnp.sqrt(gain_square / correction) + adam_epsilon
    )
    return (
        output[None],
        input_grad[None],
        fraction,
        moment_first,
        moment_second,
        new_weights,
        gain_update,
        gain_moment,
        gain_square,
    )


def solution(mesh):
    in_specs = (
        P("dp", "seq", None),
        P("dp", None),
        P("dp"),
        P(),
        P(),
        P(),
        P(),
        P(),
        P(("dp", "seq"), None, None),
        P(("dp", "seq"), None, None),
        P(("dp", "seq"), None, None),
        P(("dp", "seq"), None, None),
        P(("dp", "seq"), None, None),
        P("dp", "seq", None),
    )
    out_specs = (
        P("dp", "seq", None),
        P("dp", "seq", None),
        P("dp"),
        P(("dp", "seq"), None, None),
        P(("dp", "seq"), None, None),
        P(("dp", "seq"), None, None),
        P(),
        P(),
        P(),
    )
    return jax.shard_map(local, mesh=mesh, in_specs=in_specs, out_specs=out_specs, check_vma=False)
```

```python
import functools

import jax
import jax.numpy as jnp
from jax import lax
from jax.experimental import pallas as pl
from jax.experimental.pallas import tpu as pltpu
from jax.sharding import PartitionSpec as P

H = 12
HD = 64
FF = 3072
STEP = 3
SPAN = 512
CHUNK = 768
ADAM_GROUP = 7

select_scale = 0.2
fraction_slope = 2.0
first_decay = 0.5
second_decay = 0.5
adam_epsilon = 1e-08
weight_rate = 0.05
gain_rate = 0.2
decay_rate = 0.1
norm_epsilon = 1e-05

BF = jnp.bfloat16
F32 = jnp.float32
VMEM = pltpu.VMEM
SMEM = pltpu.SMEM


def mm(a, b):
    return lax.dot_general(a, b, (((1,), (0,)), ((), ())), preferred_element_type=F32)


def mm_nt(a, b):
    return lax.dot_general(a, b, (((1,), (1,)), ((), ())), preferred_element_type=F32)


def split(x):
    high = x.astype(BF)
    return high, (x - high.astype(F32)).astype(BF)


def mm_split(x, exact):
    high, rest = split(x)
    return mm(high, exact) + mm(rest, exact)


def lane_half(shape, second):
    lane = lax.broadcasted_iota(jnp.int32, shape, 1)
    return (lane >= HD) if second else (lane < HD)


def keep_half(x, second):
    return jnp.where(lane_half(x.shape, second), x, jnp.zeros_like(x))


def norm_parts(x):
    centred = x - jnp.mean(x, axis=-1, keepdims=True)
    rate = lax.rsqrt(jnp.mean(centred * centred, axis=-1, keepdims=True) + norm_epsilon)
    return centred * rate, rate


def send_tile(tile_ref, dst, sums, sem):
    low = 0
    for buffer in sums:
        high = low + buffer.shape[0]

        @pl.when((dst >= low) & (dst < high))
        def _(buffer=buffer, low=low):
            pltpu.make_async_copy(tile_ref, buffer.at[dst - low], sem).start()

        low = high


def wait_tiles(stage_ref, sums, sem):
    pltpu.make_async_copy(stage_ref, sums[0].at[pl.ds(0, stage_ref.shape[0])], sem).wait()


def mm3(a, b):
    (ah, al), (bh, bl) = a, b
    return mm(jnp.concatenate([ah, ah, al], axis=1), jnp.concatenate([bh, bl, bh], axis=0))


def mm3_nt(a, b):
    (ah, al), (bh, bl) = a, b
    return mm_nt(jnp.concatenate([ah, ah, al], axis=1), jnp.concatenate([bh, bl, bh], axis=1))


def layer_kernel(tiles, sizes, *refs):
    (src, dst, scal, thr, tok, gains, dy, segc, segr), refs = refs[:9], refs[9:]
    w_parts, refs = refs[: len(sizes)], refs[len(sizes) :]
    (out_h, ghid_h, gq_h, gk_h, gv_h, nrm_t_h, wqkv_h, q0_h, k0t_h, part0_h, mask0_h, colsum, small, *sums), refs = (
        refs[:16],
        refs[16:],
    )
    (out, ghid, gq, gk, gv, nrm_t, wqkv, part0, mask0), refs = refs[:9], refs[9:]
    (wall, nrm, q_s, q_e, k_s, v_s, kt_s, vt_s, bias, gsh, probs, mixt, mixb, mixbt, wout, hid, xhat), refs = (
        refs[:17],
        refs[17:],
    )
    nm, nmt, acc, gmid, g_s, gt_s, wu, wd, stage, zero, wsem, gsem, zsem, osem = refs

    writes = []

    def write(ref, target):
        copy = pltpu.make_async_copy(ref, target, osem.at[len(writes)])
        copy.start()
        writes.append(copy)

    n_qkv, n_out, n_up, n_down = tiles
    width = tok.shape[1]
    own = dy.shape[0]
    window = tok.shape[0]
    back = window - own
    side = wall.shape[-1]
    dt = width // side
    pairs = width // side
    total_slots = 2 * sums[0].shape[0]
    loads = []
    at = 0
    for index, (part, size) in enumerate(zip(w_parts, sizes)):
        loads.append(pltpu.make_async_copy(part, wall.at[pl.ds(at, size)], wsem.at[index]))
        loads[-1].start()
        at += size
    zero[...] = jnp.zeros_like(zero)
    tile_count = n_qkv + n_out + n_up + n_down
    empty = total_slots - tile_count

    @pl.loop(0, empty)
    def _(e):
        send_tile(zero, dst[tile_count + e], sums, zsem)

    gain_pre = gains[0:1, :]
    gain_mid = gains[1:2, :]

    @pl.loop(0, window // own)
    def _(b):
        rows = pl.ds(pl.multiple_of(b * own, own), own)
        hat, _ = norm_parts(tok[rows, :].astype(F32))
        value = (hat * gain_pre).astype(BF)
        nrm[rows, :] = value
        nrm_t[:, rows] = value.T

    write(nrm_t, nrm_t_h)
    for load in loads:
        load.wait()
    per_row = 3 * dt

    @pl.loop(0, 3 * dt // 2)
    def _(j):
        for i in range(dt):
            for jj in range(2):
                wqkv[i * side : (i + 1) * side, pl.ds(pl.multiple_of((2 * j + jj) * side, side), side)] = wall[
                    src[i * per_row + 2 * j + jj]
                ]

    write(wqkv, wqkv_h)
    for i in range(dt):
        for j in range(dt):
            wout[i * side : (i + 1) * side, j * side : (j + 1) * side] = wall[src[n_qkv + i * dt + j]]

    @pl.loop(0, dt // 2, unroll=True)
    def _(j):
        cols = pl.ds(pl.multiple_of(2 * j * side, 2 * side), 2 * side)
        got = (mm(nrm[back:, :], wqkv[:, cols]) * 0.125).astype(BF)
        q_s[2 * j] = got[:, :side]
        q_s[2 * j + 1] = got[:, side:]

    q_e[...] = (mm(nrm[:back, :], wqkv[:, 0:side]) * 0.125).astype(BF)

    @pl.loop(0, dt // 2, unroll=True)
    def _(j):
        cols = pl.ds(pl.multiple_of(width + 2 * j * side, 2 * side), 2 * side)
        got = mm(nrm[...], wqkv[:, cols]).astype(BF)
        got_t = got.T
        k_s[2 * j] = got[:, :side]
        k_s[2 * j + 1] = got[:, side:]
        kt_s[2 * j] = got_t[:side, :]
        kt_s[2 * j + 1] = got_t[side:, :]

    @pl.loop(0, dt // 2, unroll=True)
    def _(j):
        cols = pl.ds(pl.multiple_of(2 * width + 2 * j * side, 2 * side), 2 * side)
        got = mm(nrm[...], wqkv[:, cols]).astype(BF)
        got_t = got.T
        v_s[2 * j] = got[:, :side]
        v_s[2 * j + 1] = got[:, side:]
        vt_s[2 * j] = got_t[:side, :]
        vt_s[2 * j + 1] = got_t[side:, :]

    write(q_s.at[0], q0_h)
    write(kt_s.at[0], k0t_h)

    valid_len = scal[0]
    start = scal[1]
    is_last = scal[2]
    key_at = lax.broadcasted_iota(jnp.int32, (window, own), 0)
    query_at = lax.broadcasted_iota(jnp.int32, (window, own), 1)
    key_valid = (key_at + (start - back)) < valid_len
    key_seg = segc[...]
    k_first = k_s[0]

    def selected(q_rows, first):
        s = mm_nt(k_first, keep_half(q_rows, False))
        same = key_seg == segr[:, first : first + own]
        strict = same & key_valid & (key_at < query_at + first)
        return s, same, jnp.where(strict, select_scale * jnp.maximum(s, 0.0), 0.0), strict

    prefix = jnp.zeros((window, 1), F32)
    for b in range(back // own):
        _, _, chosen, _ = selected(q_e[b * own : (b + 1) * own, :], b * own)
        prefix = prefix + jnp.sum(chosen, axis=1, keepdims=True)
    s_own, same, chosen, strict = selected(q_s[0], back)
    tri_row = lax.broadcasted_iota(jnp.int32, (own, own), 0)
    tri_col = lax.broadcasted_iota(jnp.int32, (own, own), 1)
    earlier = jnp.where(tri_row < tri_col, 1.0, 0.0).astype(BF)
    shadow = prefix + mm_split(chosen, earlier)
    allowed = strict | (same & (key_at == query_at + back))
    bias[...] = jnp.where(allowed, -shadow, -1e30)
    mask0[...] = jnp.where(strict & (s_own > 0.0), 1.0, 0.0).astype(BF)
    write(mask0, mask0_h)
    column_total = prefix + jnp.sum(chosen, axis=1, keepdims=True)
    key_col = lax.broadcasted_iota(jnp.int32, (window, 1), 0)
    key_pos = key_col + (start - back)
    counts = (key_pos >= 0) & (key_pos < valid_len) & ((key_col < own) | (is_last > 0))
    soft = 1.0 / (1.0 + jnp.exp(-fraction_slope * (column_total - thr[0])))
    counted = jnp.sum(jnp.where(counts, soft, 0.0), axis=0, keepdims=True)
    small[...] = jnp.zeros_like(small)
    small[1:2, :] = jnp.broadcast_to(counted / valid_len.astype(F32), (1, width))

    @pl.loop(0, pairs, unroll=2)
    def _(p):
        q2 = q_s[p]
        k2 = k_s[p]
        both = [mm_nt(k2, keep_half(q2, hh == 1)) for hh in range(2)]
        prs = []
        for hh in range(2):
            s = both[hh] + bias[...]
            e = jnp.exp(s - jnp.max(s, axis=0, keepdims=True))
            prs.append((e * (1.0 / jnp.sum(e, axis=0, keepdims=True))).astype(BF))
        for hh in range(2):
            probs[2 * p + hh] = prs[hh]
        mixed = [mm(vt_s[p, hh * HD : (hh + 1) * HD, :], prs[hh]) for hh in range(2)]
        mixt[pl.ds(pl.multiple_of(p * side, side), side), :] = jnp.concatenate(mixed, axis=0)

    mixbt[...] = mixt[...].astype(BF)
    mixb[...] = mixbt[...].T
    hid[...] = tok[back:, :].astype(F32) + mm(mixb[...], wout[...])
    hat, rate = norm_parts(hid[...])
    xhat[...] = hat
    nm[...] = (hat * gain_mid).astype(BF)
    nmt[...] = nm[...].T

    acc[...] = jnp.zeros_like(acc)
    gmid[...] = jnp.zeros_like(gmid)
    cw = CHUNK // side
    f_tiles = FF // side
    per_chunk = 2 * cw * dt
    chunks = FF // CHUNK

    @pl.loop(0, chunks)
    def _(c):
        slot = lax.rem(c, 2)
        for i in range(dt):
            for jj in range(cw):
                wu[i * side : (i + 1) * side, jj * side : (jj + 1) * side] = wall[
                    src[n_qkv + n_out + i * f_tiles + cw * c + jj]
                ]
        for ii in range(cw):
            for j in range(dt):
                wd[ii * side : (ii + 1) * side, j * side : (j + 1) * side] = wall[
                    src[n_qkv + n_out + n_up + (cw * c + ii) * dt + j]
                ]
        up = mm(nm[...], wu[...])
        cube = 0.7978845608028654 * (up + 0.044715 * up * up * up)
        th = jnp.tanh(cube)
        active = (0.5 * up * (1.0 + th)).astype(BF)
        slope = 0.5 * (1.0 + th) + 0.5 * up * (1.0 - th * th) * (
            0.7978845608028654 * (1.0 + 3.0 * 0.044715 * up * up)
        )
        acc[...] += mm(active, wd[...])
        gu = (mm_nt(dy[...], wd[...]) * slope).astype(BF)
        gmid[...] += mm_nt(gu, wu[...])

        @pl.when(c >= 2)
        def _():
            wait_tiles(stage.at[slot], sums, gsem.at[slot])

        g_down = mm(active.T, dy[...]).astype(BF)
        for ii in range(cw):
            for j in range(dt):
                at = ii * dt + j
                stage[slot, at] = g_down[ii * side : (ii + 1) * side, j * side : (j + 1) * side]
        g_up = mm(nmt[...], gu).astype(BF)
        for i in range(dt):
            for jj in range(cw):
                at = cw * dt + i * cw + jj
                stage[slot, at] = g_up[i * side : (i + 1) * side, jj * side : (jj + 1) * side]
        for ii in range(cw):
            for j in range(dt):
                at = ii * dt + j
                t = n_qkv + n_out + n_up + (cw * c + ii) * dt + j
                send_tile(stage.at[slot, at], dst[t], sums, gsem.at[slot])
        for i in range(dt):
            for jj in range(cw):
                at = cw * dt + i * cw + jj
                t = n_qkv + n_out + i * f_tiles + cw * c + jj
                send_tile(stage.at[slot, at], dst[t], sums, gsem.at[slot])

    out[...] = (hid[...] + acc[...]).astype(BF)
    write(out, out_h)
    hat = xhat[...]
    gm = gmid[...]
    small[0:1, :] = jnp.sum(gm * hat, axis=0, keepdims=True)
    scaled = gm * gain_mid
    gh = dy[...].astype(F32) + rate * (
        scaled
        - jnp.mean(scaled, axis=-1, keepdims=True)
        - hat * jnp.mean(scaled * hat, axis=-1, keepdims=True)
    )
    ghid[...] = gh
    write(ghid, ghid_h)
    gb = gh.astype(BF)
    gmix = mm_nt(gb, wout[...]).astype(BF)
    for p in range(pairs):
        g_s[p] = gmix[:, p * side : (p + 1) * side]
    gt_s[...] = gmix.T

    for slot in range(2):
        wait_tiles(stage.at[slot], sums, gsem.at[slot])
    half_out = dt // 2
    for part in range(2):
        g_out = mm(mixbt[part * half_out * side : (part + 1) * half_out * side, :], gb).astype(BF)
        for i in range(half_out):
            for j in range(dt):
                stage[part, i * dt + j] = g_out[i * side : (i + 1) * side, j * side : (j + 1) * side]
        for i in range(half_out):
            for j in range(dt):
                t = n_qkv + (part * half_out + i) * dt + j
                send_tile(stage.at[part, i * dt + j], dst[t], sums, gsem.at[part])

    gsh[...] = jnp.zeros_like(gsh)

    @pl.loop(0, pairs)
    def _(p):
        g2 = g_s[p]
        q2 = q_s[p]
        v2 = v_s[p]
        later = jnp.where(p > 0, 1.0, 0.0)
        halves = [keep_half(g2, hh == 1) for hh in range(2)]
        dps = [mm_nt(v2, halves[hh]) for hh in range(2)]
        prs = [probs[2 * p + hh] for hh in range(2)]
        rows = pl.ds(pl.multiple_of(p * side, side), side)
        product = gt_s[rows, :].astype(F32) * mixt[rows, :]
        dls = []
        for hh in range(2):
            delta = jnp.sum(product[hh * HD : (hh + 1) * HD, :], axis=0, keepdims=True)
            dls.append(prs[hh].astype(F32) * (dps[hh] - delta))
        gsh[...] += dls[0] + dls[1]

        @pl.when(p == 0)
        def _():
            part0[...] = dls[0]

        gs = [(dls[0] * later).astype(BF), dls[1].astype(BF)]
        dv = mm(prs[0], halves[0]) + mm(prs[1], halves[1])
        dk = mm(gs[0], keep_half(q2, False)) + mm(gs[1], keep_half(q2, True))
        dqs = [mm(kt_s[p, hh * HD : (hh + 1) * HD, :], gs[hh]) for hh in range(2)]
        cols = pl.ds(pl.multiple_of(p * side, side), side)
        gq[:, cols] = (jnp.concatenate(dqs, axis=0) * 0.125).T.astype(BF)
        gk[:, cols] = dk.astype(BF)
        gv[:, cols] = dv.astype(BF)

    write(gq, gq_h)
    write(gk, gk_h)
    write(gv, gv_h)
    ones = jnp.ones((8, own), BF)
    high, rest = split(-gsh[...])
    colsum[...] = mm_nt(ones, high) + mm_nt(ones, rest)
    after = jnp.where(tri_row > tri_col, 1.0, 0.0).astype(BF)
    part0[...] += select_scale * mask0[...].astype(F32) * (mm(high, after) + mm(rest, after))
    write(part0, part0_h)

    for part in range(2):
        wait_tiles(stage.at[part, pl.ds(0, half_out * dt)], sums, gsem.at[part])
    pltpu.make_async_copy(sums[0].at[pl.ds(0, empty)], sums[0].at[pl.ds(0, empty)], zsem).wait()
    for copy in writes:
        copy.wait()


def load_all(pairs, sem):
    copies = [pltpu.make_async_copy(a, b, sem.at[i]) for i, (a, b) in enumerate(pairs)]
    for copy in copies:
        copy.start()
    return copies


def qkv_kernel(dst, gq_h, gk_h, gv_h, nrm_h, *refs):
    sums = refs[3:6]
    gq, gk, gv, nrm_t, stage, lsem, gsem = refs[6:]
    own, width = gq.shape
    side = stage.shape[-1]
    dt = width // side
    back = gk.shape[0] - own
    copies = load_all([(nrm_h, nrm_t), (gv_h, gv), (gk_h, gk), (gq_h, gq)], lsem)
    copies[0].wait()
    count = 0
    for which, copy in ((2, copies[1]), (1, copies[2]), (0, copies[3])):
        copy.wait()
        bounds = [(c, c + 2) for c in range(0, dt, 2)] if which == 2 else [(1, 2)] + [(c, c + 2) for c in range(2, dt, 2)]
        for lo, hi in bounds:
            cols = slice(lo * side, hi * side)
            if which == 0:
                g = mm(nrm_t[:, back:], gq[:, cols])
            else:
                g = mm(nrm_t[...], (gk if which == 1 else gv)[:, cols])
            g = g.astype(BF)
            for i in range(dt):
                for j in range(lo, hi):
                    stage[count] = g[i * side : (i + 1) * side, (j - lo) * side : (j - lo + 1) * side]
                    send_tile(stage.at[count], dst[i * 3 * dt + which * dt + j], sums, gsem)
                    count += 1
    wait_tiles(stage, sums, gsem)


def head_kernel(dst, near_sums, far_sums, part0_h, mask0_h, q0_h, k0t_h, gq_h, gk_h, nrm_h, *refs):
    gq_out, gk_out = refs[3:5]
    sums = refs[5:8]
    part0, mask0, q0, k0t, gq, gk, nrm_t, stage, lsem, gsem = refs[8:]
    own, side = gq.shape
    window = gk.shape[0]
    back = window - own
    dt = nrm_t.shape[0] // side
    head = pl.ds(0, side)
    copies = load_all(
        [
            (part0_h, part0),
            (mask0_h, mask0),
            (k0t_h, k0t),
            (q0_h, q0),
            (gq_h.at[:, head], gq),
            (gk_h.at[:, head], gk),
            (nrm_h, nrm_t),
        ],
        lsem,
    )
    none = jnp.zeros((1, own), F32)
    suffix = jnp.concatenate([none, near_sums[0:1, : window - own]], axis=1)
    suffix = suffix + jnp.concatenate([none, none, far_sums[0:1, : window - 2 * own]], axis=1)
    column = jnp.broadcast_to(suffix, (side, window)).T
    column = jnp.concatenate([column] * (own // side), axis=1)
    for copy in copies[:-1]:
        copy.wait()
    gs = (part0[...] + select_scale * mask0[...].astype(F32) * column).astype(BF)
    dq = (mm(k0t[0:HD, :], gs) * 0.125).T
    dk = mm(gs, keep_half(q0[...], False)).astype(BF)
    gq_new = gq[...] + jnp.concatenate([dq, jnp.zeros_like(dq)], axis=1).astype(BF)
    gk_new = gk[...] + dk
    gq_out[...] = gq_new
    gk_out[...] = gk_new
    copies[-1].wait()
    g_q = mm(nrm_t[:, back:], gq_new).astype(BF)
    g_k = mm(nrm_t[...], gk_new).astype(BF)
    for which, g in ((0, g_q), (1, g_k)):
        for i in range(dt):
            stage[which * dt + i] = g[i * side : (i + 1) * side, :]
            send_tile(stage.at[which * dt + i], dst[i * 3 * dt + which * dt], sums, gsem)
    wait_tiles(stage, sums, gsem)


def pre_kernel(
    row_at, tok, small, gq_head, gk_head, gq_h, gk_h, gv_h, wqkv_h, far, near, mine, totals, gq, gk, gv, wqkv, lsem
):
    own, width = gq.shape
    window = gk.shape[0]
    side = gq_head.shape[1]
    rest = pl.ds(side, width - side)
    copies = load_all(
        [(wqkv_h, wqkv), (gk_h.at[:, rest], gk.at[:, rest]), (gv_h, gv), (gq_h.at[:, rest], gq.at[:, rest])], lsem
    )
    gq[:, 0:side] = gq_head[...]
    gk[:, 0:side] = gk_head[...]
    for copy in copies:
        copy.wait()
    total = jnp.zeros((1, width), F32)
    for b in range(window // own):
        rows = slice(b * own, (b + 1) * own)
        g = mm_nt(gk[rows, :], wqkv[:, width : 2 * width]) + mm_nt(gv[rows, :], wqkv[:, 2 * width :])
        if b == window // own - 1:
            g = g + mm_nt(gq[...], wqkv[:, :width])
            mine[...] = g
        elif b == 0:
            far[...] = g.astype(far.dtype)
        else:
            near[...] = g.astype(near.dtype)
        hat, _ = norm_parts(tok[rows, :].astype(F32))
        total = total + jnp.sum(g * hat, axis=0, keepdims=True)
    totals[...] = jnp.zeros_like(totals)
    spots = lax.broadcasted_iota(jnp.int32, (1, width), 1)
    placed = jnp.where(spots == row_at[0], small[1:2, :], 0.0)
    for index, line in enumerate((total, small[0:1, :], placed)):
        for i in range(width // side):
            at = index * (width // side) + i
            totals[at : at + 1, :] = line[:, i * side : (i + 1) * side]


def input_kernel(tok, gains, ghid, mine, near, far, out):
    hat, rate = norm_parts(tok[...].astype(F32))
    g = mine[...] + near[...].astype(F32) + far[...].astype(F32)
    scaled = g * gains[0:1, :]
    out[...] = ghid[...] + rate * (
        scaled
        - jnp.mean(scaled, axis=-1, keepdims=True)
        - hat * jnp.mean(scaled * hat, axis=-1, keepdims=True)
    )


def adam_kernel(correction, parts, *refs):
    grads, refs = refs[: 2 * len(parts)], refs[2 * len(parts) :]
    holds, first, second, left, right, weight, first_out, second_out, weight_out = refs
    slots = []
    for index, (at, size, _) in enumerate(parts):
        slots += [(at + k, grads[2 * index], grads[2 * index + 1], k) for k in range(size)]
    for low in range(0, len(slots), ADAM_GROUP):
        group = slots[low : low + ADAM_GROUP]
        rights, turned, steps, undone = {}, {}, {}, {}
        for slot, mine, other, k in group:
            grad = mine[k].astype(F32) + other[k].astype(F32)
            grad = jnp.where(holds[slot] > 0, grad, 0.0)
            rights[slot] = split(right[slot])
            turned[slot] = mm3(split(grad), rights[slot])
        for slot, *_ in group:
            turned[slot] = mm3(split(left[slot].T), split(turned[slot]))
        for slot, *_ in group:
            t = turned[slot]
            first_new = first_decay * first[slot] + (1.0 - first_decay) * t
            second_new = second_decay * second[slot] + (1.0 - second_decay) * t * t
            first_out[slot] = first_new
            second_out[slot] = second_new
            steps[slot] = first_new / correction / (jnp.sqrt(second_new / correction) + adam_epsilon)
        for slot, *_ in group:
            undone[slot] = mm3_nt(split(steps[slot]), rights[slot])
        for slot, *_ in group:
            back = mm3(split(left[slot]), split(undone[slot]))
            w = weight[slot]
            weight_out[slot] = w - weight_rate * back - weight_rate * decay_rate * w


def after(x, earlier):
    return lax.optimization_barrier((x, earlier))[0]


def bit_plan(devices, per_device):
    bits = [1 << b for b in range(devices.bit_length() - 1)]
    first, rest = bits[0], bits[1:]
    if devices == 32:
        orders = [(2, 4, 8, 16), (4, 8, 2, 16), (8, 16, 2, 4)]
    else:
        orders = [tuple(rest[i:] + rest[:i]) for i in range(3)]
    if per_device < 4:
        sizes = [1] * per_device
    else:
        sizes = [per_device * 3 // 7, per_device * 5 // 14]
        sizes.append(per_device - sum(sizes))
    plan = []
    at = 0
    for size, order in zip(sizes, orders):
        if size:
            plan.append((at, size, order))
            at += size
    return first, plan


def gather_parts(devices, per_device):
    if devices != 32 or per_device < 8:
        return per_device, []
    size = per_device * 2 // 7
    first = per_device * 3 // 14
    return first, [
        (first, size, (16, 8, 4, 2, 1)),
        (first + size, size, (16, 8, 2, 4, 1)),
        (first + 2 * size, per_device - first - 2 * size, (4, 2, 16, 8, 1)),
    ]


def local(
    tokens,
    segment_ids,
    pad_lengths,
    threshold,
    gains,
    gain_first,
    gain_second,
    slot_tiles,
    weight_slots,
    first_moment,
    second_moment,
    basis_left,
    basis_right,
    out_grad,
):
    axes = ("dp", "seq")
    n_dp, n_seq = lax.axis_size("dp"), lax.axis_size("seq")
    devices = n_dp * n_seq
    me = lax.axis_index(axes)
    seq_at = lax.axis_index("seq")
    _, own, width = tokens.shape
    length = segment_ids.shape[1]
    side = weight_slots.shape[-1]
    per_device = weight_slots.shape[0]
    slot_total = slot_tiles.shape[0]
    dt = width // side
    tiles = (3 * dt * dt, dt * dt, dt * (FF // side), dt * (FF // side))
    tile_count = sum(tiles)
    back = SPAN
    window = back + own

    def swap(x, bit):
        return lax.ppermute(x, axes, [(i, i ^ bit) for i in range(devices)])

    slot_ids = jnp.arange(slot_total, dtype=jnp.int32)
    position = jnp.sum(
        jnp.where(slot_tiles[None, :] == slot_ids[:, None], slot_ids[None, :], 0), axis=1
    )
    owner = position // per_device
    inner = position % per_device
    apart = owner ^ me
    first_bit, plan = bit_plan(devices, per_device)
    half = slot_total // 2
    spread = devices // 2
    place = jnp.zeros_like(position)
    for at, size, order in plan:
        index = jnp.zeros_like(position)
        for bit in order:
            index = index * 2 + ((apart & bit) != 0).astype(jnp.int32)
        here = at * spread + index * size + (inner - at)
        place = jnp.where((inner >= at) & (inner < at + size), here, place)
    dst = place + jnp.where((apart & first_bit) != 0, half, 0)
    by_gather, gather_plan = gather_parts(devices, per_device)
    src = owner * by_gather + inner
    base = devices * by_gather
    for at, size, order in gather_plan:
        index = jnp.zeros_like(position)
        for bit in reversed(order):
            index = index * 2 + ((apart & bit) != 0).astype(jnp.int32)
        here = base + index * size + (inner - at)
        src = jnp.where((inner >= at) & (inner < at + size), here, src)
        base += devices * size

    mine_tok = tokens[0]
    seen = []
    for step in range(back // own, 0, -1):
        seen.append(lax.ppermute(mine_tok, "seq", [(i, i + step) for i in range(n_seq - step)]))
    tok = jnp.concatenate(seen + [mine_tok], axis=0)
    start = seq_at * own
    seg_window = lax.dynamic_slice_in_dim(
        jnp.concatenate([jnp.full((back,), -1, jnp.int32), segment_ids[0]]), start, window
    )
    valid_len = length - pad_lengths[0]
    scal = jnp.stack([valid_len, start, (seq_at == n_seq - 1).astype(jnp.int32)])

    segc, segr = seg_window[:, None], seg_window[None, :]

    rounded = weight_slots.astype(BF)
    pieces = [lax.all_gather(rounded[:by_gather], axes, axis=0, tiled=True)]
    held = [rounded[at : at + size] for at, size, _ in gather_plan]
    for step in range(len(gather_plan[0][2]) - 2 if gather_plan else 0):
        held = [jnp.concatenate([h, swap(h, o[2][step])], axis=0) for h, o in zip(held, gather_plan)]
        if step == 1:
            held[0], tok, src, dst, scal, segc, segr = lax.optimization_barrier(
                (held[0], tok, src, dst, scal, segc, segr)
            )
    for h, (_, _, order) in zip(held, gather_plan):
        two = [h, swap(h, order[-2])]
        pieces += two + [swap(x, order[-1]) for x in two]
    sizes = [p.shape[0] for p in pieces]

    hbm = pl.BlockSpec(memory_space=pltpu.HBM)
    vm = pl.BlockSpec(memory_space=VMEM)
    sm = pl.BlockSpec(memory_space=SMEM)
    shp = jax.ShapeDtypeStruct
    first_rows = plan[0][1] * spread
    sums_shapes = [shp((n, side, side), BF) for n in (half, first_rows, half - first_rows)]
    per_chunk = 2 * (CHUNK // side) * dt
    outs = pl.pallas_call(
        functools.partial(layer_kernel, tiles, sizes),
        out_shape=(
            shp((own, width), BF),
            shp((own, width), F32),
            shp((own, width), BF),
            shp((window, width), BF),
            shp((window, width), BF),
            shp((width, window), BF),
            shp((width, 3 * width), BF),
            shp((own, side), BF),
            shp((side, window), BF),
            shp((window, own), F32),
            shp((window, own), BF),
            shp((8, window), F32),
            shp((8, width), F32),
            *sums_shapes,
        ),
        in_specs=[sm] * 4 + [vm] * 5 + [hbm] * len(sizes),
        out_specs=tuple([hbm] * 11 + [vm] * 2 + [hbm] * 3),
        scratch_shapes=[
            VMEM((own, width), BF),
            VMEM((own, width), F32),
            VMEM((own, width), BF),
            VMEM((window, width), BF),
            VMEM((window, width), BF),
            VMEM((width, window), BF),
            VMEM((width, 3 * width), BF),
            VMEM((window, own), F32),
            VMEM((window, own), BF),
            VMEM((slot_total, side, side), BF),
            VMEM((window, width), BF),
            VMEM((dt, own, side), BF),
            VMEM((back, side), BF),
            VMEM((dt, window, side), BF),
            VMEM((dt, window, side), BF),
            VMEM((dt, side, window), BF),
            VMEM((dt, side, window), BF),
            VMEM((window, own), F32),
            VMEM((window, own), F32),
            VMEM((H, window, own), BF),
            VMEM((width, own), F32),
            VMEM((own, width), BF),
            VMEM((width, own), BF),
            VMEM((width, width), BF),
            VMEM((own, width), F32),
            VMEM((own, width), F32),
            VMEM((own, width), BF),
            VMEM((width, own), BF),
            VMEM((own, width), F32),
            VMEM((own, width), F32),
            VMEM((dt, own, side), BF),
            VMEM((width, own), BF),
            VMEM((width, CHUNK), BF),
            VMEM((CHUNK, width), BF),
            VMEM((2, per_chunk, side, side), BF),
            VMEM((side, side), BF),
            pltpu.SemaphoreType.DMA((len(sizes),)),
            pltpu.SemaphoreType.DMA((2,)),
            pltpu.SemaphoreType.DMA,
            pltpu.SemaphoreType.DMA((11,)),
        ],
        compiler_params=pltpu.CompilerParams(vmem_limit_bytes=60 << 20),
        name="layer",
    )(
        src,
        dst,
        scal,
        threshold,
        tok,
        gains,
        out_grad[0],
        segc,
        segr,
        *pieces,
    )
    (output, ghid, gq, gk, gv, nrm_t, wqkv, q0, k0t, part0, mask0, colsum, small, *sums) = outs

    near_sums, far_sums = [
        lax.ppermute(colsum, "seq", [(i, i - step) for i in range(step, n_seq)]) for step in (1, 2)
    ]
    main_tiles = tiles[0] - 2 * dt
    sums = pl.pallas_call(
        qkv_kernel,
        out_shape=sums_shapes,
        in_specs=[sm] + [hbm] * 7,
        out_specs=[hbm] * 3,
        scratch_shapes=[
            VMEM((own, width), BF),
            VMEM((window, width), BF),
            VMEM((window, width), BF),
            VMEM((width, window), BF),
            VMEM((main_tiles, side, side), BF),
            pltpu.SemaphoreType.DMA((4,)),
            pltpu.SemaphoreType.DMA,
        ],
        input_output_aliases={5: 0, 6: 1, 7: 2},
        compiler_params=pltpu.CompilerParams(vmem_limit_bytes=60 << 20),
        cost_estimate=pl.CostEstimate(
            flops=2 * (2 * window + own) * width * width, bytes_accessed=8 << 20, transcendentals=0
        ),
        name="qkv_grad",
    )(dst, gq, gk, gv, nrm_t, *sums)
    gq_head, gk_head, stay, *aways = pl.pallas_call(
        head_kernel,
        out_shape=(shp((own, side), BF), shp((window, side), BF), *sums_shapes),
        in_specs=[sm, vm, vm] + [hbm] * 10,
        out_specs=(vm, vm, hbm, hbm, hbm),
        scratch_shapes=[
            VMEM((window, own), F32),
            VMEM((window, own), BF),
            VMEM((own, side), BF),
            VMEM((side, window), BF),
            VMEM((own, side), BF),
            VMEM((window, side), BF),
            VMEM((width, window), BF),
            VMEM((2 * dt, side, side), BF),
            pltpu.SemaphoreType.DMA((7,)),
            pltpu.SemaphoreType.DMA,
        ],
        input_output_aliases={10: 2, 11: 3, 12: 4},
        compiler_params=pltpu.CompilerParams(vmem_limit_bytes=60 << 20),
        cost_estimate=pl.CostEstimate(flops=1 << 30, bytes_accessed=4 << 20, transcendentals=0),
        name="head_grad",
    )(dst, near_sums, far_sums, part0, mask0, q0, k0t, gq, gk, nrm_t, *sums)

    def plus(a, b):
        return (a.astype(F32) + b.astype(F32)).astype(BF)

    got = [swap(aways[0], first_bit)]
    aways[1] = after(aways[1], got[0])
    got.append(swap(aways[1], first_bit))
    steps = len(plan[0][2])

    def from_got(which, low, high):
        at, size, _ = plan[which]
        start = at * spread
        source, base = (got[0], 0) if which == 0 else (got[1], first_rows)
        rows = slice(start + low * size * spread // 2, start + high * size * spread // 2)
        return plus(stay[rows], source[rows.start - base : rows.stop - base])

    sent = [from_got(0, 1, 2)]
    for which in range(1, len(plan)):
        got[1] = after(got[1], sent[-1])
        sent.append(from_got(which, 1, 2))
    came = [swap(piece, order[0]) for piece, (_, _, order) in zip(sent, plan)]
    left = [from_got(which, 0, 1) for which in range(len(plan))]
    gq_head = after(gq_head, sent[-1])
    row_at = lax.axis_index("dp")
    far, near, mine, totals = pl.pallas_call(
        pre_kernel,
        out_shape=(
            shp((own, width), BF),
            shp((own, width), BF),
            shp((own, width), F32),
            shp((side // 2, side), F32),
        ),
        in_specs=[sm] + [vm] * 4 + [hbm] * 4,
        out_specs=tuple([vm] * 4),
        scratch_shapes=[
            VMEM((own, width), BF),
            VMEM((window, width), BF),
            VMEM((window, width), BF),
            VMEM((width, 3 * width), BF),
            pltpu.SemaphoreType.DMA((4,)),
        ],
        compiler_params=pltpu.CompilerParams(vmem_limit_bytes=30 << 20),
        cost_estimate=pl.CostEstimate(
            flops=2 * (2 * window + own) * width * width, bytes_accessed=10 << 20, transcendentals=0
        ),
        name="pre_grad",
    )(row_at[None], tok, small, gq_head, gk_head, gq, gk, gv, wqkv)
    gathered = lax.all_gather(totals, axes)
    last = (sent[-1], totals)
    for step in range(1, steps):
        for which in reversed(range(len(plan))):
            order = plan[which][2]
            came[which] = after(came[which], last)
            middle = left[which].shape[0] // 2
            piece = plus(left[which][middle:], came[which][middle:])
            rest = plus(left[which][:middle], came[which][:middle])
            if which == 1 and step == steps - 1:
                far, near = after(far, piece), after(near, piece)
                far = lax.ppermute(far, "seq", [(i, i - 2) for i in range(2, n_seq)])
                near = lax.ppermute(near, "seq", [(i, i - 1) for i in range(1, n_seq)])
            if which == 0 and step == steps - 1:
                far, near, mine = after(far, piece), after(near, piece), after(mine, piece)
                rest, gathered = lax.optimization_barrier((rest, gathered))
            came[which] = swap(piece, order[step])
            left[which] = rest
            last = piece
    pairs = list(zip(left, came))
    totals = jnp.sum(gathered[:, : 3 * dt], axis=0).reshape(3, width)
    correction = 1.0 - first_decay**STEP
    holds = lax.dynamic_slice_in_dim((slot_tiles < tile_count).astype(jnp.int32), me * per_device, per_device)
    moment_first, moment_second, new_weights = pl.pallas_call(
        functools.partial(adam_kernel, correction, plan),
        out_shape=tuple([shp(weight_slots.shape, F32)] * 3),
        in_specs=[vm] * (2 * len(plan)) + [sm] + [vm] * 5,
        out_specs=tuple([vm] * 3),
        compiler_params=pltpu.CompilerParams(vmem_limit_bytes=30 << 20),
        name="adam",
    )(*[x for pair in pairs for x in pair], holds, first_moment, second_moment, basis_left, basis_right, weight_slots)
    input_grad = pl.pallas_call(
        input_kernel,
        out_shape=shp((own, width), F32),
        in_specs=[vm] * 6,
        out_specs=vm,
        compiler_params=pltpu.CompilerParams(vmem_limit_bytes=20 << 20),
        name="input_grad",
    )(mine_tok, gains, ghid, mine, near, far)

    gain_total = totals[:2]
    fraction = lax.dynamic_slice_in_dim(totals[2], row_at, 1)

    gain_moment = first_decay * gain_first + (1.0 - first_decay) * gain_total
    gain_square = second_decay * gain_second + (1.0 - second_decay) * gain_total * gain_total
    gain_update = gains - gain_rate * (gain_moment / correction) / (
        jnp.sqrt(gain_square / correction) + adam_epsilon
    )
    return (
        output[None],
        input_grad[None],
        fraction,
        moment_first,
        moment_second,
        new_weights,
        gain_update,
        gain_moment,
        gain_square,
    )


def solution(mesh):
    in_specs = (
        P("dp", "seq", None),
        P("dp", None),
        P("dp"),
        P(),
        P(),
        P(),
        P(),
        P(),
        P(("dp", "seq"), None, None),
        P(("dp", "seq"), None, None),
        P(("dp", "seq"), None, None),
        P(("dp", "seq"), None, None),
        P(("dp", "seq"), None, None),
        P("dp", "seq", None),
    )
    out_specs = (
        P("dp", "seq", None),
        P("dp", "seq", None),
        P("dp"),
        P(("dp", "seq"), None, None),
        P(("dp", "seq"), None, None),
        P(("dp", "seq"), None, None),
        P(),
        P(),
        P(),
    )
    return jax.shard_map(local, mesh=mesh, in_specs=in_specs, out_specs=out_specs, check_vma=False)
```

```python
import functools

import jax
import jax.numpy as jnp
from jax import lax
from jax.experimental import pallas as pl
from jax.experimental.pallas import tpu as pltpu
from jax.sharding import PartitionSpec as P

H = 12
HD = 64
FF = 3072
STEP = 3
SPAN = 512
CHUNK = 768
ADAM_GROUP = 7

select_scale = 0.2
fraction_slope = 2.0
first_decay = 0.5
second_decay = 0.5
adam_epsilon = 1e-08
weight_rate = 0.05
gain_rate = 0.2
decay_rate = 0.1
norm_epsilon = 1e-05

BF = jnp.bfloat16
F32 = jnp.float32
VMEM = pltpu.VMEM
SMEM = pltpu.SMEM


def mm(a, b):
    return lax.dot_general(a, b, (((1,), (0,)), ((), ())), preferred_element_type=F32)


def mm_nt(a, b):
    return lax.dot_general(a, b, (((1,), (1,)), ((), ())), preferred_element_type=F32)


def split(x):
    high = x.astype(BF)
    return high, (x - high.astype(F32)).astype(BF)


def mm_split(x, exact):
    high, rest = split(x)
    return mm(high, exact) + mm(rest, exact)


def lane_half(shape, second):
    lane = lax.broadcasted_iota(jnp.int32, shape, 1)
    return (lane >= HD) if second else (lane < HD)


def keep_half(x, second):
    return jnp.where(lane_half(x.shape, second), x, jnp.zeros_like(x))


def norm_parts(x):
    centred = x - jnp.mean(x, axis=-1, keepdims=True)
    rate = lax.rsqrt(jnp.mean(centred * centred, axis=-1, keepdims=True) + norm_epsilon)
    return centred * rate, rate


def send_tile(tile_ref, dst, sums, sem):
    low = 0
    for buffer in sums:
        high = low + buffer.shape[0]

        @pl.when((dst >= low) & (dst < high))
        def _(buffer=buffer, low=low):
            pltpu.make_async_copy(tile_ref, buffer.at[dst - low], sem).start()

        low = high


def wait_tiles(stage_ref, sums, sem):
    pltpu.make_async_copy(stage_ref, sums[0].at[pl.ds(0, stage_ref.shape[0])], sem).wait()


def mm3(a, b):
    (ah, al), (bh, bl) = a, b
    return mm(jnp.concatenate([ah, ah, al], axis=1), jnp.concatenate([bh, bl, bh], axis=0))


def mm3_nt(a, b):
    (ah, al), (bh, bl) = a, b
    return mm_nt(jnp.concatenate([ah, ah, al], axis=1), jnp.concatenate([bh, bl, bh], axis=1))


def layer_kernel(tiles, sizes, *refs):
    (src, dst, scal, thr, tok, gains, dy, segc, segr), refs = refs[:9], refs[9:]
    w_parts, refs = refs[: len(sizes)], refs[len(sizes) :]
    (out_h, ghid_h, gq_h, gk_h, gv_h, nrm_t_h, wqkv_h, q0_h, k0t_h, part0_h, mask0_h, colsum, small, *sums), refs = (
        refs[:16],
        refs[16:],
    )
    (out, ghid, gq, gk, gv, nrm_t, wqkv, part0, mask0), refs = refs[:9], refs[9:]
    (wall, nrm, q_s, q_e, k_s, v_s, kt_s, vt_s, bias, gsh, probs, mixt, mixb, mixbt, wout, hid, xhat), refs = (
        refs[:17],
        refs[17:],
    )
    nm, nmt, acc, gmid, g_s, gt_s, wu, wd, stage, zero, wsem, gsem, zsem, osem = refs

    writes = []

    def write(ref, target):
        copy = pltpu.make_async_copy(ref, target, osem.at[len(writes)])
        copy.start()
        writes.append(copy)

    n_qkv, n_out, n_up, n_down = tiles
    width = tok.shape[1]
    own = dy.shape[0]
    window = tok.shape[0]
    back = window - own
    side = wall.shape[-1]
    dt = width // side
    pairs = width // side
    total_slots = 2 * sums[0].shape[0]
    loads = []
    at = 0
    for index, (part, size) in enumerate(zip(w_parts, sizes)):
        loads.append(pltpu.make_async_copy(part, wall.at[pl.ds(at, size)], wsem.at[index]))
        loads[-1].start()
        at += size
    zero[...] = jnp.zeros_like(zero)
    tile_count = n_qkv + n_out + n_up + n_down
    empty = total_slots - tile_count

    @pl.loop(0, empty)
    def _(e):
        send_tile(zero, dst[tile_count + e], sums, zsem)

    gain_pre = gains[0:1, :]
    gain_mid = gains[1:2, :]

    @pl.loop(0, window // own)
    def _(b):
        rows = pl.ds(pl.multiple_of(b * own, own), own)
        hat, _ = norm_parts(tok[rows, :].astype(F32))
        value = (hat * gain_pre).astype(BF)
        nrm[rows, :] = value
        nrm_t[:, rows] = value.T

    write(nrm_t, nrm_t_h)
    for load in loads:
        load.wait()
    per_row = 3 * dt

    @pl.loop(0, 3 * dt // 2)
    def _(j):
        for i in range(dt):
            for jj in range(2):
                wqkv[i * side : (i + 1) * side, pl.ds(pl.multiple_of((2 * j + jj) * side, side), side)] = wall[
                    src[i * per_row + 2 * j + jj]
                ]

    write(wqkv, wqkv_h)
    for i in range(dt):
        for j in range(dt):
            wout[i * side : (i + 1) * side, j * side : (j + 1) * side] = wall[src[n_qkv + i * dt + j]]

    @pl.loop(0, dt // 2, unroll=True)
    def _(j):
        cols = pl.ds(pl.multiple_of(2 * j * side, 2 * side), 2 * side)
        got = (mm(nrm[back:, :], wqkv[:, cols]) * 0.125).astype(BF)
        q_s[2 * j] = got[:, :side]
        q_s[2 * j + 1] = got[:, side:]

    q_e[...] = (mm(nrm[:back, :], wqkv[:, 0:side]) * 0.125).astype(BF)

    @pl.loop(0, dt // 2, unroll=True)
    def _(j):
        cols = pl.ds(pl.multiple_of(width + 2 * j * side, 2 * side), 2 * side)
        got = mm(nrm[...], wqkv[:, cols]).astype(BF)
        got_t = got.T
        k_s[2 * j] = got[:, :side]
        k_s[2 * j + 1] = got[:, side:]
        kt_s[2 * j] = got_t[:side, :]
        kt_s[2 * j + 1] = got_t[side:, :]

    @pl.loop(0, dt // 2, unroll=True)
    def _(j):
        cols = pl.ds(pl.multiple_of(2 * width + 2 * j * side, 2 * side), 2 * side)
        got = mm(nrm[...], wqkv[:, cols]).astype(BF)
        got_t = got.T
        v_s[2 * j] = got[:, :side]
        v_s[2 * j + 1] = got[:, side:]
        vt_s[2 * j] = got_t[:side, :]
        vt_s[2 * j + 1] = got_t[side:, :]

    write(q_s.at[0], q0_h)
    write(kt_s.at[0], k0t_h)

    valid_len = scal[0]
    start = scal[1]
    is_last = scal[2]
    key_at = lax.broadcasted_iota(jnp.int32, (window, own), 0)
    query_at = lax.broadcasted_iota(jnp.int32, (window, own), 1)
    key_valid = (key_at + (start - back)) < valid_len
    key_seg = segc[...]
    k_first = k_s[0]

    def selected(q_rows, first):
        s = mm_nt(k_first, keep_half(q_rows, False))
        same = key_seg == segr[:, first : first + own]
        strict = same & key_valid & (key_at < query_at + first)
        return s, same, jnp.where(strict, select_scale * jnp.maximum(s, 0.0), 0.0), strict

    prefix = jnp.zeros((window, 1), F32)
    for b in range(back // own):
        _, _, chosen, _ = selected(q_e[b * own : (b + 1) * own, :], b * own)
        prefix = prefix + jnp.sum(chosen, axis=1, keepdims=True)
    s_own, same, chosen, strict = selected(q_s[0], back)
    tri_row = lax.broadcasted_iota(jnp.int32, (own, own), 0)
    tri_col = lax.broadcasted_iota(jnp.int32, (own, own), 1)
    earlier = jnp.where(tri_row < tri_col, 1.0, 0.0).astype(BF)
    shadow = prefix + mm_split(chosen, earlier)
    allowed = strict | (same & (key_at == query_at + back))
    bias[...] = jnp.where(allowed, -shadow, -1e30)
    mask0[...] = jnp.where(strict & (s_own > 0.0), 1.0, 0.0).astype(BF)
    write(mask0, mask0_h)
    column_total = prefix + jnp.sum(chosen, axis=1, keepdims=True)
    key_col = lax.broadcasted_iota(jnp.int32, (window, 1), 0)
    key_pos = key_col + (start - back)
    counts = (key_pos >= 0) & (key_pos < valid_len) & ((key_col < own) | (is_last > 0))
    soft = 1.0 / (1.0 + jnp.exp(-fraction_slope * (column_total - thr[0])))
    counted = jnp.sum(jnp.where(counts, soft, 0.0), axis=0, keepdims=True)
    small[...] = jnp.zeros_like(small)
    small[1:2, :] = jnp.broadcast_to(counted / valid_len.astype(F32), (1, width))

    @pl.loop(0, pairs, unroll=2)
    def _(p):
        q2 = q_s[p]
        k2 = k_s[p]
        both = [mm_nt(k2, keep_half(q2, hh == 1)) for hh in range(2)]
        prs = []
        for hh in range(2):
            s = both[hh] + bias[...]
            e = jnp.exp(s - jnp.max(s, axis=0, keepdims=True))
            prs.append((e * (1.0 / jnp.sum(e, axis=0, keepdims=True))).astype(BF))
        for hh in range(2):
            probs[2 * p + hh] = prs[hh]
        mixed = [mm(vt_s[p, hh * HD : (hh + 1) * HD, :], prs[hh]) for hh in range(2)]
        mixt[pl.ds(pl.multiple_of(p * side, side), side), :] = jnp.concatenate(mixed, axis=0)

    mixbt[...] = mixt[...].astype(BF)
    mixb[...] = mixbt[...].T
    hid[...] = tok[back:, :].astype(F32) + mm(mixb[...], wout[...])
    hat, rate = norm_parts(hid[...])
    xhat[...] = hat
    nm[...] = (hat * gain_mid).astype(BF)
    nmt[...] = nm[...].T

    acc[...] = jnp.zeros_like(acc)
    gmid[...] = jnp.zeros_like(gmid)
    cw = CHUNK // side
    f_tiles = FF // side
    per_chunk = 2 * cw * dt
    chunks = FF // CHUNK

    @pl.loop(0, chunks)
    def _(c):
        slot = lax.rem(c, 2)
        for i in range(dt):
            for jj in range(cw):
                wu[i * side : (i + 1) * side, jj * side : (jj + 1) * side] = wall[
                    src[n_qkv + n_out + i * f_tiles + cw * c + jj]
                ]
        for ii in range(cw):
            for j in range(dt):
                wd[ii * side : (ii + 1) * side, j * side : (j + 1) * side] = wall[
                    src[n_qkv + n_out + n_up + (cw * c + ii) * dt + j]
                ]
        up = mm(nm[...], wu[...])
        cube = 0.7978845608028654 * (up + 0.044715 * up * up * up)
        th = jnp.tanh(cube)
        active = (0.5 * up * (1.0 + th)).astype(BF)
        slope = 0.5 * (1.0 + th) + 0.5 * up * (1.0 - th * th) * (
            0.7978845608028654 * (1.0 + 3.0 * 0.044715 * up * up)
        )
        acc[...] += mm(active, wd[...])
        gu = (mm_nt(dy[...], wd[...]) * slope).astype(BF)
        gmid[...] += mm_nt(gu, wu[...])

        @pl.when(c >= 2)
        def _():
            wait_tiles(stage.at[slot], sums, gsem.at[slot])

        g_down = mm(active.T, dy[...]).astype(BF)
        for ii in range(cw):
            for j in range(dt):
                at = ii * dt + j
                stage[slot, at] = g_down[ii * side : (ii + 1) * side, j * side : (j + 1) * side]
        g_up = mm(nmt[...], gu).astype(BF)
        for i in range(dt):
            for jj in range(cw):
                at = cw * dt + i * cw + jj
                stage[slot, at] = g_up[i * side : (i + 1) * side, jj * side : (jj + 1) * side]
        for ii in range(cw):
            for j in range(dt):
                at = ii * dt + j
                t = n_qkv + n_out + n_up + (cw * c + ii) * dt + j
                send_tile(stage.at[slot, at], dst[t], sums, gsem.at[slot])
        for i in range(dt):
            for jj in range(cw):
                at = cw * dt + i * cw + jj
                t = n_qkv + n_out + i * f_tiles + cw * c + jj
                send_tile(stage.at[slot, at], dst[t], sums, gsem.at[slot])

    out[...] = (hid[...] + acc[...]).astype(BF)
    write(out, out_h)
    hat = xhat[...]
    gm = gmid[...]
    small[0:1, :] = jnp.sum(gm * hat, axis=0, keepdims=True)
    scaled = gm * gain_mid
    gh = dy[...].astype(F32) + rate * (
        scaled
        - jnp.mean(scaled, axis=-1, keepdims=True)
        - hat * jnp.mean(scaled * hat, axis=-1, keepdims=True)
    )
    ghid[...] = gh
    write(ghid, ghid_h)
    gb = gh.astype(BF)
    gmix = mm_nt(gb, wout[...]).astype(BF)
    for p in range(pairs):
        g_s[p] = gmix[:, p * side : (p + 1) * side]
    gt_s[...] = gmix.T

    for slot in range(2):
        wait_tiles(stage.at[slot], sums, gsem.at[slot])
    half_out = dt // 2
    for part in range(2):
        g_out = mm(mixbt[part * half_out * side : (part + 1) * half_out * side, :], gb).astype(BF)
        for i in range(half_out):
            for j in range(dt):
                stage[part, i * dt + j] = g_out[i * side : (i + 1) * side, j * side : (j + 1) * side]
        for i in range(half_out):
            for j in range(dt):
                t = n_qkv + (part * half_out + i) * dt + j
                send_tile(stage.at[part, i * dt + j], dst[t], sums, gsem.at[part])

    gsh[...] = jnp.zeros_like(gsh)

    @pl.loop(0, pairs)
    def _(p):
        g2 = g_s[p]
        q2 = q_s[p]
        v2 = v_s[p]
        later = jnp.where(p > 0, 1.0, 0.0)
        halves = [keep_half(g2, hh == 1) for hh in range(2)]
        dps = [mm_nt(v2, halves[hh]) for hh in range(2)]
        prs = [probs[2 * p + hh] for hh in range(2)]
        rows = pl.ds(pl.multiple_of(p * side, side), side)
        product = gt_s[rows, :].astype(F32) * mixt[rows, :]
        dls = []
        for hh in range(2):
            delta = jnp.sum(product[hh * HD : (hh + 1) * HD, :], axis=0, keepdims=True)
            dls.append(prs[hh].astype(F32) * (dps[hh] - delta))
        gsh[...] += dls[0] + dls[1]

        @pl.when(p == 0)
        def _():
            part0[...] = dls[0]

        gs = [(dls[0] * later).astype(BF), dls[1].astype(BF)]
        dv = mm(prs[0], halves[0]) + mm(prs[1], halves[1])
        dk = mm(gs[0], keep_half(q2, False)) + mm(gs[1], keep_half(q2, True))
        dqs = [mm(kt_s[p, hh * HD : (hh + 1) * HD, :], gs[hh]) for hh in range(2)]
        cols = pl.ds(pl.multiple_of(p * side, side), side)
        gq[:, cols] = (jnp.concatenate(dqs, axis=0) * 0.125).T.astype(BF)
        gk[:, cols] = dk.astype(BF)
        gv[:, cols] = dv.astype(BF)

    write(gq, gq_h)
    write(gk, gk_h)
    write(gv, gv_h)
    ones = jnp.ones((8, own), BF)
    high, rest = split(-gsh[...])
    colsum[...] = mm_nt(ones, high) + mm_nt(ones, rest)
    after = jnp.where(tri_row > tri_col, 1.0, 0.0).astype(BF)
    part0[...] += select_scale * mask0[...].astype(F32) * (mm(high, after) + mm(rest, after))
    write(part0, part0_h)

    for part in range(2):
        wait_tiles(stage.at[part, pl.ds(0, half_out * dt)], sums, gsem.at[part])
    pltpu.make_async_copy(sums[0].at[pl.ds(0, empty)], sums[0].at[pl.ds(0, empty)], zsem).wait()
    for copy in writes:
        copy.wait()


def load_all(pairs, sem):
    copies = [pltpu.make_async_copy(a, b, sem.at[i]) for i, (a, b) in enumerate(pairs)]
    for copy in copies:
        copy.start()
    return copies


def qkv_kernel(dst, gq_h, gk_h, gv_h, nrm_h, *refs):
    sums = refs[3:6]
    gq, gk, gv, nrm_t, stage, lsem, gsem = refs[6:]
    own, width = gq.shape
    side = stage.shape[-1]
    dt = width // side
    back = gk.shape[0] - own
    copies = load_all([(nrm_h, nrm_t), (gv_h, gv), (gk_h, gk), (gq_h, gq)], lsem)
    copies[0].wait()
    count = 0
    for which, copy in ((2, copies[1]), (1, copies[2]), (0, copies[3])):
        copy.wait()
        bounds = [(c, c + 2) for c in range(0, dt, 2)] if which == 2 else [(1, 2)] + [(c, c + 2) for c in range(2, dt, 2)]
        for lo, hi in bounds:
            cols = slice(lo * side, hi * side)
            if which == 0:
                g = mm(nrm_t[:, back:], gq[:, cols])
            else:
                g = mm(nrm_t[...], (gk if which == 1 else gv)[:, cols])
            g = g.astype(BF)
            for i in range(dt):
                for j in range(lo, hi):
                    stage[count] = g[i * side : (i + 1) * side, (j - lo) * side : (j - lo + 1) * side]
                    send_tile(stage.at[count], dst[i * 3 * dt + which * dt + j], sums, gsem)
                    count += 1
    wait_tiles(stage, sums, gsem)


def head_kernel(dst, near_sums, far_sums, part0_h, mask0_h, q0_h, k0t_h, gq_h, gk_h, nrm_h, *refs):
    gq_out, gk_out = refs[3:5]
    sums = refs[5:8]
    part0, mask0, q0, k0t, gq, gk, nrm_t, stage, lsem, gsem = refs[8:]
    own, side = gq.shape
    window = gk.shape[0]
    back = window - own
    dt = nrm_t.shape[0] // side
    head = pl.ds(0, side)
    copies = load_all(
        [
            (part0_h, part0),
            (mask0_h, mask0),
            (k0t_h, k0t),
            (q0_h, q0),
            (gq_h.at[:, head], gq),
            (gk_h.at[:, head], gk),
            (nrm_h, nrm_t),
        ],
        lsem,
    )
    none = jnp.zeros((1, own), F32)
    suffix = jnp.concatenate([none, near_sums[0:1, : window - own]], axis=1)
    suffix = suffix + jnp.concatenate([none, none, far_sums[0:1, : window - 2 * own]], axis=1)
    column = jnp.broadcast_to(suffix, (side, window)).T
    column = jnp.concatenate([column] * (own // side), axis=1)
    for copy in copies[:-1]:
        copy.wait()
    gs = (part0[...] + select_scale * mask0[...].astype(F32) * column).astype(BF)
    dq = (mm(k0t[0:HD, :], gs) * 0.125).T
    dk = mm(gs, keep_half(q0[...], False)).astype(BF)
    gq_new = gq[...] + jnp.concatenate([dq, jnp.zeros_like(dq)], axis=1).astype(BF)
    gk_new = gk[...] + dk
    gq_out[...] = gq_new
    gk_out[...] = gk_new
    copies[-1].wait()
    g_q = mm(nrm_t[:, back:], gq_new).astype(BF)
    g_k = mm(nrm_t[...], gk_new).astype(BF)
    for which, g in ((0, g_q), (1, g_k)):
        for i in range(dt):
            stage[which * dt + i] = g[i * side : (i + 1) * side, :]
            send_tile(stage.at[which * dt + i], dst[i * 3 * dt + which * dt], sums, gsem)
    wait_tiles(stage, sums, gsem)


def pre_kernel(
    row_at, tok, small, gq_head, gk_head, gq_h, gk_h, gv_h, wqkv_h, far, near, mine, totals, gq, gk, gv, wqkv, lsem
):
    own, width = gq.shape
    window = gk.shape[0]
    side = gq_head.shape[1]
    rest = pl.ds(side, width - side)
    copies = load_all(
        [(wqkv_h, wqkv), (gk_h.at[:, rest], gk.at[:, rest]), (gv_h, gv), (gq_h.at[:, rest], gq.at[:, rest])], lsem
    )
    gq[:, 0:side] = gq_head[...]
    gk[:, 0:side] = gk_head[...]
    for copy in copies:
        copy.wait()
    total = jnp.zeros((1, width), F32)
    for b in range(window // own):
        rows = slice(b * own, (b + 1) * own)
        g = mm_nt(gk[rows, :], wqkv[:, width : 2 * width]) + mm_nt(gv[rows, :], wqkv[:, 2 * width :])
        if b == window // own - 1:
            g = g + mm_nt(gq[...], wqkv[:, :width])
            mine[...] = g
        elif b == 0:
            far[...] = g.astype(far.dtype)
        else:
            near[...] = g.astype(near.dtype)
        hat, _ = norm_parts(tok[rows, :].astype(F32))
        total = total + jnp.sum(g * hat, axis=0, keepdims=True)
    totals[...] = jnp.zeros_like(totals)
    spots = lax.broadcasted_iota(jnp.int32, (1, width), 1)
    placed = jnp.where(spots == row_at[0], small[1:2, :], 0.0)
    for index, line in enumerate((total, small[0:1, :], placed)):
        for i in range(width // side):
            at = index * (width // side) + i
            totals[at : at + 1, :] = line[:, i * side : (i + 1) * side]


def input_kernel(tok, gains, ghid, mine, near, far, out):
    hat, rate = norm_parts(tok[...].astype(F32))
    g = mine[...] + near[...].astype(F32) + far[...].astype(F32)
    scaled = g * gains[0:1, :]
    out[...] = ghid[...] + rate * (
        scaled
        - jnp.mean(scaled, axis=-1, keepdims=True)
        - hat * jnp.mean(scaled * hat, axis=-1, keepdims=True)
    )


def adam_kernel(correction, parts, *refs):
    grads, refs = refs[: 2 * len(parts)], refs[2 * len(parts) :]
    holds, first, second, left, right, weight, first_out, second_out, weight_out = refs
    slots = []
    for index, (at, size, _) in enumerate(parts):
        slots += [(at + k, grads[2 * index], grads[2 * index + 1], k) for k in range(size)]
    for low in range(0, len(slots), ADAM_GROUP):
        group = slots[low : low + ADAM_GROUP]
        rights, turned, steps, undone = {}, {}, {}, {}
        for slot, mine, other, k in group:
            grad = mine[k].astype(F32) + other[k].astype(F32)
            grad = jnp.where(holds[slot] > 0, grad, 0.0)
            rights[slot] = split(right[slot])
            turned[slot] = mm3(split(grad), rights[slot])
        for slot, *_ in group:
            turned[slot] = mm3(split(left[slot].T), split(turned[slot]))
        for slot, *_ in group:
            t = turned[slot]
            first_new = first_decay * first[slot] + (1.0 - first_decay) * t
            second_new = second_decay * second[slot] + (1.0 - second_decay) * t * t
            first_out[slot] = first_new
            second_out[slot] = second_new
            steps[slot] = first_new / correction / (jnp.sqrt(second_new / correction) + adam_epsilon)
        for slot, *_ in group:
            undone[slot] = mm3_nt(split(steps[slot]), rights[slot])
        for slot, *_ in group:
            back = mm3(split(left[slot]), split(undone[slot]))
            w = weight[slot]
            weight_out[slot] = w - weight_rate * back - weight_rate * decay_rate * w


def after(x, earlier):
    return lax.optimization_barrier((x, earlier))[0]


def bit_plan(devices, per_device):
    bits = [1 << b for b in range(devices.bit_length() - 1)]
    first, rest = bits[0], bits[1:]
    if devices == 32:
        orders = [(2, 4, 8, 16), (4, 8, 2, 16), (8, 16, 2, 4)]
    else:
        orders = [tuple(rest[i:] + rest[:i]) for i in range(3)]
    if per_device < 4:
        sizes = [1] * per_device
    else:
        sizes = [per_device * 3 // 7, per_device * 5 // 14]
        sizes.append(per_device - sum(sizes))
    plan = []
    at = 0
    for size, order in zip(sizes, orders):
        if size:
            plan.append((at, size, order))
            at += size
    return first, plan


def gather_parts(devices, per_device):
    if devices != 32 or per_device < 8:
        return per_device, []
    size = per_device * 2 // 7
    first = per_device * 3 // 14
    return first, [
        (first, size, (16, 8, 4, 2, 1)),
        (first + size, size, (16, 8, 2, 4, 1)),
        (first + 2 * size, per_device - first - 2 * size, (4, 2, 16, 8, 1)),
    ]


def local(
    tokens,
    segment_ids,
    pad_lengths,
    threshold,
    gains,
    gain_first,
    gain_second,
    slot_tiles,
    weight_slots,
    first_moment,
    second_moment,
    basis_left,
    basis_right,
    out_grad,
):
    axes = ("dp", "seq")
    n_dp, n_seq = lax.axis_size("dp"), lax.axis_size("seq")
    devices = n_dp * n_seq
    me = lax.axis_index(axes)
    seq_at = lax.axis_index("seq")
    _, own, width = tokens.shape
    length = segment_ids.shape[1]
    side = weight_slots.shape[-1]
    per_device = weight_slots.shape[0]
    slot_total = slot_tiles.shape[0]
    dt = width // side
    tiles = (3 * dt * dt, dt * dt, dt * (FF // side), dt * (FF // side))
    tile_count = sum(tiles)
    back = SPAN
    window = back + own

    def swap(x, bit):
        return lax.ppermute(x, axes, [(i, i ^ bit) for i in range(devices)])

    slot_ids = jnp.arange(slot_total, dtype=jnp.int32)
    position = jnp.sum(
        jnp.where(slot_tiles[None, :] == slot_ids[:, None], slot_ids[None, :], 0), axis=1
    )
    owner = position // per_device
    inner = position % per_device
    apart = owner ^ me
    first_bit, plan = bit_plan(devices, per_device)
    half = slot_total // 2
    spread = devices // 2
    place = jnp.zeros_like(position)
    for at, size, order in plan:
        index = jnp.zeros_like(position)
        for bit in order:
            index = index * 2 + ((apart & bit) != 0).astype(jnp.int32)
        here = at * spread + index * size + (inner - at)
        place = jnp.where((inner >= at) & (inner < at + size), here, place)
    dst = place + jnp.where((apart & first_bit) != 0, half, 0)
    by_gather, gather_plan = gather_parts(devices, per_device)
    src = owner * by_gather + inner
    base = devices * by_gather
    for at, size, order in gather_plan:
        index = jnp.zeros_like(position)
        for bit in reversed(order):
            index = index * 2 + ((apart & bit) != 0).astype(jnp.int32)
        here = base + index * size + (inner - at)
        src = jnp.where((inner >= at) & (inner < at + size), here, src)
        base += devices * size

    mine_tok = tokens[0]
    seen = []
    for step in range(back // own, 0, -1):
        seen.append(lax.ppermute(mine_tok, "seq", [(i, i + step) for i in range(n_seq - step)]))
    tok = jnp.concatenate(seen + [mine_tok], axis=0)
    start = seq_at * own
    seg_window = lax.dynamic_slice_in_dim(
        jnp.concatenate([jnp.full((back,), -1, jnp.int32), segment_ids[0]]), start, window
    )
    valid_len = length - pad_lengths[0]
    scal = jnp.stack([valid_len, start, (seq_at == n_seq - 1).astype(jnp.int32)])

    segc, segr = seg_window[:, None], seg_window[None, :]

    rounded = weight_slots.astype(BF)
    pieces = [lax.all_gather(rounded[:by_gather], axes, axis=0, tiled=True)]
    held = [rounded[at : at + size] for at, size, _ in gather_plan]
    for step in range(len(gather_plan[0][2]) - 2 if gather_plan else 0):
        held = [jnp.concatenate([h, swap(h, o[2][step])], axis=0) for h, o in zip(held, gather_plan)]
        if step == 1:
            held[0], tok, src, dst, scal, segc, segr = lax.optimization_barrier(
                (held[0], tok, src, dst, scal, segc, segr)
            )
    for h, (_, _, order) in zip(held, gather_plan):
        two = [h, swap(h, order[-2])]
        pieces += two + [swap(x, order[-1]) for x in two]
    sizes = [p.shape[0] for p in pieces]

    hbm = pl.BlockSpec(memory_space=pltpu.HBM)
    vm = pl.BlockSpec(memory_space=VMEM)
    sm = pl.BlockSpec(memory_space=SMEM)
    shp = jax.ShapeDtypeStruct
    first_rows = plan[0][1] * spread
    sums_shapes = [shp((n, side, side), BF) for n in (half, first_rows, half - first_rows)]
    per_chunk = 2 * (CHUNK // side) * dt
    outs = pl.pallas_call(
        functools.partial(layer_kernel, tiles, sizes),
        out_shape=(
            shp((own, width), BF),
            shp((own, width), F32),
            shp((own, width), BF),
            shp((window, width), BF),
            shp((window, width), BF),
            shp((width, window), BF),
            shp((width, 3 * width), BF),
            shp((own, side), BF),
            shp((side, window), BF),
            shp((window, own), F32),
            shp((window, own), BF),
            shp((8, window), F32),
            shp((8, width), F32),
            *sums_shapes,
        ),
        in_specs=[sm] * 4 + [vm] * 5 + [hbm] * len(sizes),
        out_specs=tuple([hbm] * 11 + [vm] * 2 + [hbm] * 3),
        scratch_shapes=[
            VMEM((own, width), BF),
            VMEM((own, width), F32),
            VMEM((own, width), BF),
            VMEM((window, width), BF),
            VMEM((window, width), BF),
            VMEM((width, window), BF),
            VMEM((width, 3 * width), BF),
            VMEM((window, own), F32),
            VMEM((window, own), BF),
            VMEM((slot_total, side, side), BF),
            VMEM((window, width), BF),
            VMEM((dt, own, side), BF),
            VMEM((back, side), BF),
            VMEM((dt, window, side), BF),
            VMEM((dt, window, side), BF),
            VMEM((dt, side, window), BF),
            VMEM((dt, side, window), BF),
            VMEM((window, own), F32),
            VMEM((window, own), F32),
            VMEM((H, window, own), BF),
            VMEM((width, own), F32),
            VMEM((own, width), BF),
            VMEM((width, own), BF),
            VMEM((width, width), BF),
            VMEM((own, width), F32),
            VMEM((own, width), F32),
            VMEM((own, width), BF),
            VMEM((width, own), BF),
            VMEM((own, width), F32),
            VMEM((own, width), F32),
            VMEM((dt, own, side), BF),
            VMEM((width, own), BF),
            VMEM((width, CHUNK), BF),
            VMEM((CHUNK, width), BF),
            VMEM((2, per_chunk, side, side), BF),
            VMEM((side, side), BF),
            pltpu.SemaphoreType.DMA((len(sizes),)),
            pltpu.SemaphoreType.DMA((2,)),
            pltpu.SemaphoreType.DMA,
            pltpu.SemaphoreType.DMA((11,)),
        ],
        compiler_params=pltpu.CompilerParams(vmem_limit_bytes=60 << 20),
        name="layer",
    )(
        src,
        dst,
        scal,
        threshold,
        tok,
        gains,
        out_grad[0],
        segc,
        segr,
        *pieces,
    )
    (output, ghid, gq, gk, gv, nrm_t, wqkv, q0, k0t, part0, mask0, colsum, small, *sums) = outs

    near_sums, far_sums = [
        lax.ppermute(colsum, "seq", [(i, i - step) for i in range(step, n_seq)]) for step in (1, 2)
    ]
    main_tiles = tiles[0] - 2 * dt
    sums = pl.pallas_call(
        qkv_kernel,
        out_shape=sums_shapes,
        in_specs=[sm] + [hbm] * 7,
        out_specs=[hbm] * 3,
        scratch_shapes=[
            VMEM((own, width), BF),
            VMEM((window, width), BF),
            VMEM((window, width), BF),
            VMEM((width, window), BF),
            VMEM((main_tiles, side, side), BF),
            pltpu.SemaphoreType.DMA((4,)),
            pltpu.SemaphoreType.DMA,
        ],
        input_output_aliases={5: 0, 6: 1, 7: 2},
        compiler_params=pltpu.CompilerParams(vmem_limit_bytes=60 << 20),
        cost_estimate=pl.CostEstimate(
            flops=2 * (2 * window + own) * width * width, bytes_accessed=8 << 20, transcendentals=0
        ),
        name="qkv_grad",
    )(dst, gq, gk, gv, nrm_t, *sums)
    gq_head, gk_head, stay, *aways = pl.pallas_call(
        head_kernel,
        out_shape=(shp((own, side), BF), shp((window, side), BF), *sums_shapes),
        in_specs=[sm, vm, vm] + [hbm] * 10,
        out_specs=(vm, vm, hbm, hbm, hbm),
        scratch_shapes=[
            VMEM((window, own), F32),
            VMEM((window, own), BF),
            VMEM((own, side), BF),
            VMEM((side, window), BF),
            VMEM((own, side), BF),
            VMEM((window, side), BF),
            VMEM((width, window), BF),
            VMEM((2 * dt, side, side), BF),
            pltpu.SemaphoreType.DMA((7,)),
            pltpu.SemaphoreType.DMA,
        ],
        input_output_aliases={10: 2, 11: 3, 12: 4},
        compiler_params=pltpu.CompilerParams(vmem_limit_bytes=60 << 20),
        cost_estimate=pl.CostEstimate(flops=1 << 30, bytes_accessed=4 << 20, transcendentals=0),
        name="head_grad",
    )(dst, near_sums, far_sums, part0, mask0, q0, k0t, gq, gk, nrm_t, *sums)

    def plus(a, b):
        return (a.astype(F32) + b.astype(F32)).astype(BF)

    got = [swap(aways[0], first_bit)]
    aways[1] = after(aways[1], got[0])
    got.append(swap(aways[1], first_bit))
    steps = len(plan[0][2])

    def from_got(which, low, high):
        at, size, _ = plan[which]
        start = at * spread
        source, base = (got[0], 0) if which == 0 else (got[1], first_rows)
        rows = slice(start + low * size * spread // 2, start + high * size * spread // 2)
        return plus(stay[rows], source[rows.start - base : rows.stop - base])

    sent = [from_got(0, 1, 2)]
    for which in range(1, len(plan)):
        got[1] = after(got[1], sent[-1])
        sent.append(from_got(which, 1, 2))
    came = [swap(piece, order[0]) for piece, (_, _, order) in zip(sent, plan)]
    left = [from_got(which, 0, 1) for which in range(len(plan))]
    gq_head = after(gq_head, sent[-1])
    row_at = lax.axis_index("dp")
    far, near, mine, totals = pl.pallas_call(
        pre_kernel,
        out_shape=(
            shp((own, width), BF),
            shp((own, width), BF),
            shp((own, width), F32),
            shp((side // 2, side), F32),
        ),
        in_specs=[sm] + [vm] * 4 + [hbm] * 4,
        out_specs=tuple([vm] * 4),
        scratch_shapes=[
            VMEM((own, width), BF),
            VMEM((window, width), BF),
            VMEM((window, width), BF),
            VMEM((width, 3 * width), BF),
            pltpu.SemaphoreType.DMA((4,)),
        ],
        compiler_params=pltpu.CompilerParams(vmem_limit_bytes=30 << 20),
        cost_estimate=pl.CostEstimate(
            flops=2 * (2 * window + own) * width * width, bytes_accessed=10 << 20, transcendentals=0
        ),
        name="pre_grad",
    )(row_at[None], tok, small, gq_head, gk_head, gq, gk, gv, wqkv)
    gathered = lax.all_gather(totals, axes)
    last = (sent[-1], totals)
    for step in range(1, steps):
        for which in reversed(range(len(plan))):
            order = plan[which][2]
            came[which] = after(came[which], last)
            middle = left[which].shape[0] // 2
            piece = plus(left[which][middle:], came[which][middle:])
            rest = plus(left[which][:middle], came[which][:middle])
            if which == 0 and step == 1:
                far, near = after(far, piece), after(near, piece)
                far = lax.ppermute(far, "seq", [(i, i - 2) for i in range(2, n_seq)])
                near = lax.ppermute(near, "seq", [(i, i - 1) for i in range(1, n_seq)])
            if which == 0 and step == steps - 1:
                far, near, mine = after(far, piece), after(near, piece), after(mine, piece)
                rest, gathered = lax.optimization_barrier((rest, gathered))
            came[which] = swap(piece, order[step])
            left[which] = rest
            last = (piece, far, near) if which == len(plan) - 2 and step == 2 else piece
    pairs = list(zip(left, came))
    totals = jnp.sum(gathered[:, : 3 * dt], axis=0).reshape(3, width)
    correction = 1.0 - first_decay**STEP
    holds = lax.dynamic_slice_in_dim((slot_tiles < tile_count).astype(jnp.int32), me * per_device, per_device)
    moment_first, moment_second, new_weights = pl.pallas_call(
        functools.partial(adam_kernel, correction, plan),
        out_shape=tuple([shp(weight_slots.shape, F32)] * 3),
        in_specs=[vm] * (2 * len(plan)) + [sm] + [vm] * 5,
        out_specs=tuple([vm] * 3),
        compiler_params=pltpu.CompilerParams(vmem_limit_bytes=30 << 20),
        name="adam",
    )(*[x for pair in pairs for x in pair], holds, first_moment, second_moment, basis_left, basis_right, weight_slots)
    input_grad = pl.pallas_call(
        input_kernel,
        out_shape=shp((own, width), F32),
        in_specs=[vm] * 6,
        out_specs=vm,
        compiler_params=pltpu.CompilerParams(vmem_limit_bytes=20 << 20),
        name="input_grad",
    )(mine_tok, gains, ghid, mine, near, far)

    gain_total = totals[:2]
    fraction = lax.dynamic_slice_in_dim(totals[2], row_at, 1)

    gain_moment = first_decay * gain_first + (1.0 - first_decay) * gain_total
    gain_square = second_decay * gain_second + (1.0 - second_decay) * gain_total * gain_total
    gain_update = gains - gain_rate * (gain_moment / correction) / (
        jnp.sqrt(gain_square / correction) + adam_epsilon
    )
    return (
        output[None],
        input_grad[None],
        fraction,
        moment_first,
        moment_second,
        new_weights,
        gain_update,
        gain_moment,
        gain_square,
    )


def solution(mesh):
    in_specs = (
        P("dp", "seq", None),
        P("dp", None),
        P("dp"),
        P(),
        P(),
        P(),
        P(),
        P(),
        P(("dp", "seq"), None, None),
        P(("dp", "seq"), None, None),
        P(("dp", "seq"), None, None),
        P(("dp", "seq"), None, None),
        P(("dp", "seq"), None, None),
        P("dp", "seq", None),
    )
    out_specs = (
        P("dp", "seq", None),
        P("dp", "seq", None),
        P("dp"),
        P(("dp", "seq"), None, None),
        P(("dp", "seq"), None, None),
        P(("dp", "seq"), None, None),
        P(),
        P(),
        P(),
    )
    return jax.shard_map(local, mesh=mesh, in_specs=in_specs, out_specs=out_specs, check_vma=False)
```

```python
import functools

import jax
import jax.numpy as jnp
from jax import lax
from jax.experimental import pallas as pl
from jax.experimental.pallas import tpu as pltpu
from jax.sharding import PartitionSpec as P

H = 12
HD = 64
FF = 3072
STEP = 3
SPAN = 512
CHUNK = 768
ADAM_GROUP = 7

select_scale = 0.2
fraction_slope = 2.0
first_decay = 0.5
second_decay = 0.5
adam_epsilon = 1e-08
weight_rate = 0.05
gain_rate = 0.2
decay_rate = 0.1
norm_epsilon = 1e-05

BF = jnp.bfloat16
F32 = jnp.float32
VMEM = pltpu.VMEM
SMEM = pltpu.SMEM


def mm(a, b):
    return lax.dot_general(a, b, (((1,), (0,)), ((), ())), preferred_element_type=F32)


def mm_nt(a, b):
    return lax.dot_general(a, b, (((1,), (1,)), ((), ())), preferred_element_type=F32)


def split(x):
    high = x.astype(BF)
    return high, (x - high.astype(F32)).astype(BF)


def mm_split(x, exact):
    high, rest = split(x)
    return mm(high, exact) + mm(rest, exact)


def lane_half(shape, second):
    lane = lax.broadcasted_iota(jnp.int32, shape, 1)
    return (lane >= HD) if second else (lane < HD)


def keep_half(x, second):
    return jnp.where(lane_half(x.shape, second), x, jnp.zeros_like(x))


def norm_parts(x):
    centred = x - jnp.mean(x, axis=-1, keepdims=True)
    rate = lax.rsqrt(jnp.mean(centred * centred, axis=-1, keepdims=True) + norm_epsilon)
    return centred * rate, rate


def send_tile(tile_ref, dst, sums, sem):
    low = 0
    for buffer in sums:
        high = low + buffer.shape[0]

        @pl.when((dst >= low) & (dst < high))
        def _(buffer=buffer, low=low):
            pltpu.make_async_copy(tile_ref, buffer.at[dst - low], sem).start()

        low = high


def wait_tiles(stage_ref, sums, sem):
    pltpu.make_async_copy(stage_ref, sums[0].at[pl.ds(0, stage_ref.shape[0])], sem).wait()


def mm3(a, b):
    (ah, al), (bh, bl) = a, b
    return mm(jnp.concatenate([ah, ah, al], axis=1), jnp.concatenate([bh, bl, bh], axis=0))


def mm3_nt(a, b):
    (ah, al), (bh, bl) = a, b
    return mm_nt(jnp.concatenate([ah, ah, al], axis=1), jnp.concatenate([bh, bl, bh], axis=1))


def layer_kernel(tiles, sizes, *refs):
    (src, dst, scal, thr, tok, gains, dy, segc, segr), refs = refs[:9], refs[9:]
    w_parts, refs = refs[: len(sizes)], refs[len(sizes) :]
    (out_h, ghid_h, gq_h, gk_h, gv_h, nrm_t_h, wqkv_h, q0_h, k0t_h, part0_h, mask0_h, colsum, small, *sums), refs = (
        refs[:16],
        refs[16:],
    )
    (out, ghid, gq, gk, gv, nrm_t, wqkv, part0, mask0), refs = refs[:9], refs[9:]
    (wall, nrm, q_s, q_e, k_s, v_s, kt_s, vt_s, bias, gsh, probs, mixt, mixb, mixbt, wout, hid, xhat), refs = (
        refs[:17],
        refs[17:],
    )
    nm, nmt, acc, gmid, g_s, gt_s, wu, wd, stage, zero, wsem, gsem, zsem, osem = refs

    writes = []

    def write(ref, target):
        copy = pltpu.make_async_copy(ref, target, osem.at[len(writes)])
        copy.start()
        writes.append(copy)

    n_qkv, n_out, n_up, n_down = tiles
    width = tok.shape[1]
    own = dy.shape[0]
    window = tok.shape[0]
    back = window - own
    side = wall.shape[-1]
    dt = width // side
    pairs = width // side
    total_slots = 2 * sums[0].shape[0]
    loads = []
    at = 0
    for index, (part, size) in enumerate(zip(w_parts, sizes)):
        loads.append(pltpu.make_async_copy(part, wall.at[pl.ds(at, size)], wsem.at[index]))
        loads[-1].start()
        at += size
    zero[...] = jnp.zeros_like(zero)
    tile_count = n_qkv + n_out + n_up + n_down
    empty = total_slots - tile_count

    @pl.loop(0, empty)
    def _(e):
        send_tile(zero, dst[tile_count + e], sums, zsem)

    gain_pre = gains[0:1, :]
    gain_mid = gains[1:2, :]

    @pl.loop(0, window // own)
    def _(b):
        rows = pl.ds(pl.multiple_of(b * own, own), own)
        hat, _ = norm_parts(tok[rows, :].astype(F32))
        value = (hat * gain_pre).astype(BF)
        nrm[rows, :] = value
        nrm_t[:, rows] = value.T

    write(nrm_t, nrm_t_h)
    for load in loads:
        load.wait()
    per_row = 3 * dt

    @pl.loop(0, 3 * dt // 2)
    def _(j):
        for i in range(dt):
            for jj in range(2):
                wqkv[i * side : (i + 1) * side, pl.ds(pl.multiple_of((2 * j + jj) * side, side), side)] = wall[
                    src[i * per_row + 2 * j + jj]
                ]

    write(wqkv, wqkv_h)

    @pl.loop(0, dt)
    def _(i):
        rows = pl.ds(pl.multiple_of(i * side, side), side)
        for j in range(dt):
            wout[rows, j * side : (j + 1) * side] = wall[src[n_qkv + i * dt + j]]


    @pl.loop(0, dt // 2, unroll=True)
    def _(j):
        cols = pl.ds(pl.multiple_of(2 * j * side, 2 * side), 2 * side)
        got = (mm(nrm[back:, :], wqkv[:, cols]) * 0.125).astype(BF)
        q_s[2 * j] = got[:, :side]
        q_s[2 * j + 1] = got[:, side:]

    q_e[...] = (mm(nrm[:back, :], wqkv[:, 0:side]) * 0.125).astype(BF)

    @pl.loop(0, dt // 2, unroll=True)
    def _(j):
        cols = pl.ds(pl.multiple_of(width + 2 * j * side, 2 * side), 2 * side)
        got = mm(nrm[...], wqkv[:, cols]).astype(BF)
        got_t = got.T
        k_s[2 * j] = got[:, :side]
        k_s[2 * j + 1] = got[:, side:]
        kt_s[2 * j] = got_t[:side, :]
        kt_s[2 * j + 1] = got_t[side:, :]

    @pl.loop(0, dt // 2, unroll=True)
    def _(j):
        cols = pl.ds(pl.multiple_of(2 * width + 2 * j * side, 2 * side), 2 * side)
        got = mm(nrm[...], wqkv[:, cols]).astype(BF)
        got_t = got.T
        v_s[2 * j] = got[:, :side]
        v_s[2 * j + 1] = got[:, side:]
        vt_s[2 * j] = got_t[:side, :]
        vt_s[2 * j + 1] = got_t[side:, :]

    write(q_s.at[0], q0_h)
    write(kt_s.at[0], k0t_h)

    valid_len = scal[0]
    start = scal[1]
    is_last = scal[2]
    key_at = lax.broadcasted_iota(jnp.int32, (window, own), 0)
    query_at = lax.broadcasted_iota(jnp.int32, (window, own), 1)
    key_valid = (key_at + (start - back)) < valid_len
    key_seg = segc[...]
    k_first = k_s[0]

    def selected(q_rows, first):
        s = mm_nt(k_first, keep_half(q_rows, False))
        same = key_seg == segr[:, first : first + own]
        strict = same & key_valid & (key_at < query_at + first)
        return s, same, jnp.where(strict, select_scale * jnp.maximum(s, 0.0), 0.0), strict

    prefix = jnp.zeros((window, 1), F32)
    for b in range(back // own):
        _, _, chosen, _ = selected(q_e[b * own : (b + 1) * own, :], b * own)
        prefix = prefix + jnp.sum(chosen, axis=1, keepdims=True)
    s_own, same, chosen, strict = selected(q_s[0], back)
    tri_row = lax.broadcasted_iota(jnp.int32, (own, own), 0)
    tri_col = lax.broadcasted_iota(jnp.int32, (own, own), 1)
    earlier = jnp.where(tri_row < tri_col, 1.0, 0.0).astype(BF)
    shadow = prefix + mm_split(chosen, earlier)
    allowed = strict | (same & (key_at == query_at + back))
    bias[...] = jnp.where(allowed, -shadow, -1e30)
    mask0[...] = jnp.where(strict & (s_own > 0.0), 1.0, 0.0).astype(BF)
    write(mask0, mask0_h)
    column_total = prefix + jnp.sum(chosen, axis=1, keepdims=True)
    key_col = lax.broadcasted_iota(jnp.int32, (window, 1), 0)
    key_pos = key_col + (start - back)
    counts = (key_pos >= 0) & (key_pos < valid_len) & ((key_col < own) | (is_last > 0))
    soft = 1.0 / (1.0 + jnp.exp(-fraction_slope * (column_total - thr[0])))
    counted = jnp.sum(jnp.where(counts, soft, 0.0), axis=0, keepdims=True)
    small[...] = jnp.zeros_like(small)
    small[1:2, :] = jnp.broadcast_to(counted / valid_len.astype(F32), (1, width))

    @pl.loop(0, pairs, unroll=2)
    def _(p):
        q2 = q_s[p]
        k2 = k_s[p]
        both = [mm_nt(k2, keep_half(q2, hh == 1)) for hh in range(2)]
        prs = []
        for hh in range(2):
            s = both[hh] + bias[...]
            e = jnp.exp(s - jnp.max(s, axis=0, keepdims=True))
            prs.append((e * (1.0 / jnp.sum(e, axis=0, keepdims=True))).astype(BF))
        for hh in range(2):
            probs[2 * p + hh] = prs[hh]
        mixed = [mm(vt_s[p, hh * HD : (hh + 1) * HD, :], prs[hh]) for hh in range(2)]
        mixt[pl.ds(pl.multiple_of(p * side, side), side), :] = jnp.concatenate(mixed, axis=0)

    mixbt[...] = mixt[...].astype(BF)
    mixb[...] = mixbt[...].T
    hid[...] = tok[back:, :].astype(F32) + mm(mixb[...], wout[...])
    hat, rate = norm_parts(hid[...])
    xhat[...] = hat
    nm[...] = (hat * gain_mid).astype(BF)
    nmt[...] = nm[...].T

    acc[...] = jnp.zeros_like(acc)
    gmid[...] = jnp.zeros_like(gmid)
    cw = CHUNK // side
    f_tiles = FF // side
    per_chunk = 2 * cw * dt
    chunks = FF // CHUNK

    @pl.loop(0, chunks)
    def _(c):
        slot = lax.rem(c, 2)
        for i in range(dt):
            for jj in range(cw):
                wu[i * side : (i + 1) * side, jj * side : (jj + 1) * side] = wall[
                    src[n_qkv + n_out + i * f_tiles + cw * c + jj]
                ]
        for ii in range(cw):
            for j in range(dt):
                wd[ii * side : (ii + 1) * side, j * side : (j + 1) * side] = wall[
                    src[n_qkv + n_out + n_up + (cw * c + ii) * dt + j]
                ]
        up = mm(nm[...], wu[...])
        cube = 0.7978845608028654 * (up + 0.044715 * up * up * up)
        th = jnp.tanh(cube)
        active = (0.5 * up * (1.0 + th)).astype(BF)
        slope = 0.5 * (1.0 + th) + 0.5 * up * (1.0 - th * th) * (
            0.7978845608028654 * (1.0 + 3.0 * 0.044715 * up * up)
        )
        acc[...] += mm(active, wd[...])
        gu = (mm_nt(dy[...], wd[...]) * slope).astype(BF)
        gmid[...] += mm_nt(gu, wu[...])

        @pl.when(c >= 2)
        def _():
            wait_tiles(stage.at[slot], sums, gsem.at[slot])

        g_down = mm(active.T, dy[...]).astype(BF)
        for ii in range(cw):
            for j in range(dt):
                at = ii * dt + j
                stage[slot, at] = g_down[ii * side : (ii + 1) * side, j * side : (j + 1) * side]
        g_up = mm(nmt[...], gu).astype(BF)
        for i in range(dt):
            for jj in range(cw):
                at = cw * dt + i * cw + jj
                stage[slot, at] = g_up[i * side : (i + 1) * side, jj * side : (jj + 1) * side]
        for ii in range(cw):
            for j in range(dt):
                at = ii * dt + j
                t = n_qkv + n_out + n_up + (cw * c + ii) * dt + j
                send_tile(stage.at[slot, at], dst[t], sums, gsem.at[slot])
        for i in range(dt):
            for jj in range(cw):
                at = cw * dt + i * cw + jj
                t = n_qkv + n_out + i * f_tiles + cw * c + jj
                send_tile(stage.at[slot, at], dst[t], sums, gsem.at[slot])

    out[...] = (hid[...] + acc[...]).astype(BF)
    write(out, out_h)
    hat = xhat[...]
    gm = gmid[...]
    small[0:1, :] = jnp.sum(gm * hat, axis=0, keepdims=True)
    scaled = gm * gain_mid
    gh = dy[...].astype(F32) + rate * (
        scaled
        - jnp.mean(scaled, axis=-1, keepdims=True)
        - hat * jnp.mean(scaled * hat, axis=-1, keepdims=True)
    )
    ghid[...] = gh
    write(ghid, ghid_h)
    gb = gh.astype(BF)
    gmix = mm_nt(gb, wout[...]).astype(BF)
    for p in range(pairs):
        g_s[p] = gmix[:, p * side : (p + 1) * side]
    gt_s[...] = gmix.T

    for slot in range(2):
        wait_tiles(stage.at[slot], sums, gsem.at[slot])
    half_out = dt // 2
    for part in range(2):
        g_out = mm(mixbt[part * half_out * side : (part + 1) * half_out * side, :], gb).astype(BF)
        for i in range(half_out):
            for j in range(dt):
                stage[part, i * dt + j] = g_out[i * side : (i + 1) * side, j * side : (j + 1) * side]
        for i in range(half_out):
            for j in range(dt):
                t = n_qkv + (part * half_out + i) * dt + j
                send_tile(stage.at[part, i * dt + j], dst[t], sums, gsem.at[part])

    gsh[...] = jnp.zeros_like(gsh)

    @pl.loop(0, pairs, unroll=2)
    def _(p):
        g2 = g_s[p]
        q2 = q_s[p]
        v2 = v_s[p]
        later = jnp.where(p > 0, 1.0, 0.0)
        halves = [keep_half(g2, hh == 1) for hh in range(2)]
        dps = [mm_nt(v2, halves[hh]) for hh in range(2)]
        prs = [probs[2 * p + hh] for hh in range(2)]
        rows = pl.ds(pl.multiple_of(p * side, side), side)
        product = gt_s[rows, :].astype(F32) * mixt[rows, :]
        dls = []
        for hh in range(2):
            delta = jnp.sum(product[hh * HD : (hh + 1) * HD, :], axis=0, keepdims=True)
            dls.append(prs[hh].astype(F32) * (dps[hh] - delta))
        gsh[...] += dls[0] + dls[1]

        @pl.when(p == 0)
        def _():
            part0[...] = dls[0]

        gs = [(dls[0] * later).astype(BF), dls[1].astype(BF)]
        dv = mm(prs[0], halves[0]) + mm(prs[1], halves[1])
        dk = mm(gs[0], keep_half(q2, False)) + mm(gs[1], keep_half(q2, True))
        dqs = [mm(kt_s[p, hh * HD : (hh + 1) * HD, :], gs[hh]) for hh in range(2)]
        cols = pl.ds(pl.multiple_of(p * side, side), side)
        gq[:, cols] = (jnp.concatenate(dqs, axis=0) * 0.125).T.astype(BF)
        gk[:, cols] = dk.astype(BF)
        gv[:, cols] = dv.astype(BF)

    write(gq, gq_h)
    write(gk, gk_h)
    write(gv, gv_h)
    ones = jnp.ones((8, own), BF)
    high, rest = split(-gsh[...])
    colsum[...] = mm_nt(ones, high) + mm_nt(ones, rest)
    after = jnp.where(tri_row > tri_col, 1.0, 0.0).astype(BF)
    part0[...] += select_scale * mask0[...].astype(F32) * (mm(high, after) + mm(rest, after))
    write(part0, part0_h)

    for part in range(2):
        wait_tiles(stage.at[part, pl.ds(0, half_out * dt)], sums, gsem.at[part])
    pltpu.make_async_copy(sums[0].at[pl.ds(0, empty)], sums[0].at[pl.ds(0, empty)], zsem).wait()
    for copy in writes:
        copy.wait()


def load_all(pairs, sem):
    copies = [pltpu.make_async_copy(a, b, sem.at[i]) for i, (a, b) in enumerate(pairs)]
    for copy in copies:
        copy.start()
    return copies


def qkv_kernel(dst, gq_h, gk_h, gv_h, nrm_h, *refs):
    sums = refs[3:6]
    gq, gk, gv, nrm_t, stage, lsem, gsem = refs[6:]
    own, width = gq.shape
    side = stage.shape[-1]
    dt = width // side
    back = gk.shape[0] - own
    copies = load_all([(nrm_h, nrm_t), (gv_h, gv), (gk_h, gk), (gq_h, gq)], lsem)
    copies[0].wait()
    count = 0
    for which, copy in ((2, copies[1]), (1, copies[2]), (0, copies[3])):
        copy.wait()
        bounds = [(c, c + 2) for c in range(0, dt, 2)] if which == 2 else [(1, 2)] + [(c, c + 2) for c in range(2, dt, 2)]
        for lo, hi in bounds:
            cols = slice(lo * side, hi * side)
            if which == 0:
                g = mm(nrm_t[:, back:], gq[:, cols])
            else:
                g = mm(nrm_t[...], (gk if which == 1 else gv)[:, cols])
            g = g.astype(BF)
            for i in range(dt):
                for j in range(lo, hi):
                    stage[count] = g[i * side : (i + 1) * side, (j - lo) * side : (j - lo + 1) * side]
                    send_tile(stage.at[count], dst[i * 3 * dt + which * dt + j], sums, gsem)
                    count += 1
    wait_tiles(stage, sums, gsem)


def head_kernel(dst, near_sums, far_sums, part0_h, mask0_h, q0_h, k0t_h, gq_h, gk_h, nrm_h, *refs):
    gq_out, gk_out = refs[3:5]
    sums = refs[5:8]
    part0, mask0, q0, k0t, gq, gk, nrm_t, stage, lsem, gsem = refs[8:]
    own, side = gq.shape
    window = gk.shape[0]
    back = window - own
    dt = nrm_t.shape[0] // side
    head = pl.ds(0, side)
    copies = load_all(
        [
            (part0_h, part0),
            (mask0_h, mask0),
            (k0t_h, k0t),
            (q0_h, q0),
            (gq_h.at[:, head], gq),
            (gk_h.at[:, head], gk),
            (nrm_h, nrm_t),
        ],
        lsem,
    )
    none = jnp.zeros((1, own), F32)
    suffix = jnp.concatenate([none, near_sums[0:1, : window - own]], axis=1)
    suffix = suffix + jnp.concatenate([none, none, far_sums[0:1, : window - 2 * own]], axis=1)
    column = jnp.broadcast_to(suffix, (side, window)).T
    column = jnp.concatenate([column] * (own // side), axis=1)
    for copy in copies[:-1]:
        copy.wait()
    gs = (part0[...] + select_scale * mask0[...].astype(F32) * column).astype(BF)
    dq = (mm(k0t[0:HD, :], gs) * 0.125).T
    dk = mm(gs, keep_half(q0[...], False)).astype(BF)
    gq_new = gq[...] + jnp.concatenate([dq, jnp.zeros_like(dq)], axis=1).astype(BF)
    gk_new = gk[...] + dk
    gq_out[...] = gq_new
    gk_out[...] = gk_new
    copies[-1].wait()
    g_q = mm(nrm_t[:, back:], gq_new).astype(BF)
    g_k = mm(nrm_t[...], gk_new).astype(BF)
    for which, g in ((0, g_q), (1, g_k)):
        for i in range(dt):
            stage[which * dt + i] = g[i * side : (i + 1) * side, :]
            send_tile(stage.at[which * dt + i], dst[i * 3 * dt + which * dt], sums, gsem)
    wait_tiles(stage, sums, gsem)


def pre_kernel(
    row_at, tok, small, gq_head, gk_head, gq_h, gk_h, gv_h, wqkv_h, far, near, mine, totals, gq, gk, gv, wqkv, lsem
):
    own, width = gq.shape
    window = gk.shape[0]
    side = gq_head.shape[1]
    rest = pl.ds(side, width - side)
    copies = load_all(
        [(wqkv_h, wqkv), (gk_h.at[:, rest], gk.at[:, rest]), (gv_h, gv), (gq_h.at[:, rest], gq.at[:, rest])], lsem
    )
    gq[:, 0:side] = gq_head[...]
    gk[:, 0:side] = gk_head[...]
    for copy in copies:
        copy.wait()
    total = jnp.zeros((1, width), F32)
    for b in range(window // own):
        rows = slice(b * own, (b + 1) * own)
        g = mm_nt(gk[rows, :], wqkv[:, width : 2 * width]) + mm_nt(gv[rows, :], wqkv[:, 2 * width :])
        if b == window // own - 1:
            g = g + mm_nt(gq[...], wqkv[:, :width])
            mine[...] = g
        elif b == 0:
            far[...] = g.astype(far.dtype)
        else:
            near[...] = g.astype(near.dtype)
        hat, _ = norm_parts(tok[rows, :].astype(F32))
        total = total + jnp.sum(g * hat, axis=0, keepdims=True)
    totals[...] = jnp.zeros_like(totals)
    spots = lax.broadcasted_iota(jnp.int32, (1, width), 1)
    placed = jnp.where(spots == row_at[0], small[1:2, :], 0.0)
    for index, line in enumerate((total, small[0:1, :], placed)):
        for i in range(width // side):
            at = index * (width // side) + i
            totals[at : at + 1, :] = line[:, i * side : (i + 1) * side]


def input_kernel(tok, gains, ghid, mine, near, far, out):
    hat, rate = norm_parts(tok[...].astype(F32))
    g = mine[...] + near[...].astype(F32) + far[...].astype(F32)
    scaled = g * gains[0:1, :]
    out[...] = ghid[...] + rate * (
        scaled
        - jnp.mean(scaled, axis=-1, keepdims=True)
        - hat * jnp.mean(scaled * hat, axis=-1, keepdims=True)
    )


def adam_kernel(correction, parts, *refs):
    grads, refs = refs[: 2 * len(parts)], refs[2 * len(parts) :]
    holds, first, second, left, right, weight, first_out, second_out, weight_out = refs
    slots = []
    for index, (at, size, _) in enumerate(parts):
        slots += [(at + k, grads[2 * index], grads[2 * index + 1], k) for k in range(size)]
    for low in range(0, len(slots), ADAM_GROUP):
        group = slots[low : low + ADAM_GROUP]
        rights, turned, steps, undone = {}, {}, {}, {}
        for slot, mine, other, k in group:
            grad = mine[k].astype(F32) + other[k].astype(F32)
            grad = jnp.where(holds[slot] > 0, grad, 0.0)
            rights[slot] = split(right[slot])
            turned[slot] = mm3(split(grad), rights[slot])
        for slot, *_ in group:
            turned[slot] = mm3(split(left[slot].T), split(turned[slot]))
        for slot, *_ in group:
            t = turned[slot]
            first_new = first_decay * first[slot] + (1.0 - first_decay) * t
            second_new = second_decay * second[slot] + (1.0 - second_decay) * t * t
            first_out[slot] = first_new
            second_out[slot] = second_new
            steps[slot] = first_new / correction / (jnp.sqrt(second_new / correction) + adam_epsilon)
        for slot, *_ in group:
            undone[slot] = mm3_nt(split(steps[slot]), rights[slot])
        for slot, *_ in group:
            back = mm3(split(left[slot]), split(undone[slot]))
            w = weight[slot]
            weight_out[slot] = w - weight_rate * back - weight_rate * decay_rate * w


def after(x, earlier):
    return lax.optimization_barrier((x, earlier))[0]


def bit_plan(devices, per_device):
    bits = [1 << b for b in range(devices.bit_length() - 1)]
    first, rest = bits[0], bits[1:]
    if devices == 32:
        orders = [(2, 4, 8, 16), (4, 8, 2, 16), (8, 16, 2, 4)]
    else:
        orders = [tuple(rest[i:] + rest[:i]) for i in range(3)]
    if per_device < 4:
        sizes = [1] * per_device
    else:
        sizes = [per_device * 3 // 7, per_device * 5 // 14]
        sizes.append(per_device - sum(sizes))
    plan = []
    at = 0
    for size, order in zip(sizes, orders):
        if size:
            plan.append((at, size, order))
            at += size
    return first, plan


def gather_parts(devices, per_device):
    if devices != 32 or per_device < 8:
        return per_device, []
    size = per_device * 2 // 7
    first = per_device * 3 // 14
    return first, [
        (first, size, (16, 8, 4, 2, 1)),
        (first + size, size, (16, 8, 2, 4, 1)),
        (first + 2 * size, per_device - first - 2 * size, (4, 2, 16, 8, 1)),
    ]


def local(
    tokens,
    segment_ids,
    pad_lengths,
    threshold,
    gains,
    gain_first,
    gain_second,
    slot_tiles,
    weight_slots,
    first_moment,
    second_moment,
    basis_left,
    basis_right,
    out_grad,
):
    axes = ("dp", "seq")
    n_dp, n_seq = lax.axis_size("dp"), lax.axis_size("seq")
    devices = n_dp * n_seq
    me = lax.axis_index(axes)
    seq_at = lax.axis_index("seq")
    _, own, width = tokens.shape
    length = segment_ids.shape[1]
    side = weight_slots.shape[-1]
    per_device = weight_slots.shape[0]
    slot_total = slot_tiles.shape[0]
    dt = width // side
    tiles = (3 * dt * dt, dt * dt, dt * (FF // side), dt * (FF // side))
    tile_count = sum(tiles)
    back = SPAN
    window = back + own

    def swap(x, bit):
        return lax.ppermute(x, axes, [(i, i ^ bit) for i in range(devices)])

    slot_ids = jnp.arange(slot_total, dtype=jnp.int32)
    position = jnp.sum(
        jnp.where(slot_tiles[None, :] == slot_ids[:, None], slot_ids[None, :], 0), axis=1
    )
    owner = position // per_device
    inner = position % per_device
    apart = owner ^ me
    first_bit, plan = bit_plan(devices, per_device)
    half = slot_total // 2
    spread = devices // 2
    place = jnp.zeros_like(position)
    for at, size, order in plan:
        index = jnp.zeros_like(position)
        for bit in order:
            index = index * 2 + ((apart & bit) != 0).astype(jnp.int32)
        here = at * spread + index * size + (inner - at)
        place = jnp.where((inner >= at) & (inner < at + size), here, place)
    dst = place + jnp.where((apart & first_bit) != 0, half, 0)
    by_gather, gather_plan = gather_parts(devices, per_device)
    src = owner * by_gather + inner
    base = devices * by_gather
    for at, size, order in gather_plan:
        index = jnp.zeros_like(position)
        for bit in reversed(order):
            index = index * 2 + ((apart & bit) != 0).astype(jnp.int32)
        here = base + index * size + (inner - at)
        src = jnp.where((inner >= at) & (inner < at + size), here, src)
        base += devices * size

    mine_tok = tokens[0]
    seen = []
    for step in range(back // own, 0, -1):
        seen.append(lax.ppermute(mine_tok, "seq", [(i, i + step) for i in range(n_seq - step)]))
    tok = jnp.concatenate(seen + [mine_tok], axis=0)
    start = seq_at * own
    seg_window = lax.dynamic_slice_in_dim(
        jnp.concatenate([jnp.full((back,), -1, jnp.int32), segment_ids[0]]), start, window
    )
    valid_len = length - pad_lengths[0]
    scal = jnp.stack([valid_len, start, (seq_at == n_seq - 1).astype(jnp.int32)])

    segc, segr = seg_window[:, None], seg_window[None, :]

    rounded = weight_slots.astype(BF)
    pieces = [lax.all_gather(rounded[:by_gather], axes, axis=0, tiled=True)]
    held = [rounded[at : at + size] for at, size, _ in gather_plan]
    for step in range(len(gather_plan[0][2]) - 2 if gather_plan else 0):
        held = [jnp.concatenate([h, swap(h, o[2][step])], axis=0) for h, o in zip(held, gather_plan)]
        if step == 1:
            held[0], tok, src, dst, scal, segc, segr = lax.optimization_barrier(
                (held[0], tok, src, dst, scal, segc, segr)
            )
    for h, (_, _, order) in zip(held, gather_plan):
        two = [h, swap(h, order[-2])]
        pieces += two + [swap(x, order[-1]) for x in two]
    sizes = [p.shape[0] for p in pieces]

    hbm = pl.BlockSpec(memory_space=pltpu.HBM)
    vm = pl.BlockSpec(memory_space=VMEM)
    sm = pl.BlockSpec(memory_space=SMEM)
    shp = jax.ShapeDtypeStruct
    first_rows = plan[0][1] * spread
    sums_shapes = [shp((n, side, side), BF) for n in (half, first_rows, half - first_rows)]
    per_chunk = 2 * (CHUNK // side) * dt
    outs = pl.pallas_call(
        functools.partial(layer_kernel, tiles, sizes),
        out_shape=(
            shp((own, width), BF),
            shp((own, width), F32),
            shp((own, width), BF),
            shp((window, width), BF),
            shp((window, width), BF),
            shp((width, window), BF),
            shp((width, 3 * width), BF),
            shp((own, side), BF),
            shp((side, window), BF),
            shp((window, own), F32),
            shp((window, own), BF),
            shp((8, window), F32),
            shp((8, width), F32),
            *sums_shapes,
        ),
        in_specs=[sm] * 4 + [vm] * 5 + [hbm] * len(sizes),
        out_specs=tuple([hbm] * 11 + [vm] * 2 + [hbm] * 3),
        scratch_shapes=[
            VMEM((own, width), BF),
            VMEM((own, width), F32),
            VMEM((own, width), BF),
            VMEM((window, width), BF),
            VMEM((window, width), BF),
            VMEM((width, window), BF),
            VMEM((width, 3 * width), BF),
            VMEM((window, own), F32),
            VMEM((window, own), BF),
            VMEM((slot_total, side, side), BF),
            VMEM((window, width), BF),
            VMEM((dt, own, side), BF),
            VMEM((back, side), BF),
            VMEM((dt, window, side), BF),
            VMEM((dt, window, side), BF),
            VMEM((dt, side, window), BF),
            VMEM((dt, side, window), BF),
            VMEM((window, own), F32),
            VMEM((window, own), F32),
            VMEM((H, window, own), BF),
            VMEM((width, own), F32),
            VMEM((own, width), BF),
            VMEM((width, own), BF),
            VMEM((width, width), BF),
            VMEM((own, width), F32),
            VMEM((own, width), F32),
            VMEM((own, width), BF),
            VMEM((width, own), BF),
            VMEM((own, width), F32),
            VMEM((own, width), F32),
            VMEM((dt, own, side), BF),
            VMEM((width, own), BF),
            VMEM((width, CHUNK), BF),
            VMEM((CHUNK, width), BF),
            VMEM((2, per_chunk, side, side), BF),
            VMEM((side, side), BF),
            pltpu.SemaphoreType.DMA((len(sizes),)),
            pltpu.SemaphoreType.DMA((2,)),
            pltpu.SemaphoreType.DMA,
            pltpu.SemaphoreType.DMA((11,)),
        ],
        compiler_params=pltpu.CompilerParams(vmem_limit_bytes=60 << 20),
        name="layer",
    )(
        src,
        dst,
        scal,
        threshold,
        tok,
        gains,
        out_grad[0],
        segc,
        segr,
        *pieces,
    )
    (output, ghid, gq, gk, gv, nrm_t, wqkv, q0, k0t, part0, mask0, colsum, small, *sums) = outs

    near_sums, far_sums = [
        lax.ppermute(colsum, "seq", [(i, i - step) for i in range(step, n_seq)]) for step in (1, 2)
    ]
    main_tiles = tiles[0] - 2 * dt
    sums = pl.pallas_call(
        qkv_kernel,
        out_shape=sums_shapes,
        in_specs=[sm] + [hbm] * 7,
        out_specs=[hbm] * 3,
        scratch_shapes=[
            VMEM((own, width), BF),
            VMEM((window, width), BF),
            VMEM((window, width), BF),
            VMEM((width, window), BF),
            VMEM((main_tiles, side, side), BF),
            pltpu.SemaphoreType.DMA((4,)),
            pltpu.SemaphoreType.DMA,
        ],
        input_output_aliases={5: 0, 6: 1, 7: 2},
        compiler_params=pltpu.CompilerParams(vmem_limit_bytes=60 << 20),
        cost_estimate=pl.CostEstimate(
            flops=2 * (2 * window + own) * width * width, bytes_accessed=8 << 20, transcendentals=0
        ),
        name="qkv_grad",
    )(dst, gq, gk, gv, nrm_t, *sums)
    gq_head, gk_head, stay, *aways = pl.pallas_call(
        head_kernel,
        out_shape=(shp((own, side), BF), shp((window, side), BF), *sums_shapes),
        in_specs=[sm, vm, vm] + [hbm] * 10,
        out_specs=(vm, vm, hbm, hbm, hbm),
        scratch_shapes=[
            VMEM((window, own), F32),
            VMEM((window, own), BF),
            VMEM((own, side), BF),
            VMEM((side, window), BF),
            VMEM((own, side), BF),
            VMEM((window, side), BF),
            VMEM((width, window), BF),
            VMEM((2 * dt, side, side), BF),
            pltpu.SemaphoreType.DMA((7,)),
            pltpu.SemaphoreType.DMA,
        ],
        input_output_aliases={10: 2, 11: 3, 12: 4},
        compiler_params=pltpu.CompilerParams(vmem_limit_bytes=60 << 20),
        cost_estimate=pl.CostEstimate(flops=1 << 30, bytes_accessed=4 << 20, transcendentals=0),
        name="head_grad",
    )(dst, near_sums, far_sums, part0, mask0, q0, k0t, gq, gk, nrm_t, *sums)

    def plus(a, b):
        return (a.astype(F32) + b.astype(F32)).astype(BF)

    got = [swap(aways[0], first_bit)]
    aways[1] = after(aways[1], got[0])
    got.append(swap(aways[1], first_bit))
    steps = len(plan[0][2])

    def from_got(which, low, high):
        at, size, _ = plan[which]
        start = at * spread
        source, base = (got[0], 0) if which == 0 else (got[1], first_rows)
        rows = slice(start + low * size * spread // 2, start + high * size * spread // 2)
        return plus(stay[rows], source[rows.start - base : rows.stop - base])

    sent = [from_got(0, 1, 2)]
    for which in range(1, len(plan)):
        got[1] = after(got[1], sent[-1])
        sent.append(from_got(which, 1, 2))
    came = [swap(piece, order[0]) for piece, (_, _, order) in zip(sent, plan)]
    left = [from_got(which, 0, 1) for which in range(len(plan))]
    gq_head = after(gq_head, sent[-1])
    row_at = lax.axis_index("dp")
    far, near, mine, totals = pl.pallas_call(
        pre_kernel,
        out_shape=(
            shp((own, width), BF),
            shp((own, width), BF),
            shp((own, width), F32),
            shp((side // 2, side), F32),
        ),
        in_specs=[sm] + [vm] * 4 + [hbm] * 4,
        out_specs=tuple([vm] * 4),
        scratch_shapes=[
            VMEM((own, width), BF),
            VMEM((window, width), BF),
            VMEM((window, width), BF),
            VMEM((width, 3 * width), BF),
            pltpu.SemaphoreType.DMA((4,)),
        ],
        compiler_params=pltpu.CompilerParams(vmem_limit_bytes=30 << 20),
        cost_estimate=pl.CostEstimate(
            flops=2 * (2 * window + own) * width * width, bytes_accessed=10 << 20, transcendentals=0
        ),
        name="pre_grad",
    )(row_at[None], tok, small, gq_head, gk_head, gq, gk, gv, wqkv)
    gathered = lax.all_gather(totals, axes)
    last = (sent[-1], totals)
    for step in range(1, steps):
        for which in reversed(range(len(plan))):
            order = plan[which][2]
            came[which] = after(came[which], last)
            middle = left[which].shape[0] // 2
            piece = plus(left[which][middle:], came[which][middle:])
            rest = plus(left[which][:middle], came[which][:middle])
            if which == 0 and step == 1:
                far, near = after(far, piece), after(near, piece)
                far = lax.ppermute(far, "seq", [(i, i - 2) for i in range(2, n_seq)])
                near = lax.ppermute(near, "seq", [(i, i - 1) for i in range(1, n_seq)])
            if which == 0 and step == steps - 1:
                far, near, mine = after(far, piece), after(near, piece), after(mine, piece)
                rest, gathered = lax.optimization_barrier((rest, gathered))
            came[which] = swap(piece, order[step])
            left[which] = rest
            last = (piece, far, near) if which == len(plan) - 2 and step == 2 else piece
    pairs = list(zip(left, came))
    totals = jnp.sum(gathered[:, : 3 * dt], axis=0).reshape(3, width)
    correction = 1.0 - first_decay**STEP
    holds = lax.dynamic_slice_in_dim((slot_tiles < tile_count).astype(jnp.int32), me * per_device, per_device)
    moment_first, moment_second, new_weights = pl.pallas_call(
        functools.partial(adam_kernel, correction, plan),
        out_shape=tuple([shp(weight_slots.shape, F32)] * 3),
        in_specs=[vm] * (2 * len(plan)) + [sm] + [vm] * 5,
        out_specs=tuple([vm] * 3),
        compiler_params=pltpu.CompilerParams(vmem_limit_bytes=30 << 20),
        name="adam",
    )(*[x for pair in pairs for x in pair], holds, first_moment, second_moment, basis_left, basis_right, weight_slots)
    input_grad = pl.pallas_call(
        input_kernel,
        out_shape=shp((own, width), F32),
        in_specs=[vm] * 6,
        out_specs=vm,
        compiler_params=pltpu.CompilerParams(vmem_limit_bytes=20 << 20),
        name="input_grad",
    )(mine_tok, gains, ghid, mine, near, far)

    gain_total = totals[:2]
    fraction = lax.dynamic_slice_in_dim(totals[2], row_at, 1)

    gain_moment = first_decay * gain_first + (1.0 - first_decay) * gain_total
    gain_square = second_decay * gain_second + (1.0 - second_decay) * gain_total * gain_total
    gain_update = gains - gain_rate * (gain_moment / correction) / (
        jnp.sqrt(gain_square / correction) + adam_epsilon
    )
    return (
        output[None],
        input_grad[None],
        fraction,
        moment_first,
        moment_second,
        new_weights,
        gain_update,
        gain_moment,
        gain_square,
    )


def solution(mesh):
    in_specs = (
        P("dp", "seq", None),
        P("dp", None),
        P("dp"),
        P(),
        P(),
        P(),
        P(),
        P(),
        P(("dp", "seq"), None, None),
        P(("dp", "seq"), None, None),
        P(("dp", "seq"), None, None),
        P(("dp", "seq"), None, None),
        P(("dp", "seq"), None, None),
        P("dp", "seq", None),
    )
    out_specs = (
        P("dp", "seq", None),
        P("dp", "seq", None),
        P("dp"),
        P(("dp", "seq"), None, None),
        P(("dp", "seq"), None, None),
        P(("dp", "seq"), None, None),
        P(),
        P(),
        P(),
    )
    return jax.shard_map(local, mesh=mesh, in_specs=in_specs, out_specs=out_specs, check_vma=False)
```
